32 devices in a mesh: groups: 2 (over y), slab: 4 (over x, core), head: 4 (over z).
Axes of the slice: x: 2, y: 2, z: 4, core: 2. Of those that a mesh axis runs over, the one named last changes fastest.
Arguments:
- query_rows: bfloat16 [2048, 5120], P(('groups', 'slab', 'head')), parts along dimension 0, may hold values from -16 to 16
- key_rows: bfloat16 [2048, 5120], P(('groups', 'slab', 'head')), parts along dimension 0, may hold values from -16 to 16
- value_rows: bfloat16 [2048, 5120], P(('groups', 'slab', 'head')), parts along dimension 0, may hold values from -4 to 4
- tile_mask: int32 [40, 16, 5], P(None, ('groups', 'slab')), parts along dimension 1, may hold values from 0 to 1, as said below
- head_slot: int32 [40], replicated, may hold values from 0 to 39, as said below
Outputs:
- attended: bfloat16 [2048, 5120], P(('groups', 'slab', 'head')), parts along dimension 0
- slot_lse: float32 [40, 2048], P('head', ('groups', 'slab')), parts along dimension 1
The draws below stay inside these ranges and needn't reach their ends.
There are 2 independent parts, one for each index of `groups`. The reference program is written for one: setup_inputs(seed, part) draws one part's arguments, and reference() takes and returns one part's arrays. A program takes and returns all parts, laid end to end along the dimension named above; an argument that names none is the same for every part. Nothing has to cross between parts.
Inputs may be any that keep to these rules, and one draw needn't show every extreme that they name: `tile_mask`: entry 2 of every row of every head is 1. `head_slot`: distinct; slots o * 10 to o * 10 + 9 belong to owner o along the head axis; every owner holds at most 10 heads and some owner holds 10.
All inputs are finite; a program needn't handle non-finite values.
Results may differ from the reference program's by a relative error of at most 0.0045.
Values may be sent and summed in bfloat16 or wider, within the bound.
A program may use at most 64 MiB of HBM per device.

```python
import jax
import jax.numpy as jnp
from jax import lax

HEADS = 40
DH = 128
D = 5120
BLK = 128
REACH = 2
BAND = 5
HALO = 256
TOKENS = 1024
NBLK = 8
CAP = 10
SLOTS = 40


def paired_rows(key):
    base = jax.random.fold_in(key, 7)
    query_base = jnp.clip(jax.random.normal(jax.random.fold_in(base, 1), (TOKENS, D), jnp.float32), -4.0, 4.0)
    key_base = jnp.clip(jax.random.normal(jax.random.fold_in(base, 2), (TOKENS, D), jnp.float32), -4.0, 4.0)
    return (query_base, key_base)


def draw_query_rows(key, part):
    return paired_rows(key)[0].astype(jnp.bfloat16)


def draw_key_rows(key, part):
    return paired_rows(key)[1].astype(jnp.bfloat16)


def draw_tile_mask(key, part):
    first = jax.random.fold_in(key, 21)
    levels = jax.random.randint(jax.random.fold_in(first, 1), (HEADS, 1, 1), 3, 11)
    votes = jax.random.randint(jax.random.fold_in(first, 2), (HEADS, NBLK, BAND), 0, 10)
    column = jnp.arange(BAND, dtype=jnp.int32)[None, None, :]
    return jnp.where(column == REACH, 1, (votes < levels).astype(jnp.int32)).astype(jnp.int32)


def draw_head_slot(key, part):
    first = jax.random.fold_in(key, 33)
    owners = SLOTS // CAP
    base_count = HEADS // owners
    extra = HEADS - base_count * owners
    order = jax.random.permutation(jax.random.fold_in(first, 1), owners)
    ranks = jnp.argsort(order, stable=True).astype(jnp.int32)
    counts = base_count + (ranks < extra).astype(jnp.int32)
    slot_ids = jnp.arange(SLOTS, dtype=jnp.int32)
    used = slot_ids % CAP < counts[slot_ids // CAP]
    used_first = jnp.argsort(1 - used.astype(jnp.int32), stable=True).astype(jnp.int32)[:HEADS]
    shuffle = jax.random.permutation(jax.random.fold_in(first, 2), HEADS)
    return used_first[shuffle].astype(jnp.int32)


def block_levels(rng, extent, cuts, least, largest):
    gain = 1.0
    for axis_at, blocks in cuts:
        draws = jax.random.uniform(jax.random.fold_in(jax.random.fold_in(rng, 6), axis_at), (blocks,), jnp.float32, least / len(cuts), largest / len(cuts))
        gain = gain * jnp.repeat(jnp.exp(draws), extent[axis_at] // blocks).reshape((-1,) + (1,) * (len(extent) - 1 - axis_at))
    return gain


def centred(rng, extent, spread, limit, split=(), kind=jnp.bfloat16):
    entries = spread * jax.random.normal(rng, extent, jnp.float32)
    if split:
        entries = entries * block_levels(rng, extent, split, -0.22, 0.18)
    return jnp.clip(entries, -limit, limit).astype(kind)


def setup_inputs(seed: int = 0, part: int = 0) -> dict:
    keys = jax.random.split(jax.random.key(seed), 6)
    part_splits = jax.random.split(jax.random.fold_in(keys[5], part), 6)
    query_rows = draw_query_rows(jax.random.fold_in(jax.random.fold_in(keys[5], part), 71), part)
    key_rows = draw_key_rows(jax.random.fold_in(jax.random.fold_in(keys[5], part), 71), part)
    value_rows = centred(part_splits[2], (TOKENS, D), 1.0, 4.0, ((0, 16),))
    tile_mask = draw_tile_mask(jax.random.fold_in(jax.random.fold_in(keys[5], part), 71), part)
    head_slot = draw_head_slot(jax.random.fold_in(keys[5], 71), part)
    return {"query_rows": query_rows, "key_rows": key_rows, "value_rows": value_rows, "tile_mask": tile_mask, "head_slot": head_slot}


def reference(query_rows, key_rows, value_rows, tile_mask, head_slot):
    scale = DH ** -0.5
    head_queries = query_rows.reshape(TOKENS, HEADS, DH).transpose(1, 0, 2)
    head_keys = jnp.pad(key_rows.reshape(TOKENS, HEADS, DH).transpose(1, 0, 2), ((0, 0), (HALO, HALO), (0, 0)))
    head_values = jnp.pad(value_rows.reshape(TOKENS, HEADS, DH).transpose(1, 0, 2), ((0, 0), (HALO, HALO), (0, 0)))

    def one_head(head_args):
        queries, keys_ext, values_ext, head_mask = head_args

        def one_tile(block):
            start = (block * BLK).astype(jnp.int32)
            rows_query = lax.dynamic_slice_in_dim(queries, start, BLK, 0)
            window_keys = lax.dynamic_slice_in_dim(keys_ext, start, BAND * BLK, 0)
            window_values = lax.dynamic_slice_in_dim(values_ext, start, BAND * BLK, 0)
            scores = jnp.dot(rows_query, window_keys.T, preferred_element_type=jnp.float32) * scale
            targets = block - REACH + jnp.arange(BAND, dtype=jnp.int32)
            allowed = (head_mask[block] > 0) & (targets >= 0) & (targets < NBLK)
            allowed_full = jnp.repeat(allowed, BLK)
            masked = jnp.where(allowed_full[None, :], scores, -1e30)
            highest = jnp.max(masked, axis=1, keepdims=True)
            weights = jnp.exp(masked - highest)
            total = jnp.sum(weights, axis=1)
            summed = jnp.dot(weights.astype(jnp.bfloat16), window_values, preferred_element_type=jnp.float32)
            result = (summed / total[:, None]).astype(jnp.bfloat16)
            return result, highest[:, 0] + jnp.log(total)

        tiles_out, tiles_lse = jax.vmap(one_tile)(jnp.arange(NBLK, dtype=jnp.int32))
        return tiles_out.reshape(TOKENS, DH), tiles_lse.reshape(TOKENS)

    head_out, head_lse = lax.map(one_head, (head_queries, head_keys, head_values, tile_mask))
    attended = head_out.transpose(1, 0, 2).reshape(TOKENS, HEADS * DH)
    slot_ids = jnp.arange(SLOTS, dtype=jnp.int32)
    placed = (head_slot[None, :] == slot_ids[:, None]).astype(jnp.float32)
    slot_lse = jnp.dot(placed, head_lse, precision=lax.Precision.HIGHEST)
    return attended, slot_lse
```

```python
import functools

import jax
import jax.numpy as jnp
from jax import lax
from jax.experimental import pallas as pl
from jax.experimental.pallas import tpu as pltpu
from jax.sharding import PartitionSpec as P

MESH = pl.DeviceIdType.MESH
HEADS_PER_CHUNK = 2
EARLY_CHUNKS = 2
HELD_CHUNKS = 3
FLOOR = -1e30


def attention_kernel(
    owners,
    slabs,
    dims,
    q_ref,
    k_ref,
    v_ref,
    mask_ref,
    slot_ref,
    out_ref,
    slot_lse_ref,
    q_buf,
    k_buf,
    v_buf,
    o_buf,
    lse_buf,
    mask_buf,
    slot_buf,
    in_send,
    in_recv,
    halo_send,
    halo_recv,
    out_send,
    out_recv,
    lse_send,
    lse_recv,
    small_sem,
):
    heads, head_dim, capacity, width, tok_dev, tile, reach = dims
    chunks = capacity // width
    lanes = width * head_dim
    tok_slab = tok_dev * owners
    tiles_dev = tok_slab // tile
    band = 2 * reach + 1
    halo = reach * tile
    full = heads == owners * capacity
    scale = head_dim ** (-0.5)
    me = lax.axis_index("head")
    slab = lax.axis_index("slab")
    inputs = ((k_ref, k_buf, halo), (v_ref, v_buf, halo), (q_ref, q_buf, 0))
    peers = [(sign, dist) for dist in range(owners - 1, 0, -1) for sign in (1, -1)]

    def when(condition, body):
        pl.when(condition)(body)

    def per_peer(body):
        for sign, dist in peers:
            other = me + sign * dist
            when((other >= 0) & (other < owners), functools.partial(body, other))

    def if_held(owner, chunk, body):
        if full:
            body()
        else:
            when(owner * capacity + chunk * width < heads, body)

    def columns(owner, chunk):
        first = (owner * capacity + chunk * width) * head_dim
        return pl.ds(pl.multiple_of(first, head_dim), lanes)

    def rows(owner, base):
        return pl.ds(pl.multiple_of(owner * tok_dev + base, tok_dev), tok_dev)

    def in_copy(which, chunk, src_owner, dst_owner):
        ref, buf, base = inputs[which]
        return pltpu.make_async_remote_copy(
            src_ref=ref.at[:, columns(dst_owner, chunk)],
            dst_ref=buf.at[chunk, rows(src_owner, base), :],
            send_sem=in_send.at[which, chunk, dst_owner],
            recv_sem=in_recv.at[which, chunk, src_owner],
            device_id={"head": dst_owner},
            device_id_type=MESH,
        )

    def own_copy(which, chunk):
        ref, buf, base = inputs[which]
        return pltpu.make_async_copy(
            ref.at[:, columns(me, chunk)],
            buf.at[chunk, rows(me, base), :],
            in_recv.at[which, chunk, me],
        )

    def halo_copy(which, chunk, up):
        buf = inputs[which][1]
        source = tok_slab if up else halo
        target = 0 if up else halo + tok_slab
        return pltpu.make_async_remote_copy(
            src_ref=buf.at[chunk, pl.ds(source, halo), :],
            dst_ref=buf.at[chunk, pl.ds(target, halo), :],
            send_sem=halo_send.at[which, chunk, int(up)],
            recv_sem=halo_recv.at[which, chunk, int(up)],
            device_id={"slab": slab + 1 if up else slab - 1},
            device_id_type=MESH,
        )

    def out_copy(chunk, src_owner, dst_owner):
        return pltpu.make_async_remote_copy(
            src_ref=o_buf.at[chunk, rows(dst_owner, 0), :],
            dst_ref=out_ref.at[:, columns(src_owner, chunk)],
            send_sem=out_send.at[chunk, dst_owner],
            recv_sem=out_recv.at[chunk, src_owner],
            device_id={"head": dst_owner},
            device_id_type=MESH,
        )

    def out_own(chunk):
        return pltpu.make_async_copy(
            o_buf.at[chunk, rows(me, 0), :],
            out_ref.at[:, columns(me, chunk)],
            out_recv.at[chunk, me],
        )

    def lse_copy(src_owner, dst_owner):
        return pltpu.make_async_remote_copy(
            src_ref=lse_buf.at[src_owner],
            dst_ref=lse_buf.at[src_owner],
            send_sem=lse_send.at[dst_owner],
            recv_sem=lse_recv.at[src_owner],
            device_id={"head": dst_owner},
            device_id_type=MESH,
        )

    has_up = slab < slabs - 1
    has_down = slab > 0
    barrier = pltpu.get_barrier_semaphore()

    def greet(other):
        pl.semaphore_signal(barrier, inc=1, device_id={"head": other}, device_id_type=MESH)

    per_peer(greet)

    @pl.when(has_up)
    def _():
        pl.semaphore_signal(barrier, inc=1, device_id={"slab": slab + 1}, device_id_type=MESH)

    @pl.when(has_down)
    def _():
        pl.semaphore_signal(barrier, inc=1, device_id={"slab": slab - 1}, device_id_type=MESH)

    mask_copy = pltpu.make_async_copy(mask_ref, mask_buf, small_sem.at[0])
    slot_copy = pltpu.make_async_copy(slot_ref, slot_buf, small_sem.at[1])
    mask_copy.start()
    slot_copy.start()
    pl.semaphore_wait(
        barrier, owners - 1 + has_up.astype(jnp.int32) + has_down.astype(jnp.int32)
    )

    low_half = me < owners // 2

    def send_inputs(crossing, chunk, carry):
        for which in range(3):

            def to_peer(other, which=which):
                def go():
                    if_held(other, chunk, lambda: in_copy(which, chunk, me, other).start())

                other_side = low_half != (other < owners // 2)
                when(other_side if crossing else jnp.logical_not(other_side), go)

            per_peer(to_peer)
            if crossing:
                if_held(me, chunk, lambda which=which: own_copy(which, chunk).start())
        return carry

    lax.fori_loop(0, chunks, functools.partial(send_inputs, False), 0)
    lax.fori_loop(0, chunks, functools.partial(send_inputs, True), 0)

    if not full:
        lse_buf[me] = jnp.zeros(lse_buf.shape[1:], jnp.float32)

    @pl.when(jnp.logical_not(has_down))
    def _():
        v_buf[:, :halo, :] = jnp.zeros((chunks, halo, lanes), jnp.bfloat16)

    @pl.when(jnp.logical_not(has_up))
    def _():
        v_buf[:, halo + tok_slab :, :] = jnp.zeros((chunks, halo, lanes), jnp.bfloat16)

    mask_copy.wait()
    slot_copy.wait()

    def wait_input(which, chunk):
        per_peer(lambda other: in_copy(which, chunk, other, me).wait_recv())
        own_copy(which, chunk).wait()

    def forward(chunk):
        for which in range(2):
            wait_input(which, chunk)
            when(has_up, lambda: halo_copy(which, chunk, True).start())
            when(has_down, lambda: halo_copy(which, chunk, False).start())

    def attend(chunk):
        for which in range(2):
            when(has_down, lambda: halo_copy(which, chunk, True).wait_recv())
            when(has_up, lambda: halo_copy(which, chunk, False).wait_recv())
        wait_input(2, chunk)
        for within in range(width):
            column = slice(within * head_dim, (within + 1) * head_dim)
            local_head = chunk * width + within
            global_head = me * capacity + local_head
            for block in range(tiles_dev):
                q_rows = slice(block * tile, (block + 1) * tile)
                queries = q_buf[chunk, q_rows, column]
                window = slice(block * tile, (block + band) * tile)
                keys = k_buf[chunk, window, column]
                values = v_buf[chunk, window, column]
                scores = (
                    lax.dot_general(
                        keys, queries, (((1,), (1,)), ((), ())), preferred_element_type=jnp.float32
                    )
                    * scale
                )
                parts = []
                for place in range(band):
                    key_tile = slab * tiles_dev + block + place - reach
                    inside = ((key_tile >= 0) & (key_tile < slabs * tiles_dev)).astype(jnp.int32)
                    flag = mask_buf[place, block, global_head] * inside
                    allowed = jnp.full((tile, tile), flag, jnp.int32) > 0
                    parts.append(
                        jnp.where(allowed, scores[place * tile : (place + 1) * tile], FLOOR)
                    )
                masked = jnp.concatenate(parts, axis=0)
                highest = jnp.max(masked, axis=0, keepdims=True)
                weights = jnp.exp(masked - highest)
                total = jnp.sum(weights, axis=0, keepdims=True)
                summed = lax.dot_general(
                    values,
                    weights.astype(jnp.bfloat16),
                    (((0,), (0,)), ((), ())),
                    preferred_element_type=jnp.float32,
                )
                result = jnp.transpose(summed / total)
                o_buf[chunk, q_rows, column] = result.astype(jnp.bfloat16)
                lse_buf[me, local_head, :, q_rows] = highest + jnp.log(total)

    def send_out(chunk):
        per_peer(lambda other: out_copy(chunk, me, other).start())
        out_own(chunk).start()

    if_held(me, 0, lambda: forward(0))

    def step(chunk, carry):
        if_held(me, chunk, lambda: forward(chunk))

        def finish():
            attend(chunk - 1)
            send_out(chunk - 1)

        if_held(me, chunk - 1, finish)
        return carry

    lax.fori_loop(1, chunks, step, 0)
    last = chunks - 1
    if_held(me, last, lambda: attend(last))
    per_peer(lambda other: lse_copy(me, other).start())
    if_held(me, last, lambda: send_out(last))

    per_peer(lambda other: lse_copy(other, me).wait_recv())
    slot_rows = lax.broadcasted_iota(jnp.int32, (capacity, tok_slab), 0) + me * capacity
    slot_lse = jnp.zeros((capacity, tok_slab), jnp.float32)
    for head in range(heads):
        row = jnp.broadcast_to(lse_buf[head // capacity, head % capacity], (capacity, tok_slab))
        slot_lse = jnp.where(slot_rows == slot_buf[head], row, slot_lse)
    slot_lse_ref[...] = slot_lse

    def drain(chunk, carry):
        for which in range(3):

            def sent(other, which=which):
                if_held(other, chunk, lambda: in_copy(which, chunk, me, other).wait_send())

            per_peer(sent)

        def mine():
            for which in range(2):
                when(has_up, lambda: halo_copy(which, chunk, True).wait_send())
                when(has_down, lambda: halo_copy(which, chunk, False).wait_send())
            per_peer(lambda other: out_copy(chunk, me, other).wait_send())
            out_own(chunk).wait()

        if_held(me, chunk, mine)

        def arrived(other):
            if_held(other, chunk, lambda: out_copy(chunk, other, me).wait_recv())

        per_peer(arrived)
        return carry

    lax.fori_loop(0, chunks, drain, 0)
    per_peer(lambda other: lse_copy(me, other).wait_send())


def line_kernel(
    owners,
    slabs,
    dims,
    q_ref,
    k_ref,
    v_ref,
    mask_ref,
    slot_ref,
    out_ref,
    slot_lse_ref,
    q_buf,
    k_buf,
    v_buf,
    o_buf,
    lse_buf,
    lse_box,
    mask_buf,
    slot_buf,
    in_send,
    in_recv,
    halo_send,
    halo_recv,
    out_send,
    out_recv,
    lse_send,
    lse_recv,
    seen,
    small_sem,
):
    heads, head_dim, capacity, width, tok_dev, tile, reach = dims
    chunks = capacity // width
    lanes = width * head_dim
    tok_slab = tok_dev * owners
    tiles_dev = tok_slab // tile
    band = 2 * reach + 1
    halo = reach * tile
    mid = owners // 2
    early = min(EARLY_CHUNKS, chunks)
    hold_from = max(chunks - HELD_CHUNKS, 0)
    scale = head_dim ** (-0.5)
    me = lax.axis_index("head")
    slab = lax.axis_index("slab")
    low = me < mid
    inward = jnp.where(low, 1, -1)
    inner = me + inward
    outer = me - inward
    across = jnp.where(low, mid, mid - 1)
    has_up = slab < slabs - 1
    has_down = slab > 0
    inputs = ((k_ref, k_buf, halo), (v_ref, v_buf, halo), (q_ref, q_buf, 0))
    peers = [(sign, dist) for dist in range(owners - 1, 0, -1) for sign in (1, -1)]

    def when(condition, body):
        pl.when(condition)(body)

    def exists(other):
        return (other >= 0) & (other < owners)

    def columns(owner, chunk):
        first = (owner * capacity + chunk * width) * head_dim
        return pl.ds(pl.multiple_of(first, head_dim), lanes)

    def rows(owner, base):
        return pl.ds(pl.multiple_of(owner * tok_dev + base, tok_dev), tok_dev)

    def wait_bytes(ref, sem):
        pltpu.make_async_copy(ref, ref, sem).wait()

    def in_copy(which, chunk, dst_owner):
        ref, buf, base = inputs[which]
        return pltpu.make_async_remote_copy(
            src_ref=ref.at[:, columns(dst_owner, chunk)],
            dst_ref=buf.at[chunk, rows(me, base), :],
            send_sem=in_send.at[which],
            recv_sem=in_recv.at[which, chunk],
            device_id={"head": dst_owner},
            device_id_type=MESH,
        )

    def own_copy(which, chunk):
        ref, buf, base = inputs[which]
        return pltpu.make_async_copy(
            ref.at[:, columns(me, chunk)],
            buf.at[chunk, rows(me, base), :],
            in_recv.at[which, chunk],
        )

    def halo_copy(which, chunk, up):
        buf = inputs[which][1]
        source = tok_slab if up else halo
        target = 0 if up else halo + tok_slab
        return pltpu.make_async_remote_copy(
            src_ref=buf.at[chunk, pl.ds(source, halo), :],
            dst_ref=buf.at[chunk, pl.ds(target, halo), :],
            send_sem=halo_send.at[which, int(up)],
            recv_sem=halo_recv.at[which, chunk, int(up)],
            device_id={"slab": slab + 1 if up else slab - 1},
            device_id_type=MESH,
        )

    def out_copy(chunk, dst_owner):
        return pltpu.make_async_remote_copy(
            src_ref=o_buf.at[chunk, rows(dst_owner, 0), :],
            dst_ref=out_ref.at[:, columns(me, chunk)],
            send_sem=out_send.at[0],
            recv_sem=out_recv.at[0],
            device_id={"head": dst_owner},
            device_id_type=MESH,
        )

    def out_own(chunk):
        return pltpu.make_async_copy(
            o_buf.at[chunk, rows(me, 0), :],
            out_ref.at[:, columns(me, chunk)],
            out_recv.at[0],
        )

    def lse_copy(dst_owner):
        return pltpu.make_async_remote_copy(
            src_ref=lse_box.at[me],
            dst_ref=lse_box.at[me],
            send_sem=lse_send.at[0],
            recv_sem=lse_recv.at[0],
            device_id={"head": dst_owner},
            device_id_type=MESH,
        )

    barrier = pltpu.get_barrier_semaphore()

    def greet(device):
        pl.semaphore_signal(barrier, inc=1, device_id=device, device_id_type=MESH)

    when(inner == across, lambda: greet({"head": inner}))
    when(exists(outer), lambda: greet({"head": outer}))
    when(has_up, lambda: greet({"slab": slab + 1}))
    when(has_down, lambda: greet({"slab": slab - 1}))

    mask_copy = pltpu.make_async_copy(mask_ref, mask_buf, small_sem.at[0])
    slot_copy = pltpu.make_async_copy(slot_ref, slot_buf, small_sem.at[1])
    mask_copy.start()
    slot_copy.start()
    pl.semaphore_wait(barrier, 1 + has_up.astype(jnp.int32) + has_down.astype(jnp.int32))

    for chunk in range(early):
        for which in range(3):
            in_copy(which, chunk, inner).start()

    def tell(owner, about):
        pl.semaphore_signal(seen.at[about], inc=1, device_id={"head": owner}, device_id_type=MESH)

    when(inner != across, lambda: tell(inner, me))
    for dist in range(1, mid):
        other = me - inward * dist

        def outward(other=other, dist=dist):
            pl.semaphore_wait(seen.at[other], 1)
            tell(inner, other)
            if dist == 1:
                tell(outer, inner)

        when(exists(other), outward)
    for dist in range(2, owners):
        other = me + inward * dist

        def further(other=other):
            pl.semaphore_wait(seen.at[other], 1)
            when(exists(outer), lambda: tell(outer, other))

        when(exists(other), further)

    def send_inputs(chunk, carry):
        for which in range(3):
            for sign, dist in peers:
                other = me + sign * dist
                wanted = exists(other)
                if dist == 1:
                    wanted = wanted & ((other != inner) | (chunk >= early))
                when(wanted, lambda which=which, other=other: in_copy(which, chunk, other).start())
            own_copy(which, chunk).start()
        return carry

    lax.fori_loop(0, chunks, send_inputs, 0)

    @pl.when(jnp.logical_not(has_down))
    def _():
        v_buf[:, :halo, :] = jnp.zeros((chunks, halo, lanes), jnp.bfloat16)

    @pl.when(jnp.logical_not(has_up))
    def _():
        v_buf[:, halo + tok_slab :, :] = jnp.zeros((chunks, halo, lanes), jnp.bfloat16)

    mask_copy.wait()
    slot_copy.wait()

    def wait_input(which, chunk):
        _, buf, base = inputs[which]
        wait_bytes(buf.at[chunk, pl.ds(base, tok_slab), :], in_recv.at[which, chunk])

    def forward(chunk):
        for which in range(2):
            wait_input(which, chunk)
            when(has_up, lambda which=which: halo_copy(which, chunk, True).start())
            when(has_down, lambda which=which: halo_copy(which, chunk, False).start())

    def attend(chunk):
        for which in range(2):
            when(has_down, lambda which=which: halo_copy(which, chunk, True).wait_recv())
            when(has_up, lambda which=which: halo_copy(which, chunk, False).wait_recv())
        wait_input(2, chunk)
        for within in range(width):
            column = slice(within * head_dim, (within + 1) * head_dim)
            local_head = chunk * width + within
            global_head = me * capacity + local_head
            for block in range(tiles_dev):
                q_rows = slice(block * tile, (block + 1) * tile)
                queries = q_buf[chunk, q_rows, column]
                window = slice(block * tile, (block + band) * tile)
                keys = k_buf[chunk, window, column]
                values = v_buf[chunk, window, column]
                scores = (
                    lax.dot_general(
                        keys, queries, (((1,), (1,)), ((), ())), preferred_element_type=jnp.float32
                    )
                    * scale
                )
                parts = []
                for place in range(band):
                    key_tile = slab * tiles_dev + block + place - reach
                    inside = ((key_tile >= 0) & (key_tile < slabs * tiles_dev)).astype(jnp.int32)
                    flag = mask_buf[place, block, global_head] * inside
                    allowed = jnp.full((tile, tile), flag, jnp.int32) > 0
                    parts.append(
                        jnp.where(allowed, scores[place * tile : (place + 1) * tile], FLOOR)
                    )
                masked = jnp.concatenate(parts, axis=0)
                highest = jnp.max(masked, axis=0, keepdims=True)
                weights = jnp.exp(masked - highest)
                total = jnp.sum(weights, axis=0, keepdims=True)
                summed = lax.dot_general(
                    values,
                    weights.astype(jnp.bfloat16),
                    (((0,), (0,)), ((), ())),
                    preferred_element_type=jnp.float32,
                )
                result = jnp.transpose(summed / total)
                o_buf[chunk, q_rows, column] = result.astype(jnp.bfloat16)
                lse_buf[local_head, :, q_rows] = highest + jnp.log(total)

    def send_out(chunk):
        for sign, dist in peers:
            other = me + sign * dist
            wanted = exists(other) & ((other != across) | (chunk < hold_from))
            when(wanted, lambda other=other: out_copy(chunk, other).start())
        out_own(chunk).start()

    forward(0)

    def step(chunk, carry):
        when(chunk < chunks, lambda: forward(chunk))
        attend(chunk - 1)
        send_out(chunk - 1)
        return carry

    lax.fori_loop(1, chunks + 1, step, 0)

    own_lse = lse_buf[...].reshape(capacity, tok_slab)
    lse_box[me] = own_lse.astype(jnp.bfloat16)
    for sign, dist in peers:
        other = me + sign * dist
        when(exists(other), lambda other=other: lse_copy(other).start())
    for chunk in range(hold_from, chunks):
        out_copy(chunk, across).start()

    wait_bytes(lse_box.at[pl.ds(0, owners - 1)], lse_recv.at[0])
    slot_rows = lax.broadcasted_iota(jnp.int32, (capacity, tok_slab), 0) + me * capacity
    slot_lse = jnp.zeros((capacity, tok_slab), jnp.float32)
    for owner in range(owners):
        own = jnp.full((capacity, tok_slab), (me == owner).astype(jnp.int32)) > 0
        theirs = jnp.where(own, own_lse, lse_box[owner].astype(jnp.float32))
        for within in range(capacity):
            row = jnp.broadcast_to(theirs[within : within + 1], (capacity, tok_slab))
            slot_lse = jnp.where(slot_rows == slot_buf[owner * capacity + within], row, slot_lse)
    slot_lse_ref[...] = slot_lse

    others = (owners - 1) * capacity * head_dim
    for which in range(3):
        wait_bytes(inputs[which][0].at[:, pl.ds(0, others)], in_send.at[which])
    for which in range(2):
        edge = inputs[which][1].at[:, pl.ds(0, halo), :]
        when(has_up, lambda which=which, edge=edge: wait_bytes(edge, halo_send.at[which, 1]))
        when(has_down, lambda which=which, edge=edge: wait_bytes(edge, halo_send.at[which, 0]))
    wait_bytes(lse_box.at[pl.ds(0, owners - 1)], lse_send.at[0])
    wait_bytes(o_buf.at[:, pl.ds(0, (owners - 1) * tok_dev), :], out_send.at[0])
    wait_bytes(out_ref, out_recv.at[0])


def hand_over_kernel(out_in, lse_in, out_ref, lse_ref, sems):
    copies = [
        pltpu.make_async_copy(out_in, out_ref, sems.at[0]),
        pltpu.make_async_copy(lse_in, lse_ref, sems.at[1]),
    ]
    for copy in copies:
        copy.start()
    for copy in copies:
        copy.wait()


def on_device(query_rows, key_rows, value_rows, tile_mask, head_slot):
    owners = lax.axis_size("head")
    slabs = lax.axis_size("slab")
    tok_dev, model = query_rows.shape
    heads, tiles_dev, band = tile_mask.shape
    head_dim = model // heads
    capacity = (heads + owners - 1) // owners
    reach = (band - 1) // 2
    tok_slab = tok_dev * owners
    tile = tok_slab // tiles_dev
    halo = reach * tile
    whole = heads == owners * capacity
    line = whole and owners % 2 == 0
    width = HEADS_PER_CHUNK if whole and capacity % HEADS_PER_CHUNK == 0 else 1
    chunks = capacity // width
    lanes = width * head_dim
    dims = (heads, head_dim, capacity, width, tok_dev, tile, reach)
    dma = pltpu.SemaphoreType.DMA
    buffers = [
        pltpu.VMEM((chunks, tok_slab, lanes), jnp.bfloat16),
        pltpu.VMEM((chunks, tok_slab + 2 * halo, lanes), jnp.bfloat16),
        pltpu.VMEM((chunks, tok_slab + 2 * halo, lanes), jnp.bfloat16),
        pltpu.VMEM((chunks, tok_slab, lanes), jnp.bfloat16),
    ]
    tables = [
        pltpu.SMEM((band, tiles_dev, heads), jnp.int32),
        pltpu.SMEM((heads,), jnp.int32),
    ]
    if line:
        kernel = line_kernel
        scratch = [
            *buffers,
            pltpu.VMEM((capacity, 1, tok_slab), jnp.float32),
            pltpu.VMEM((owners, capacity, tok_slab), jnp.bfloat16),
            *tables,
            dma((3,)),
            dma((3, chunks)),
            dma((2, 2)),
            dma((2, chunks, 2)),
            dma((1,)),
            dma((1,)),
            dma((1,)),
            dma((1,)),
            pltpu.SemaphoreType.REGULAR((owners,)),
            dma((2,)),
        ]
    else:
        kernel = attention_kernel
        scratch = [
            *buffers,
            pltpu.VMEM((owners, capacity, 1, tok_slab), jnp.float32),
            *tables,
            dma((3, chunks, owners)),
            dma((3, chunks, owners)),
            dma((2, chunks, 2)),
            dma((2, chunks, 2)),
            dma((chunks, owners)),
            dma((chunks, owners)),
            dma((owners,)),
            dma((owners,)),
            dma((2,)),
        ]
    gathered, gathered_lse = pl.pallas_call(
        functools.partial(kernel, owners, slabs, dims),
        out_shape=(
            jax.ShapeDtypeStruct((tok_dev, model), jnp.bfloat16),
            jax.ShapeDtypeStruct((capacity, tok_slab), jnp.float32),
        ),
        in_specs=[pl.BlockSpec(memory_space=pltpu.HBM)] * 5,
        out_specs=(pl.BlockSpec(memory_space=pltpu.VMEM), pl.BlockSpec(memory_space=pltpu.VMEM)),
        scratch_shapes=scratch,
        compiler_params=pltpu.CompilerParams(collective_id=0, has_side_effects=True, vmem_limit_bytes=16 << 20),
    )(*[pltpu.with_memory_space_constraint(x, pltpu.HBM) for x in (query_rows, key_rows, value_rows, jnp.transpose(tile_mask, (2, 1, 0)), head_slot)])
    vmem = pl.BlockSpec(memory_space=pltpu.VMEM)
    hbm = pl.BlockSpec(memory_space=pltpu.HBM)
    return pl.pallas_call(
        hand_over_kernel,
        out_shape=(
            jax.ShapeDtypeStruct(gathered.shape, gathered.dtype),
            jax.ShapeDtypeStruct(gathered_lse.shape, gathered_lse.dtype),
        ),
        in_specs=[vmem, vmem],
        out_specs=(hbm, hbm),
        scratch_shapes=[dma((2,))],
        compiler_params=pltpu.CompilerParams(vmem_limit_bytes=16 << 20),
    )(gathered, gathered_lse)


def solution(mesh):
    in_specs = (
        P(("groups", "slab", "head"), None),
        P(("groups", "slab", "head"), None),
        P(("groups", "slab", "head"), None),
        P(None, ("groups", "slab"), None),
        P(),
    )
    out_specs = (P(("groups", "slab", "head"), None), P("head", ("groups", "slab")))
    return jax.shard_map(
        on_device, mesh=mesh, in_specs=in_specs, out_specs=out_specs, check_vma=False
    )
```

```python
import functools

import jax
import jax.numpy as jnp
from jax import lax
from jax.experimental import pallas as pl
from jax.experimental.pallas import tpu as pltpu
from jax.sharding import PartitionSpec as P

MESH = pl.DeviceIdType.MESH
HEADS_PER_CHUNK = 2
EARLY_CHUNKS = 2
HELD_CHUNKS = 4
FLOOR = -1e30


def attention_kernel(
    owners,
    slabs,
    dims,
    q_ref,
    k_ref,
    v_ref,
    mask_ref,
    slot_ref,
    out_ref,
    slot_lse_ref,
    q_buf,
    k_buf,
    v_buf,
    o_buf,
    lse_buf,
    mask_buf,
    slot_buf,
    in_send,
    in_recv,
    halo_send,
    halo_recv,
    out_send,
    out_recv,
    lse_send,
    lse_recv,
    small_sem,
):
    heads, head_dim, capacity, width, tok_dev, tile, reach = dims
    chunks = capacity // width
    lanes = width * head_dim
    tok_slab = tok_dev * owners
    tiles_dev = tok_slab // tile
    band = 2 * reach + 1
    halo = reach * tile
    full = heads == owners * capacity
    scale = head_dim ** (-0.5)
    me = lax.axis_index("head")
    slab = lax.axis_index("slab")
    inputs = ((k_ref, k_buf, halo), (v_ref, v_buf, halo), (q_ref, q_buf, 0))
    peers = [(sign, dist) for dist in range(owners - 1, 0, -1) for sign in (1, -1)]

    def when(condition, body):
        pl.when(condition)(body)

    def per_peer(body):
        for sign, dist in peers:
            other = me + sign * dist
            when((other >= 0) & (other < owners), functools.partial(body, other))

    def if_held(owner, chunk, body):
        if full:
            body()
        else:
            when(owner * capacity + chunk * width < heads, body)

    def columns(owner, chunk):
        first = (owner * capacity + chunk * width) * head_dim
        return pl.ds(pl.multiple_of(first, head_dim), lanes)

    def rows(owner, base):
        return pl.ds(pl.multiple_of(owner * tok_dev + base, tok_dev), tok_dev)

    def in_copy(which, chunk, src_owner, dst_owner):
        ref, buf, base = inputs[which]
        return pltpu.make_async_remote_copy(
            src_ref=ref.at[:, columns(dst_owner, chunk)],
            dst_ref=buf.at[chunk, rows(src_owner, base), :],
            send_sem=in_send.at[which, chunk, dst_owner],
            recv_sem=in_recv.at[which, chunk, src_owner],
            device_id={"head": dst_owner},
            device_id_type=MESH,
        )

    def own_copy(which, chunk):
        ref, buf, base = inputs[which]
        return pltpu.make_async_copy(
            ref.at[:, columns(me, chunk)],
            buf.at[chunk, rows(me, base), :],
            in_recv.at[which, chunk, me],
        )

    def halo_copy(which, chunk, up):
        buf = inputs[which][1]
        source = tok_slab if up else halo
        target = 0 if up else halo + tok_slab
        return pltpu.make_async_remote_copy(
            src_ref=buf.at[chunk, pl.ds(source, halo), :],
            dst_ref=buf.at[chunk, pl.ds(target, halo), :],
            send_sem=halo_send.at[which, chunk, int(up)],
            recv_sem=halo_recv.at[which, chunk, int(up)],
            device_id={"slab": slab + 1 if up else slab - 1},
            device_id_type=MESH,
        )

    def out_copy(chunk, src_owner, dst_owner):
        return pltpu.make_async_remote_copy(
            src_ref=o_buf.at[chunk, rows(dst_owner, 0), :],
            dst_ref=out_ref.at[:, columns(src_owner, chunk)],
            send_sem=out_send.at[chunk, dst_owner],
            recv_sem=out_recv.at[chunk, src_owner],
            device_id={"head": dst_owner},
            device_id_type=MESH,
        )

    def out_own(chunk):
        return pltpu.make_async_copy(
            o_buf.at[chunk, rows(me, 0), :],
            out_ref.at[:, columns(me, chunk)],
            out_recv.at[chunk, me],
        )

    def lse_copy(src_owner, dst_owner):
        return pltpu.make_async_remote_copy(
            src_ref=lse_buf.at[src_owner],
            dst_ref=lse_buf.at[src_owner],
            send_sem=lse_send.at[dst_owner],
            recv_sem=lse_recv.at[src_owner],
            device_id={"head": dst_owner},
            device_id_type=MESH,
        )

    has_up = slab < slabs - 1
    has_down = slab > 0
    barrier = pltpu.get_barrier_semaphore()

    def greet(other):
        pl.semaphore_signal(barrier, inc=1, device_id={"head": other}, device_id_type=MESH)

    per_peer(greet)

    @pl.when(has_up)
    def _():
        pl.semaphore_signal(barrier, inc=1, device_id={"slab": slab + 1}, device_id_type=MESH)

    @pl.when(has_down)
    def _():
        pl.semaphore_signal(barrier, inc=1, device_id={"slab": slab - 1}, device_id_type=MESH)

    mask_copy = pltpu.make_async_copy(mask_ref, mask_buf, small_sem.at[0])
    slot_copy = pltpu.make_async_copy(slot_ref, slot_buf, small_sem.at[1])
    mask_copy.start()
    slot_copy.start()
    pl.semaphore_wait(
        barrier, owners - 1 + has_up.astype(jnp.int32) + has_down.astype(jnp.int32)
    )

    low_half = me < owners // 2

    def send_inputs(crossing, chunk, carry):
        for which in range(3):

            def to_peer(other, which=which):
                def go():
                    if_held(other, chunk, lambda: in_copy(which, chunk, me, other).start())

                other_side = low_half != (other < owners // 2)
                when(other_side if crossing else jnp.logical_not(other_side), go)

            per_peer(to_peer)
            if crossing:
                if_held(me, chunk, lambda which=which: own_copy(which, chunk).start())
        return carry

    lax.fori_loop(0, chunks, functools.partial(send_inputs, False), 0)
    lax.fori_loop(0, chunks, functools.partial(send_inputs, True), 0)

    if not full:
        lse_buf[me] = jnp.zeros(lse_buf.shape[1:], jnp.float32)

    @pl.when(jnp.logical_not(has_down))
    def _():
        v_buf[:, :halo, :] = jnp.zeros((chunks, halo, lanes), jnp.bfloat16)

    @pl.when(jnp.logical_not(has_up))
    def _():
        v_buf[:, halo + tok_slab :, :] = jnp.zeros((chunks, halo, lanes), jnp.bfloat16)

    mask_copy.wait()
    slot_copy.wait()

    def wait_input(which, chunk):
        per_peer(lambda other: in_copy(which, chunk, other, me).wait_recv())
        own_copy(which, chunk).wait()

    def forward(chunk):
        for which in range(2):
            wait_input(which, chunk)
            when(has_up, lambda: halo_copy(which, chunk, True).start())
            when(has_down, lambda: halo_copy(which, chunk, False).start())

    def attend(chunk):
        for which in range(2):
            when(has_down, lambda: halo_copy(which, chunk, True).wait_recv())
            when(has_up, lambda: halo_copy(which, chunk, False).wait_recv())
        wait_input(2, chunk)
        for within in range(width):
            column = slice(within * head_dim, (within + 1) * head_dim)
            local_head = chunk * width + within
            global_head = me * capacity + local_head
            for block in range(tiles_dev):
                q_rows = slice(block * tile, (block + 1) * tile)
                queries = q_buf[chunk, q_rows, column]
                window = slice(block * tile, (block + band) * tile)
                keys = k_buf[chunk, window, column]
                values = v_buf[chunk, window, column]
                scores = (
                    lax.dot_general(
                        keys, queries, (((1,), (1,)), ((), ())), preferred_element_type=jnp.float32
                    )
                    * scale
                )
                parts = []
                for place in range(band):
                    key_tile = slab * tiles_dev + block + place - reach
                    inside = ((key_tile >= 0) & (key_tile < slabs * tiles_dev)).astype(jnp.int32)
                    flag = mask_buf[place, block, global_head] * inside
                    allowed = jnp.full((tile, tile), flag, jnp.int32) > 0
                    parts.append(
                        jnp.where(allowed, scores[place * tile : (place + 1) * tile], FLOOR)
                    )
                masked = jnp.concatenate(parts, axis=0)
                highest = jnp.max(masked, axis=0, keepdims=True)
                weights = jnp.exp(masked - highest)
                total = jnp.sum(weights, axis=0, keepdims=True)
                summed = lax.dot_general(
                    values,
                    weights.astype(jnp.bfloat16),
                    (((0,), (0,)), ((), ())),
                    preferred_element_type=jnp.float32,
                )
                result = jnp.transpose(summed / total)
                o_buf[chunk, q_rows, column] = result.astype(jnp.bfloat16)
                lse_buf[me, local_head, :, q_rows] = highest + jnp.log(total)

    def send_out(chunk):
        per_peer(lambda other: out_copy(chunk, me, other).start())
        out_own(chunk).start()

    if_held(me, 0, lambda: forward(0))

    def step(chunk, carry):
        if_held(me, chunk, lambda: forward(chunk))

        def finish():
            attend(chunk - 1)
            send_out(chunk - 1)

        if_held(me, chunk - 1, finish)
        return carry

    lax.fori_loop(1, chunks, step, 0)
    last = chunks - 1
    if_held(me, last, lambda: attend(last))
    per_peer(lambda other: lse_copy(me, other).start())
    if_held(me, last, lambda: send_out(last))

    per_peer(lambda other: lse_copy(other, me).wait_recv())
    slot_rows = lax.broadcasted_iota(jnp.int32, (capacity, tok_slab), 0) + me * capacity
    slot_lse = jnp.zeros((capacity, tok_slab), jnp.float32)
    for head in range(heads):
        row = jnp.broadcast_to(lse_buf[head // capacity, head % capacity], (capacity, tok_slab))
        slot_lse = jnp.where(slot_rows == slot_buf[head], row, slot_lse)
    slot_lse_ref[...] = slot_lse

    def drain(chunk, carry):
        for which in range(3):

            def sent(other, which=which):
                if_held(other, chunk, lambda: in_copy(which, chunk, me, other).wait_send())

            per_peer(sent)

        def mine():
            for which in range(2):
                when(has_up, lambda: halo_copy(which, chunk, True).wait_send())
                when(has_down, lambda: halo_copy(which, chunk, False).wait_send())
            per_peer(lambda other: out_copy(chunk, me, other).wait_send())
            out_own(chunk).wait()

        if_held(me, chunk, mine)

        def arrived(other):
            if_held(other, chunk, lambda: out_copy(chunk, other, me).wait_recv())

        per_peer(arrived)
        return carry

    lax.fori_loop(0, chunks, drain, 0)
    per_peer(lambda other: lse_copy(me, other).wait_send())


def line_kernel(
    owners,
    slabs,
    dims,
    q_ref,
    k_ref,
    v_ref,
    mask_ref,
    slot_ref,
    out_ref,
    slot_lse_ref,
    q_buf,
    k_buf,
    v_buf,
    o_buf,
    lse_buf,
    lse_box,
    last_box,
    mask_buf,
    slot_buf,
    in_send,
    in_recv,
    halo_send,
    halo_recv,
    out_send,
    out_recv,
    lse_send,
    lse_recv,
    seen,
    small_sem,
):
    heads, head_dim, capacity, width, tok_dev, tile, reach = dims
    chunks = capacity // width
    lanes = width * head_dim
    tok_slab = tok_dev * owners
    tiles_dev = tok_slab // tile
    band = 2 * reach + 1
    halo = reach * tile
    mid = owners // 2
    early = min(EARLY_CHUNKS, chunks)
    hold_from = max(chunks - HELD_CHUNKS, 0)
    first_rows = (capacity - width) * tiles_dev
    scale = head_dim ** (-0.5)
    me = lax.axis_index("head")
    slab = lax.axis_index("slab")
    low = me < mid
    inward = jnp.where(low, 1, -1)
    inner = me + inward
    outer = me - inward
    across = jnp.where(low, mid, mid - 1)
    has_up = slab < slabs - 1
    has_down = slab > 0
    inputs = ((k_ref, k_buf, halo), (v_ref, v_buf, halo), (q_ref, q_buf, 0))
    peers = [(sign, dist) for dist in range(owners - 1, 0, -1) for sign in (1, -1)]

    def when(condition, body):
        pl.when(condition)(body)

    def exists(other):
        return (other >= 0) & (other < owners)

    def columns(owner, chunk):
        first = (owner * capacity + chunk * width) * head_dim
        return pl.ds(pl.multiple_of(first, head_dim), lanes)

    def rows(owner, base):
        return pl.ds(pl.multiple_of(owner * tok_dev + base, tok_dev), tok_dev)

    def wait_bytes(ref, sem):
        pltpu.make_async_copy(ref, ref, sem).wait()

    def in_copy(which, chunk, dst_owner):
        ref, buf, base = inputs[which]
        return pltpu.make_async_remote_copy(
            src_ref=ref.at[:, columns(dst_owner, chunk)],
            dst_ref=buf.at[chunk, rows(me, base), :],
            send_sem=in_send.at[which],
            recv_sem=in_recv.at[which, chunk],
            device_id={"head": dst_owner},
            device_id_type=MESH,
        )

    def own_copy(which, chunk):
        ref, buf, base = inputs[which]
        return pltpu.make_async_copy(
            ref.at[:, columns(me, chunk)],
            buf.at[chunk, rows(me, base), :],
            in_recv.at[which, chunk],
        )

    def halo_copy(which, chunk, up):
        buf = inputs[which][1]
        source = tok_slab if up else halo
        target = 0 if up else halo + tok_slab
        return pltpu.make_async_remote_copy(
            src_ref=buf.at[chunk, pl.ds(source, halo), :],
            dst_ref=buf.at[chunk, pl.ds(target, halo), :],
            send_sem=halo_send.at[which, int(up)],
            recv_sem=halo_recv.at[which, chunk, int(up)],
            device_id={"slab": slab + 1 if up else slab - 1},
            device_id_type=MESH,
        )

    def out_copy(chunk, dst_owner):
        return pltpu.make_async_remote_copy(
            src_ref=o_buf.at[chunk, rows(dst_owner, 0), :],
            dst_ref=out_ref.at[:, columns(me, chunk)],
            send_sem=out_send.at[0],
            recv_sem=out_recv.at[0],
            device_id={"head": dst_owner},
            device_id_type=MESH,
        )

    def out_own(chunk):
        return pltpu.make_async_copy(
            o_buf.at[chunk, rows(me, 0), :],
            out_ref.at[:, columns(me, chunk)],
            out_recv.at[0],
        )

    def lse_copy(dst_owner, crossing):
        return pltpu.make_async_remote_copy(
            src_ref=lse_box.at[me],
            dst_ref=lse_box.at[me],
            send_sem=lse_send.at[owners],
            recv_sem=lse_recv.at[int(crossing)],
            device_id={"head": dst_owner},
            device_id_type=MESH,
        )

    def lse_relay(dst_owner):
        boxes = lse_box.at[pl.ds(jnp.where(low, mid, 0), mid)]
        return pltpu.make_async_remote_copy(
            src_ref=boxes,
            dst_ref=boxes,
            send_sem=lse_send.at[dst_owner],
            recv_sem=lse_recv.at[1],
            device_id={"head": dst_owner},
            device_id_type=MESH,
        )

    def last_copy(dst_owner):
        return pltpu.make_async_remote_copy(
            src_ref=last_box.at[me],
            dst_ref=last_box.at[me],
            send_sem=lse_send.at[owners + 1],
            recv_sem=lse_recv.at[2],
            device_id={"head": dst_owner},
            device_id_type=MESH,
        )

    barrier = pltpu.get_barrier_semaphore()

    def greet(device):
        pl.semaphore_signal(barrier, inc=1, device_id=device, device_id_type=MESH)

    when(inner == across, lambda: greet({"head": inner}))
    when(exists(outer), lambda: greet({"head": outer}))
    when(has_up, lambda: greet({"slab": slab + 1}))
    when(has_down, lambda: greet({"slab": slab - 1}))

    mask_copy = pltpu.make_async_copy(mask_ref, mask_buf, small_sem.at[0])
    slot_copy = pltpu.make_async_copy(slot_ref, slot_buf, small_sem.at[1])
    mask_copy.start()
    slot_copy.start()
    pl.semaphore_wait(barrier, 1 + has_up.astype(jnp.int32) + has_down.astype(jnp.int32))

    for chunk in range(early):
        for which in range(3):
            in_copy(which, chunk, inner).start()

    def tell(owner, about):
        pl.semaphore_signal(seen.at[about], inc=1, device_id={"head": owner}, device_id_type=MESH)

    when(inner != across, lambda: tell(inner, me))
    for dist in range(1, mid):
        other = me - inward * dist

        def outward(other=other, dist=dist):
            pl.semaphore_wait(seen.at[other], 1)
            tell(inner, other)
            if dist == 1:
                tell(outer, inner)

        when(exists(other), outward)
    for dist in range(2, owners):
        other = me + inward * dist

        def further(other=other):
            pl.semaphore_wait(seen.at[other], 1)
            when(exists(outer), lambda: tell(outer, other))

        when(exists(other), further)

    def send_inputs(chunk, carry):
        for which in range(3):
            for sign, dist in peers:
                other = me + sign * dist
                wanted = exists(other)
                if dist == 1:
                    wanted = wanted & ((other != inner) | (chunk >= early))
                when(wanted, lambda which=which, other=other: in_copy(which, chunk, other).start())
            own_copy(which, chunk).start()
        return carry

    lax.fori_loop(0, chunks, send_inputs, 0)

    @pl.when(jnp.logical_not(has_down))
    def _():
        v_buf[:, :halo, :] = jnp.zeros((chunks, halo, lanes), jnp.bfloat16)

    @pl.when(jnp.logical_not(has_up))
    def _():
        v_buf[:, halo + tok_slab :, :] = jnp.zeros((chunks, halo, lanes), jnp.bfloat16)

    lse_buf[...] = jnp.zeros(lse_buf.shape, jnp.float32)
    mask_copy.wait()
    slot_copy.wait()

    def wait_input(which, chunk):
        _, buf, base = inputs[which]
        wait_bytes(buf.at[chunk, pl.ds(base, tok_slab), :], in_recv.at[which, chunk])

    def forward(chunk):
        for which in range(2):
            wait_input(which, chunk)
            when(has_up, lambda which=which: halo_copy(which, chunk, True).start())
            when(has_down, lambda which=which: halo_copy(which, chunk, False).start())

    def attend(chunk):
        for which in range(2):
            when(has_down, lambda which=which: halo_copy(which, chunk, True).wait_recv())
            when(has_up, lambda which=which: halo_copy(which, chunk, False).wait_recv())
        wait_input(2, chunk)
        for within in range(width):
            column = slice(within * head_dim, (within + 1) * head_dim)
            local_head = chunk * width + within
            global_head = me * capacity + local_head
            for block in range(tiles_dev):
                q_rows = slice(block * tile, (block + 1) * tile)
                queries = q_buf[chunk, q_rows, column]
                window = slice(block * tile, (block + band) * tile)
                keys = k_buf[chunk, window, column]
                values = v_buf[chunk, window, column]
                scores = (
                    lax.dot_general(
                        keys, queries, (((1,), (1,)), ((), ())), preferred_element_type=jnp.float32
                    )
                    * scale
                )
                parts = []
                for place in range(band):
                    key_tile = slab * tiles_dev + block + place - reach
                    inside = ((key_tile >= 0) & (key_tile < slabs * tiles_dev)).astype(jnp.int32)
                    flag = mask_buf[place, block, global_head] * inside
                    allowed = jnp.full((tile, tile), flag, jnp.int32) > 0
                    parts.append(
                        jnp.where(allowed, scores[place * tile : (place + 1) * tile], FLOOR)
                    )
                masked = jnp.concatenate(parts, axis=0)
                highest = jnp.max(masked, axis=0, keepdims=True)
                weights = jnp.exp(masked - highest)
                total = jnp.sum(weights, axis=0, keepdims=True)
                summed = lax.dot_general(
                    values,
                    weights.astype(jnp.bfloat16),
                    (((0,), (0,)), ((), ())),
                    preferred_element_type=jnp.float32,
                )
                result = jnp.transpose(summed / total)
                o_buf[chunk, q_rows, column] = result.astype(jnp.bfloat16)
                row = local_head * tiles_dev + block
                lse_buf[pl.ds(row, 1), :] = highest + jnp.log(total)

    def send_out(chunk):
        for sign, dist in peers:
            other = me + sign * dist
            wanted = exists(other) & ((other != across) | (chunk < hold_from))
            when(wanted, lambda other=other: out_copy(chunk, other).start())
        out_own(chunk).start()

    side = jnp.where(low, 0, mid)
    mates = [(sign, dist) for dist in range(mid - 1, 0, -1) for sign in (1, -1)]

    def per_mate(body):
        for sign, dist in mates:
            other = me + sign * dist
            when((other >= side) & (other < side + mid), functools.partial(body, other))

    def send_lse():
        lse_box[me] = lse_buf[:first_rows, :].astype(jnp.bfloat16)
        lse_copy(across, True).start()
        per_mate(lambda other: lse_copy(other, False).start())

    forward(0)

    def step(chunk, carry):
        when(chunk < chunks, lambda: forward(chunk))
        attend(chunk - 1)
        when(chunk == chunks - 1, send_lse)
        send_out(chunk - 1)
        return carry

    lax.fori_loop(1, chunks + 1, step, 0)

    last_box[me] = lse_buf[first_rows:, :].astype(jnp.bfloat16)
    for sign, dist in peers:
        other = me + sign * dist
        when(exists(other), lambda other=other: last_copy(other).start())
    for chunk in range(hold_from, chunks):
        out_copy(chunk, across).start()

    half = lse_box.at[pl.ds(0, mid)]
    wait_bytes(half, lse_recv.at[1])
    when(inner == across, lambda: per_mate(lambda other: lse_relay(other).start()))
    if mid > 1:
        wait_bytes(lse_box.at[pl.ds(0, mid - 1)], lse_recv.at[0])
    wait_bytes(last_box.at[pl.ds(0, owners - 1)], lse_recv.at[2])
    slot_rows = lax.broadcasted_iota(jnp.int32, (capacity, tile), 0) + me * capacity
    slot_lse = [jnp.zeros((capacity, tile), jnp.float32) for _ in range(tiles_dev)]
    for owner in range(owners):
        mine = (me == owner).astype(jnp.int32)

        def values(own, box, owner=owner, mine=mine):
            return jnp.where(jnp.full(own.shape, mine) > 0, own, box[owner].astype(jnp.float32))

        theirs = values(lse_buf[:first_rows, :], lse_box)
        last = values(lse_buf[first_rows:, :], last_box)
        for head in range(capacity):
            here = slot_rows == slot_buf[owner * capacity + head]
            source, first = (theirs, 0) if head < capacity - width else (last, capacity - width)
            for block in range(tiles_dev):
                row = (head - first) * tiles_dev + block
                row = jnp.broadcast_to(source[row : row + 1], (capacity, tile))
                slot_lse[block] = jnp.where(here, row, slot_lse[block])
    for block in range(tiles_dev):
        slot_lse_ref[:, block * tile : (block + 1) * tile] = slot_lse[block]

    others = (owners - 1) * capacity * head_dim
    for which in range(3):
        wait_bytes(inputs[which][0].at[:, pl.ds(0, others)], in_send.at[which])
    for which in range(2):
        edge = inputs[which][1].at[:, pl.ds(0, halo), :]
        when(has_up, lambda which=which, edge=edge: wait_bytes(edge, halo_send.at[which, 1]))
        when(has_down, lambda which=which, edge=edge: wait_bytes(edge, halo_send.at[which, 0]))
    wait_bytes(half, lse_send.at[owners])
    when(inner == across, lambda: per_mate(lambda other: lse_relay(other).wait_send()))
    wait_bytes(last_box.at[pl.ds(0, owners - 1)], lse_send.at[owners + 1])
    wait_bytes(o_buf.at[:, pl.ds(0, (owners - 1) * tok_dev), :], out_send.at[0])
    wait_bytes(out_ref, out_recv.at[0])


def hand_over_kernel(out_in, lse_in, out_ref, lse_ref, sems):
    copies = [
        pltpu.make_async_copy(out_in, out_ref, sems.at[0]),
        pltpu.make_async_copy(lse_in, lse_ref, sems.at[1]),
    ]
    for copy in copies:
        copy.start()
    for copy in copies:
        copy.wait()


def on_device(query_rows, key_rows, value_rows, tile_mask, head_slot):
    owners = lax.axis_size("head")
    slabs = lax.axis_size("slab")
    tok_dev, model = query_rows.shape
    heads, tiles_dev, band = tile_mask.shape
    head_dim = model // heads
    capacity = (heads + owners - 1) // owners
    reach = (band - 1) // 2
    tok_slab = tok_dev * owners
    tile = tok_slab // tiles_dev
    halo = reach * tile
    whole = heads == owners * capacity
    width = HEADS_PER_CHUNK if whole and capacity % HEADS_PER_CHUNK == 0 else 1
    chunks = capacity // width
    line = whole and owners % 2 == 0 and chunks > 1
    lanes = width * head_dim
    dims = (heads, head_dim, capacity, width, tok_dev, tile, reach)
    dma = pltpu.SemaphoreType.DMA
    buffers = [
        pltpu.VMEM((chunks, tok_slab, lanes), jnp.bfloat16),
        pltpu.VMEM((chunks, tok_slab + 2 * halo, lanes), jnp.bfloat16),
        pltpu.VMEM((chunks, tok_slab + 2 * halo, lanes), jnp.bfloat16),
        pltpu.VMEM((chunks, tok_slab, lanes), jnp.bfloat16),
    ]
    tables = [
        pltpu.SMEM((band, tiles_dev, heads), jnp.int32),
        pltpu.SMEM((heads,), jnp.int32),
    ]
    if line:
        kernel = line_kernel
        first_rows = (capacity - width) * tiles_dev
        last_rows = -(-width * tiles_dev // 8) * 8
        scratch = [
            *buffers,
            pltpu.VMEM((first_rows + last_rows, tile), jnp.float32),
            pltpu.VMEM((owners, first_rows, tile), jnp.bfloat16),
            pltpu.VMEM((owners, last_rows, tile), jnp.bfloat16),
            *tables,
            dma((3,)),
            dma((3, chunks)),
            dma((2, 2)),
            dma((2, chunks, 2)),
            dma((1,)),
            dma((1,)),
            dma((owners + 2,)),
            dma((3,)),
            pltpu.SemaphoreType.REGULAR((owners,)),
            dma((2,)),
        ]
    else:
        kernel = attention_kernel
        scratch = [
            *buffers,
            pltpu.VMEM((owners, capacity, 1, tok_slab), jnp.float32),
            *tables,
            dma((3, chunks, owners)),
            dma((3, chunks, owners)),
            dma((2, chunks, 2)),
            dma((2, chunks, 2)),
            dma((chunks, owners)),
            dma((chunks, owners)),
            dma((owners,)),
            dma((owners,)),
            dma((2,)),
        ]
    gathered, gathered_lse = pl.pallas_call(
        functools.partial(kernel, owners, slabs, dims),
        out_shape=(
            jax.ShapeDtypeStruct((tok_dev, model), jnp.bfloat16),
            jax.ShapeDtypeStruct((capacity, tok_slab), jnp.float32),
        ),
        in_specs=[pl.BlockSpec(memory_space=pltpu.HBM)] * 5,
        out_specs=(pl.BlockSpec(memory_space=pltpu.VMEM), pl.BlockSpec(memory_space=pltpu.VMEM)),
        scratch_shapes=scratch,
        compiler_params=pltpu.CompilerParams(collective_id=0, has_side_effects=True, vmem_limit_bytes=16 << 20),
    )(*[pltpu.with_memory_space_constraint(x, pltpu.HBM) for x in (query_rows, key_rows, value_rows, jnp.transpose(tile_mask, (2, 1, 0)), head_slot)])
    vmem = pl.BlockSpec(memory_space=pltpu.VMEM)
    hbm = pl.BlockSpec(memory_space=pltpu.HBM)
    return pl.pallas_call(
        hand_over_kernel,
        out_shape=(
            jax.ShapeDtypeStruct(gathered.shape, gathered.dtype),
            jax.ShapeDtypeStruct(gathered_lse.shape, gathered_lse.dtype),
        ),
        in_specs=[vmem, vmem],
        out_specs=(hbm, hbm),
        scratch_shapes=[dma((2,))],
        compiler_params=pltpu.CompilerParams(vmem_limit_bytes=16 << 20),
    )(gathered, gathered_lse)


def solution(mesh):
    in_specs = (
        P(("groups", "slab", "head"), None),
        P(("groups", "slab", "head"), None),
        P(("groups", "slab", "head"), None),
        P(None, ("groups", "slab"), None),
        P(),
    )
    out_specs = (P(("groups", "slab", "head"), None), P("head", ("groups", "slab")))
    return jax.shard_map(
        on_device, mesh=mesh, in_specs=in_specs, out_specs=out_specs, check_vma=False
    )
```

```python
import functools

import jax
import jax.numpy as jnp
from jax import lax
from jax.experimental import pallas as pl
from jax.experimental.pallas import tpu as pltpu
from jax.sharding import PartitionSpec as P

MESH = pl.DeviceIdType.MESH
HEADS_PER_CHUNK = 2
EARLY_CHUNKS = 2
HELD_CHUNKS = 4
FLOOR = -1e30


def attention_kernel(
    owners,
    slabs,
    dims,
    q_ref,
    k_ref,
    v_ref,
    mask_ref,
    slot_ref,
    out_ref,
    slot_lse_ref,
    q_buf,
    k_buf,
    v_buf,
    o_buf,
    lse_buf,
    mask_buf,
    slot_buf,
    in_send,
    in_recv,
    halo_send,
    halo_recv,
    out_send,
    out_recv,
    lse_send,
    lse_recv,
    small_sem,
):
    heads, head_dim, capacity, width, tok_dev, tile, reach = dims
    chunks = capacity // width
    lanes = width * head_dim
    tok_slab = tok_dev * owners
    tiles_dev = tok_slab // tile
    band = 2 * reach + 1
    halo = reach * tile
    full = heads == owners * capacity
    scale = head_dim ** (-0.5)
    me = lax.axis_index("head")
    slab = lax.axis_index("slab")
    inputs = ((k_ref, k_buf, halo), (v_ref, v_buf, halo), (q_ref, q_buf, 0))
    peers = [(sign, dist) for dist in range(owners - 1, 0, -1) for sign in (1, -1)]

    def when(condition, body):
        pl.when(condition)(body)

    def per_peer(body):
        for sign, dist in peers:
            other = me + sign * dist
            when((other >= 0) & (other < owners), functools.partial(body, other))

    def if_held(owner, chunk, body):
        if full:
            body()
        else:
            when(owner * capacity + chunk * width < heads, body)

    def columns(owner, chunk):
        first = (owner * capacity + chunk * width) * head_dim
        return pl.ds(pl.multiple_of(first, head_dim), lanes)

    def rows(owner, base):
        return pl.ds(pl.multiple_of(owner * tok_dev + base, tok_dev), tok_dev)

    def in_copy(which, chunk, src_owner, dst_owner):
        ref, buf, base = inputs[which]
        return pltpu.make_async_remote_copy(
            src_ref=ref.at[:, columns(dst_owner, chunk)],
            dst_ref=buf.at[chunk, rows(src_owner, base), :],
            send_sem=in_send.at[which, chunk, dst_owner],
            recv_sem=in_recv.at[which, chunk, src_owner],
            device_id={"head": dst_owner},
            device_id_type=MESH,
        )

    def own_copy(which, chunk):
        ref, buf, base = inputs[which]
        return pltpu.make_async_copy(
            ref.at[:, columns(me, chunk)],
            buf.at[chunk, rows(me, base), :],
            in_recv.at[which, chunk, me],
        )

    def halo_copy(which, chunk, up):
        buf = inputs[which][1]
        source = tok_slab if up else halo
        target = 0 if up else halo + tok_slab
        return pltpu.make_async_remote_copy(
            src_ref=buf.at[chunk, pl.ds(source, halo), :],
            dst_ref=buf.at[chunk, pl.ds(target, halo), :],
            send_sem=halo_send.at[which, chunk, int(up)],
            recv_sem=halo_recv.at[which, chunk, int(up)],
            device_id={"slab": slab + 1 if up else slab - 1},
            device_id_type=MESH,
        )

    def out_copy(chunk, src_owner, dst_owner):
        return pltpu.make_async_remote_copy(
            src_ref=o_buf.at[chunk, rows(dst_owner, 0), :],
            dst_ref=out_ref.at[:, columns(src_owner, chunk)],
            send_sem=out_send.at[chunk, dst_owner],
            recv_sem=out_recv.at[chunk, src_owner],
            device_id={"head": dst_owner},
            device_id_type=MESH,
        )

    def out_own(chunk):
        return pltpu.make_async_copy(
            o_buf.at[chunk, rows(me, 0), :],
            out_ref.at[:, columns(me, chunk)],
            out_recv.at[chunk, me],
        )

    def lse_copy(src_owner, dst_owner):
        return pltpu.make_async_remote_copy(
            src_ref=lse_buf.at[src_owner],
            dst_ref=lse_buf.at[src_owner],
            send_sem=lse_send.at[dst_owner],
            recv_sem=lse_recv.at[src_owner],
            device_id={"head": dst_owner},
            device_id_type=MESH,
        )

    has_up = slab < slabs - 1
    has_down = slab > 0
    barrier = pltpu.get_barrier_semaphore()

    def greet(other):
        pl.semaphore_signal(barrier, inc=1, device_id={"head": other}, device_id_type=MESH)

    per_peer(greet)

    @pl.when(has_up)
    def _():
        pl.semaphore_signal(barrier, inc=1, device_id={"slab": slab + 1}, device_id_type=MESH)

    @pl.when(has_down)
    def _():
        pl.semaphore_signal(barrier, inc=1, device_id={"slab": slab - 1}, device_id_type=MESH)

    mask_copy = pltpu.make_async_copy(mask_ref, mask_buf, small_sem.at[0])
    slot_copy = pltpu.make_async_copy(slot_ref, slot_buf, small_sem.at[1])
    mask_copy.start()
    slot_copy.start()
    pl.semaphore_wait(
        barrier, owners - 1 + has_up.astype(jnp.int32) + has_down.astype(jnp.int32)
    )

    low_half = me < owners // 2

    def send_inputs(crossing, chunk, carry):
        for which in range(3):

            def to_peer(other, which=which):
                def go():
                    if_held(other, chunk, lambda: in_copy(which, chunk, me, other).start())

                other_side = low_half != (other < owners // 2)
                when(other_side if crossing else jnp.logical_not(other_side), go)

            per_peer(to_peer)
            if crossing:
                if_held(me, chunk, lambda which=which: own_copy(which, chunk).start())
        return carry

    lax.fori_loop(0, chunks, functools.partial(send_inputs, False), 0)
    lax.fori_loop(0, chunks, functools.partial(send_inputs, True), 0)

    if not full:
        lse_buf[me] = jnp.zeros(lse_buf.shape[1:], jnp.float32)

    @pl.when(jnp.logical_not(has_down))
    def _():
        v_buf[:, :halo, :] = jnp.zeros((chunks, halo, lanes), jnp.bfloat16)

    @pl.when(jnp.logical_not(has_up))
    def _():
        v_buf[:, halo + tok_slab :, :] = jnp.zeros((chunks, halo, lanes), jnp.bfloat16)

    mask_copy.wait()
    slot_copy.wait()

    def wait_input(which, chunk):
        per_peer(lambda other: in_copy(which, chunk, other, me).wait_recv())
        own_copy(which, chunk).wait()

    def forward(chunk):
        for which in range(2):
            wait_input(which, chunk)
            when(has_up, lambda: halo_copy(which, chunk, True).start())
            when(has_down, lambda: halo_copy(which, chunk, False).start())

    def attend(chunk):
        for which in range(2):
            when(has_down, lambda: halo_copy(which, chunk, True).wait_recv())
            when(has_up, lambda: halo_copy(which, chunk, False).wait_recv())
        wait_input(2, chunk)
        for within in range(width):
            column = slice(within * head_dim, (within + 1) * head_dim)
            local_head = chunk * width + within
            global_head = me * capacity + local_head
            for block in range(tiles_dev):
                q_rows = slice(block * tile, (block + 1) * tile)
                queries = q_buf[chunk, q_rows, column]
                window = slice(block * tile, (block + band) * tile)
                keys = k_buf[chunk, window, column]
                values = v_buf[chunk, window, column]
                scores = (
                    lax.dot_general(
                        keys, queries, (((1,), (1,)), ((), ())), preferred_element_type=jnp.float32
                    )
                    * scale
                )
                parts = []
                for place in range(band):
                    key_tile = slab * tiles_dev + block + place - reach
                    inside = ((key_tile >= 0) & (key_tile < slabs * tiles_dev)).astype(jnp.int32)
                    flag = mask_buf[place, block, global_head] * inside
                    allowed = jnp.full((tile, tile), flag, jnp.int32) > 0
                    parts.append(
                        jnp.where(allowed, scores[place * tile : (place + 1) * tile], FLOOR)
                    )
                masked = jnp.concatenate(parts, axis=0)
                highest = jnp.max(masked, axis=0, keepdims=True)
                weights = jnp.exp(masked - highest)
                total = jnp.sum(weights, axis=0, keepdims=True)
                summed = lax.dot_general(
                    values,
                    weights.astype(jnp.bfloat16),
                    (((0,), (0,)), ((), ())),
                    preferred_element_type=jnp.float32,
                )
                result = jnp.transpose(summed / total)
                o_buf[chunk, q_rows, column] = result.astype(jnp.bfloat16)
                lse_buf[me, local_head, :, q_rows] = highest + jnp.log(total)

    def send_out(chunk):
        per_peer(lambda other: out_copy(chunk, me, other).start())
        out_own(chunk).start()

    if_held(me, 0, lambda: forward(0))

    def step(chunk, carry):
        if_held(me, chunk, lambda: forward(chunk))

        def finish():
            attend(chunk - 1)
            send_out(chunk - 1)

        if_held(me, chunk - 1, finish)
        return carry

    lax.fori_loop(1, chunks, step, 0)
    last = chunks - 1
    if_held(me, last, lambda: attend(last))
    per_peer(lambda other: lse_copy(me, other).start())
    if_held(me, last, lambda: send_out(last))

    per_peer(lambda other: lse_copy(other, me).wait_recv())
    slot_rows = lax.broadcasted_iota(jnp.int32, (capacity, tok_slab), 0) + me * capacity
    slot_lse = jnp.zeros((capacity, tok_slab), jnp.float32)
    for head in range(heads):
        row = jnp.broadcast_to(lse_buf[head // capacity, head % capacity], (capacity, tok_slab))
        slot_lse = jnp.where(slot_rows == slot_buf[head], row, slot_lse)
    slot_lse_ref[...] = slot_lse

    def drain(chunk, carry):
        for which in range(3):

            def sent(other, which=which):
                if_held(other, chunk, lambda: in_copy(which, chunk, me, other).wait_send())

            per_peer(sent)

        def mine():
            for which in range(2):
                when(has_up, lambda: halo_copy(which, chunk, True).wait_send())
                when(has_down, lambda: halo_copy(which, chunk, False).wait_send())
            per_peer(lambda other: out_copy(chunk, me, other).wait_send())
            out_own(chunk).wait()

        if_held(me, chunk, mine)

        def arrived(other):
            if_held(other, chunk, lambda: out_copy(chunk, other, me).wait_recv())

        per_peer(arrived)
        return carry

    lax.fori_loop(0, chunks, drain, 0)
    per_peer(lambda other: lse_copy(me, other).wait_send())


def line_kernel(
    owners,
    slabs,
    dims,
    q_ref,
    k_ref,
    v_ref,
    mask_ref,
    slot_ref,
    out_ref,
    slot_lse_ref,
    q_buf,
    k_buf,
    v_buf,
    o_buf,
    lse_buf,
    lse_box,
    last_box,
    mask_buf,
    slot_buf,
    in_send,
    in_recv,
    halo_send,
    halo_recv,
    out_send,
    out_recv,
    lse_send,
    lse_recv,
    seen,
    beside,
    small_sem,
):
    heads, head_dim, capacity, width, tok_dev, tile, reach = dims
    chunks = capacity // width
    lanes = width * head_dim
    tok_slab = tok_dev * owners
    tiles_dev = tok_slab // tile
    band = 2 * reach + 1
    halo = reach * tile
    mid = owners // 2
    early = min(EARLY_CHUNKS, chunks)
    hold_from = max(chunks - HELD_CHUNKS, 0)
    first_rows = (capacity - width) * tiles_dev
    scale = head_dim ** (-0.5)
    me = lax.axis_index("head")
    slab = lax.axis_index("slab")
    low = me < mid
    inward = jnp.where(low, 1, -1)
    inner = me + inward
    outer = me - inward
    across = jnp.where(low, mid, mid - 1)
    has_up = slab < slabs - 1
    has_down = slab > 0
    inputs = ((k_ref, k_buf, halo), (v_ref, v_buf, halo), (q_ref, q_buf, 0))
    peers = [(sign, dist) for dist in range(owners - 1, 0, -1) for sign in (1, -1)]

    def when(condition, body):
        pl.when(condition)(body)

    def exists(other):
        return (other >= 0) & (other < owners)

    def columns(owner, chunk):
        first = (owner * capacity + chunk * width) * head_dim
        return pl.ds(pl.multiple_of(first, head_dim), lanes)

    def rows(owner, base):
        return pl.ds(pl.multiple_of(owner * tok_dev + base, tok_dev), tok_dev)

    def wait_bytes(ref, sem):
        pltpu.make_async_copy(ref, ref, sem).wait()

    def in_copy(which, chunk, dst_owner):
        ref, buf, base = inputs[which]
        return pltpu.make_async_remote_copy(
            src_ref=ref.at[:, columns(dst_owner, chunk)],
            dst_ref=buf.at[chunk, rows(me, base), :],
            send_sem=in_send.at[which],
            recv_sem=in_recv.at[which, chunk],
            device_id={"head": dst_owner},
            device_id_type=MESH,
        )

    def own_copy(which, chunk):
        ref, buf, base = inputs[which]
        return pltpu.make_async_copy(
            ref.at[:, columns(me, chunk)],
            buf.at[chunk, rows(me, base), :],
            in_recv.at[which, chunk],
        )

    def halo_copy(which, chunk, up):
        buf = inputs[which][1]
        source = tok_slab if up else halo
        target = 0 if up else halo + tok_slab
        return pltpu.make_async_remote_copy(
            src_ref=buf.at[chunk, pl.ds(source, halo), :],
            dst_ref=buf.at[chunk, pl.ds(target, halo), :],
            send_sem=halo_send.at[which, int(up)],
            recv_sem=halo_recv.at[which, chunk, int(up)],
            device_id={"slab": slab + 1 if up else slab - 1},
            device_id_type=MESH,
        )

    def out_copy(chunk, dst_owner):
        return pltpu.make_async_remote_copy(
            src_ref=o_buf.at[chunk, rows(dst_owner, 0), :],
            dst_ref=out_ref.at[:, columns(me, chunk)],
            send_sem=out_send.at[0],
            recv_sem=out_recv.at[0],
            device_id={"head": dst_owner},
            device_id_type=MESH,
        )

    def out_own(chunk):
        return pltpu.make_async_copy(
            o_buf.at[chunk, rows(me, 0), :],
            out_ref.at[:, columns(me, chunk)],
            out_recv.at[0],
        )

    def lse_copy(dst_owner, crossing):
        return pltpu.make_async_remote_copy(
            src_ref=lse_box.at[me],
            dst_ref=lse_box.at[me],
            send_sem=lse_send.at[owners],
            recv_sem=lse_recv.at[int(crossing)],
            device_id={"head": dst_owner},
            device_id_type=MESH,
        )

    def lse_relay(dst_owner):
        boxes = lse_box.at[pl.ds(jnp.where(low, mid, 0), mid)]
        return pltpu.make_async_remote_copy(
            src_ref=boxes,
            dst_ref=boxes,
            send_sem=lse_send.at[dst_owner],
            recv_sem=lse_recv.at[1],
            device_id={"head": dst_owner},
            device_id_type=MESH,
        )

    def last_copy(dst_owner):
        return pltpu.make_async_remote_copy(
            src_ref=last_box.at[me],
            dst_ref=last_box.at[me],
            send_sem=lse_send.at[owners + 1],
            recv_sem=lse_recv.at[2],
            device_id={"head": dst_owner},
            device_id_type=MESH,
        )

    barrier = pltpu.get_barrier_semaphore()

    def greet(device):
        pl.semaphore_signal(barrier, inc=1, device_id=device, device_id_type=MESH)

    when(inner == across, lambda: greet({"head": inner}))
    when(exists(outer), lambda: greet({"head": outer}))
    at_end = jnp.logical_not(exists(outer))
    end_up = at_end & has_up
    end_down = at_end & has_down
    when(end_up, lambda: greet({"slab": slab + 1}))
    when(end_down, lambda: greet({"slab": slab - 1}))

    mask_copy = pltpu.make_async_copy(mask_ref, mask_buf, small_sem.at[0])
    slot_copy = pltpu.make_async_copy(slot_ref, slot_buf, small_sem.at[1])
    mask_copy.start()
    slot_copy.start()
    pl.semaphore_wait(barrier, 1 + end_up.astype(jnp.int32) + end_down.astype(jnp.int32))

    for chunk in range(early):
        for which in range(3):
            in_copy(which, chunk, inner).start()

    def tell(owner, about):
        pl.semaphore_signal(seen.at[about], inc=1, device_id={"head": owner}, device_id_type=MESH)

    when(inner != across, lambda: tell(inner, me))
    for dist in range(1, mid):
        other = me - inward * dist

        def outward(other=other, dist=dist):
            pl.semaphore_wait(seen.at[other], 1)
            tell(inner, other)
            if dist == 1:
                tell(outer, inner)

        when(exists(other), outward)
    for dist in range(2, owners):
        other = me + inward * dist

        def further(other=other):
            pl.semaphore_wait(seen.at[other], 1)
            when(exists(outer), lambda: tell(outer, other))

        when(exists(other), further)

    def tell_beside(which, device):
        pl.semaphore_signal(beside.at[which], inc=1, device_id=device, device_id_type=MESH)

    when(end_up, lambda: tell_beside(0, {"slab": slab + 1}))
    when(end_down, lambda: tell_beside(1, {"slab": slab - 1}))

    def send_inputs(chunk, carry):
        for which in range(3):
            for sign, dist in peers:
                other = me + sign * dist
                wanted = exists(other)
                if dist == 1:
                    wanted = wanted & ((other != inner) | (chunk >= early))
                when(wanted, lambda which=which, other=other: in_copy(which, chunk, other).start())
            own_copy(which, chunk).start()
        return carry

    lax.fori_loop(0, chunks, send_inputs, 0)

    @pl.when(jnp.logical_not(has_down))
    def _():
        v_buf[:, :halo, :] = jnp.zeros((chunks, halo, lanes), jnp.bfloat16)

    @pl.when(jnp.logical_not(has_up))
    def _():
        v_buf[:, halo + tok_slab :, :] = jnp.zeros((chunks, halo, lanes), jnp.bfloat16)

    lse_buf[...] = jnp.zeros(lse_buf.shape, jnp.float32)
    for which, there in ((0, has_down), (1, has_up)):

        def hear(which=which):
            pl.semaphore_wait(beside.at[which], 1)
            when(inner != across, lambda: tell_beside(which, {"head": inner}))

        when(there, hear)

    mask_copy.wait()
    slot_copy.wait()

    def wait_input(which, chunk):
        _, buf, base = inputs[which]
        wait_bytes(buf.at[chunk, pl.ds(base, tok_slab), :], in_recv.at[which, chunk])

    def forward(chunk):
        for which in range(2):
            wait_input(which, chunk)
            when(has_up, lambda which=which: halo_copy(which, chunk, True).start())
            when(has_down, lambda which=which: halo_copy(which, chunk, False).start())

    def attend(chunk):
        for which in range(2):
            when(has_down, lambda which=which: halo_copy(which, chunk, True).wait_recv())
            when(has_up, lambda which=which: halo_copy(which, chunk, False).wait_recv())
        wait_input(2, chunk)
        for within in range(width):
            column = slice(within * head_dim, (within + 1) * head_dim)
            local_head = chunk * width + within
            global_head = me * capacity + local_head
            for block in range(tiles_dev):
                q_rows = slice(block * tile, (block + 1) * tile)
                queries = q_buf[chunk, q_rows, column]
                window = slice(block * tile, (block + band) * tile)
                keys = k_buf[chunk, window, column]
                values = v_buf[chunk, window, column]
                scores = (
                    lax.dot_general(
                        keys, queries, (((1,), (1,)), ((), ())), preferred_element_type=jnp.float32
                    )
                    * scale
                )
                parts = []
                for place in range(band):
                    key_tile = slab * tiles_dev + block + place - reach
                    inside = ((key_tile >= 0) & (key_tile < slabs * tiles_dev)).astype(jnp.int32)
                    flag = mask_buf[place, block, global_head] * inside
                    allowed = jnp.full((tile, tile), flag, jnp.int32) > 0
                    parts.append(
                        jnp.where(allowed, scores[place * tile : (place + 1) * tile], FLOOR)
                    )
                masked = jnp.concatenate(parts, axis=0)
                highest = jnp.max(masked, axis=0, keepdims=True)
                weights = jnp.exp(masked - highest)
                total = jnp.sum(weights, axis=0, keepdims=True)
                summed = lax.dot_general(
                    values,
                    weights.astype(jnp.bfloat16),
                    (((0,), (0,)), ((), ())),
                    preferred_element_type=jnp.float32,
                )
                result = jnp.transpose(summed / total)
                o_buf[chunk, q_rows, column] = result.astype(jnp.bfloat16)
                row = local_head * tiles_dev + block
                lse_buf[pl.ds(row, 1), :] = highest + jnp.log(total)

    def send_out(chunk):
        for sign, dist in peers:
            other = me + sign * dist
            wanted = exists(other) & ((other != across) | (chunk < hold_from))
            when(wanted, lambda other=other: out_copy(chunk, other).start())
        out_own(chunk).start()

    side = jnp.where(low, 0, mid)
    mates = [(sign, dist) for dist in range(mid - 1, 0, -1) for sign in (1, -1)]

    def per_mate(body):
        for sign, dist in mates:
            other = me + sign * dist
            when((other >= side) & (other < side + mid), functools.partial(body, other))

    def send_lse():
        lse_box[me] = lse_buf[:first_rows, :].astype(jnp.bfloat16)
        lse_copy(across, True).start()
        per_mate(lambda other: lse_copy(other, False).start())

    forward(0)

    def step(chunk, carry):
        when(chunk < chunks, lambda: forward(chunk))
        attend(chunk - 1)
        when(chunk == chunks - 1, send_lse)
        send_out(chunk - 1)
        return carry

    lax.fori_loop(1, chunks + 1, step, 0)

    last_box[me] = lse_buf[first_rows:, :].astype(jnp.bfloat16)
    for sign, dist in peers:
        other = me + sign * dist
        when(exists(other), lambda other=other: last_copy(other).start())
    for chunk in range(hold_from, chunks):
        out_copy(chunk, across).start()

    half = lse_box.at[pl.ds(0, mid)]
    wait_bytes(half, lse_recv.at[1])
    when(inner == across, lambda: per_mate(lambda other: lse_relay(other).start()))
    if mid > 1:
        wait_bytes(lse_box.at[pl.ds(0, mid - 1)], lse_recv.at[0])
    wait_bytes(last_box.at[pl.ds(0, owners - 1)], lse_recv.at[2])
    slot_rows = lax.broadcasted_iota(jnp.int32, (capacity, tile), 0) + me * capacity
    slot_lse = [jnp.zeros((capacity, tile), jnp.float32) for _ in range(tiles_dev)]
    for owner in range(owners):
        mine = (me == owner).astype(jnp.int32)

        def values(own, box, owner=owner, mine=mine):
            return jnp.where(jnp.full(own.shape, mine) > 0, own, box[owner].astype(jnp.float32))

        theirs = values(lse_buf[:first_rows, :], lse_box)
        last = values(lse_buf[first_rows:, :], last_box)
        for head in range(capacity):
            here = slot_rows == slot_buf[owner * capacity + head]
            source, first = (theirs, 0) if head < capacity - width else (last, capacity - width)
            for block in range(tiles_dev):
                row = (head - first) * tiles_dev + block
                row = jnp.broadcast_to(source[row : row + 1], (capacity, tile))
                slot_lse[block] = jnp.where(here, row, slot_lse[block])
    for block in range(tiles_dev):
        slot_lse_ref[:, block * tile : (block + 1) * tile] = slot_lse[block]

    others = (owners - 1) * capacity * head_dim
    for which in range(3):
        wait_bytes(inputs[which][0].at[:, pl.ds(0, others)], in_send.at[which])
    for which in range(2):
        edge = inputs[which][1].at[:, pl.ds(0, halo), :]
        when(has_up, lambda which=which, edge=edge: wait_bytes(edge, halo_send.at[which, 1]))
        when(has_down, lambda which=which, edge=edge: wait_bytes(edge, halo_send.at[which, 0]))
    wait_bytes(half, lse_send.at[owners])
    when(inner == across, lambda: per_mate(lambda other: lse_relay(other).wait_send()))
    wait_bytes(last_box.at[pl.ds(0, owners - 1)], lse_send.at[owners + 1])
    wait_bytes(o_buf.at[:, pl.ds(0, (owners - 1) * tok_dev), :], out_send.at[0])
    wait_bytes(out_ref, out_recv.at[0])


def hand_over_kernel(out_in, lse_in, out_ref, lse_ref, sems):
    copies = [
        pltpu.make_async_copy(out_in, out_ref, sems.at[0]),
        pltpu.make_async_copy(lse_in, lse_ref, sems.at[1]),
    ]
    for copy in copies:
        copy.start()
    for copy in copies:
        copy.wait()


def on_device(query_rows, key_rows, value_rows, tile_mask, head_slot):
    owners = lax.axis_size("head")
    slabs = lax.axis_size("slab")
    tok_dev, model = query_rows.shape
    heads, tiles_dev, band = tile_mask.shape
    head_dim = model // heads
    capacity = (heads + owners - 1) // owners
    reach = (band - 1) // 2
    tok_slab = tok_dev * owners
    tile = tok_slab // tiles_dev
    halo = reach * tile
    whole = heads == owners * capacity
    width = HEADS_PER_CHUNK if whole and capacity % HEADS_PER_CHUNK == 0 else 1
    chunks = capacity // width
    line = whole and owners % 2 == 0 and chunks > 1
    lanes = width * head_dim
    dims = (heads, head_dim, capacity, width, tok_dev, tile, reach)
    dma = pltpu.SemaphoreType.DMA
    buffers = [
        pltpu.VMEM((chunks, tok_slab, lanes), jnp.bfloat16),
        pltpu.VMEM((chunks, tok_slab + 2 * halo, lanes), jnp.bfloat16),
        pltpu.VMEM((chunks, tok_slab + 2 * halo, lanes), jnp.bfloat16),
        pltpu.VMEM((chunks, tok_slab, lanes), jnp.bfloat16),
    ]
    tables = [
        pltpu.SMEM((band, tiles_dev, heads), jnp.int32),
        pltpu.SMEM((heads,), jnp.int32),
    ]
    if line:
        kernel = line_kernel
        first_rows = (capacity - width) * tiles_dev
        last_rows = -(-width * tiles_dev // 8) * 8
        scratch = [
            *buffers,
            pltpu.VMEM((first_rows + last_rows, tile), jnp.float32),
            pltpu.VMEM((owners, first_rows, tile), jnp.bfloat16),
            pltpu.VMEM((owners, last_rows, tile), jnp.bfloat16),
            *tables,
            dma((3,)),
            dma((3, chunks)),
            dma((2, 2)),
            dma((2, chunks, 2)),
            dma((1,)),
            dma((1,)),
            dma((owners + 2,)),
            dma((3,)),
            pltpu.SemaphoreType.REGULAR((owners,)),
            pltpu.SemaphoreType.REGULAR((2,)),
            dma((2,)),
        ]
    else:
        kernel = attention_kernel
        scratch = [
            *buffers,
            pltpu.VMEM((owners, capacity, 1, tok_slab), jnp.float32),
            *tables,
            dma((3, chunks, owners)),
            dma((3, chunks, owners)),
            dma((2, chunks, 2)),
            dma((2, chunks, 2)),
            dma((chunks, owners)),
            dma((chunks, owners)),
            dma((owners,)),
            dma((owners,)),
            dma((2,)),
        ]
    gathered, gathered_lse = pl.pallas_call(
        functools.partial(kernel, owners, slabs, dims),
        out_shape=(
            jax.ShapeDtypeStruct((tok_dev, model), jnp.bfloat16),
            jax.ShapeDtypeStruct((capacity, tok_slab), jnp.float32),
        ),
        in_specs=[pl.BlockSpec(memory_space=pltpu.HBM)] * 5,
        out_specs=(pl.BlockSpec(memory_space=pltpu.VMEM), pl.BlockSpec(memory_space=pltpu.VMEM)),
        scratch_shapes=scratch,
        compiler_params=pltpu.CompilerParams(collective_id=0, has_side_effects=True, vmem_limit_bytes=16 << 20),
    )(*[pltpu.with_memory_space_constraint(x, pltpu.HBM) for x in (query_rows, key_rows, value_rows, jnp.transpose(tile_mask, (2, 1, 0)), head_slot)])
    vmem = pl.BlockSpec(memory_space=pltpu.VMEM)
    hbm = pl.BlockSpec(memory_space=pltpu.HBM)
    return pl.pallas_call(
        hand_over_kernel,
        out_shape=(
            jax.ShapeDtypeStruct(gathered.shape, gathered.dtype),
            jax.ShapeDtypeStruct(gathered_lse.shape, gathered_lse.dtype),
        ),
        in_specs=[vmem, vmem],
        out_specs=(hbm, hbm),
        scratch_shapes=[dma((2,))],
        compiler_params=pltpu.CompilerParams(vmem_limit_bytes=16 << 20),
    )(gathered, gathered_lse)


def solution(mesh):
    in_specs = (
        P(("groups", "slab", "head"), None),
        P(("groups", "slab", "head"), None),
        P(("groups", "slab", "head"), None),
        P(None, ("groups", "slab"), None),
        P(),
    )
    out_specs = (P(("groups", "slab", "head"), None), P("head", ("groups", "slab")))
    return jax.shard_map(
        on_device, mesh=mesh, in_specs=in_specs, out_specs=out_specs, check_vma=False
    )
```

```python
import functools

import jax
import jax.numpy as jnp
from jax import lax
from jax.experimental import pallas as pl
from jax.experimental.pallas import tpu as pltpu
from jax.sharding import PartitionSpec as P

MESH = pl.DeviceIdType.MESH
HEADS_PER_CHUNK = 2
EARLY_CHUNKS = 2
QUERY_LAG = 0
HELD_CHUNKS = 3
FLOOR = -1e30


def attention_kernel(
    owners,
    slabs,
    dims,
    q_ref,
    k_ref,
    v_ref,
    mask_ref,
    slot_ref,
    out_ref,
    slot_lse_ref,
    q_buf,
    k_buf,
    v_buf,
    o_buf,
    lse_buf,
    mask_buf,
    slot_buf,
    in_send,
    in_recv,
    halo_send,
    halo_recv,
    out_send,
    out_recv,
    lse_send,
    lse_recv,
    small_sem,
):
    heads, head_dim, capacity, width, tok_dev, tile, reach = dims
    chunks = capacity // width
    lanes = width * head_dim
    tok_slab = tok_dev * owners
    tiles_dev = tok_slab // tile
    band = 2 * reach + 1
    halo = reach * tile
    full = heads == owners * capacity
    scale = head_dim ** (-0.5)
    me = lax.axis_index("head")
    slab = lax.axis_index("slab")
    inputs = ((k_ref, k_buf, halo), (v_ref, v_buf, halo), (q_ref, q_buf, 0))
    peers = [(sign, dist) for dist in range(owners - 1, 0, -1) for sign in (1, -1)]

    def when(condition, body):
        pl.when(condition)(body)

    def per_peer(body):
        for sign, dist in peers:
            other = me + sign * dist
            when((other >= 0) & (other < owners), functools.partial(body, other))

    def if_held(owner, chunk, body):
        if full:
            body()
        else:
            when(owner * capacity + chunk * width < heads, body)

    def columns(owner, chunk):
        first = (owner * capacity + chunk * width) * head_dim
        return pl.ds(pl.multiple_of(first, head_dim), lanes)

    def rows(owner, base):
        return pl.ds(pl.multiple_of(owner * tok_dev + base, tok_dev), tok_dev)

    def in_copy(which, chunk, src_owner, dst_owner):
        ref, buf, base = inputs[which]
        return pltpu.make_async_remote_copy(
            src_ref=ref.at[:, columns(dst_owner, chunk)],
            dst_ref=buf.at[chunk, rows(src_owner, base), :],
            send_sem=in_send.at[which, chunk, dst_owner],
            recv_sem=in_recv.at[which, chunk, src_owner],
            device_id={"head": dst_owner},
            device_id_type=MESH,
        )

    def own_copy(which, chunk):
        ref, buf, base = inputs[which]
        return pltpu.make_async_copy(
            ref.at[:, columns(me, chunk)],
            buf.at[chunk, rows(me, base), :],
            in_recv.at[which, chunk, me],
        )

    def halo_copy(which, chunk, up):
        buf = inputs[which][1]
        source = tok_slab if up else halo
        target = 0 if up else halo + tok_slab
        return pltpu.make_async_remote_copy(
            src_ref=buf.at[chunk, pl.ds(source, halo), :],
            dst_ref=buf.at[chunk, pl.ds(target, halo), :],
            send_sem=halo_send.at[which, chunk, int(up)],
            recv_sem=halo_recv.at[which, chunk, int(up)],
            device_id={"slab": slab + 1 if up else slab - 1},
            device_id_type=MESH,
        )

    def out_copy(chunk, src_owner, dst_owner):
        return pltpu.make_async_remote_copy(
            src_ref=o_buf.at[chunk, rows(dst_owner, 0), :],
            dst_ref=out_ref.at[:, columns(src_owner, chunk)],
            send_sem=out_send.at[chunk, dst_owner],
            recv_sem=out_recv.at[chunk, src_owner],
            device_id={"head": dst_owner},
            device_id_type=MESH,
        )

    def out_own(chunk):
        return pltpu.make_async_copy(
            o_buf.at[chunk, rows(me, 0), :],
            out_ref.at[:, columns(me, chunk)],
            out_recv.at[chunk, me],
        )

    def lse_copy(src_owner, dst_owner):
        return pltpu.make_async_remote_copy(
            src_ref=lse_buf.at[src_owner],
            dst_ref=lse_buf.at[src_owner],
            send_sem=lse_send.at[dst_owner],
            recv_sem=lse_recv.at[src_owner],
            device_id={"head": dst_owner},
            device_id_type=MESH,
        )

    has_up = slab < slabs - 1
    has_down = slab > 0
    barrier = pltpu.get_barrier_semaphore()

    def greet(other):
        pl.semaphore_signal(barrier, inc=1, device_id={"head": other}, device_id_type=MESH)

    per_peer(greet)

    @pl.when(has_up)
    def _():
        pl.semaphore_signal(barrier, inc=1, device_id={"slab": slab + 1}, device_id_type=MESH)

    @pl.when(has_down)
    def _():
        pl.semaphore_signal(barrier, inc=1, device_id={"slab": slab - 1}, device_id_type=MESH)

    mask_copy = pltpu.make_async_copy(mask_ref, mask_buf, small_sem.at[0])
    slot_copy = pltpu.make_async_copy(slot_ref, slot_buf, small_sem.at[1])
    mask_copy.start()
    slot_copy.start()
    pl.semaphore_wait(
        barrier, owners - 1 + has_up.astype(jnp.int32) + has_down.astype(jnp.int32)
    )

    low_half = me < owners // 2

    def send_inputs(crossing, chunk, carry):
        for which in range(3):

            def to_peer(other, which=which):
                def go():
                    if_held(other, chunk, lambda: in_copy(which, chunk, me, other).start())

                other_side = low_half != (other < owners // 2)
                when(other_side if crossing else jnp.logical_not(other_side), go)

            per_peer(to_peer)
            if crossing:
                if_held(me, chunk, lambda which=which: own_copy(which, chunk).start())
        return carry

    lax.fori_loop(0, chunks, functools.partial(send_inputs, False), 0)
    lax.fori_loop(0, chunks, functools.partial(send_inputs, True), 0)

    if not full:
        lse_buf[me] = jnp.zeros(lse_buf.shape[1:], jnp.float32)

    @pl.when(jnp.logical_not(has_down))
    def _():
        v_buf[:, :halo, :] = jnp.zeros((chunks, halo, lanes), jnp.bfloat16)

    @pl.when(jnp.logical_not(has_up))
    def _():
        v_buf[:, halo + tok_slab :, :] = jnp.zeros((chunks, halo, lanes), jnp.bfloat16)

    mask_copy.wait()
    slot_copy.wait()

    def wait_input(which, chunk):
        per_peer(lambda other: in_copy(which, chunk, other, me).wait_recv())
        own_copy(which, chunk).wait()

    def forward(chunk):
        for which in range(2):
            wait_input(which, chunk)
            when(has_up, lambda: halo_copy(which, chunk, True).start())
            when(has_down, lambda: halo_copy(which, chunk, False).start())

    def attend(chunk):
        for which in range(2):
            when(has_down, lambda: halo_copy(which, chunk, True).wait_recv())
            when(has_up, lambda: halo_copy(which, chunk, False).wait_recv())
        wait_input(2, chunk)
        for within in range(width):
            column = slice(within * head_dim, (within + 1) * head_dim)
            local_head = chunk * width + within
            global_head = me * capacity + local_head
            for block in range(tiles_dev):
                q_rows = slice(block * tile, (block + 1) * tile)
                queries = q_buf[chunk, q_rows, column]
                window = slice(block * tile, (block + band) * tile)
                keys = k_buf[chunk, window, column]
                values = v_buf[chunk, window, column]
                scores = (
                    lax.dot_general(
                        keys, queries, (((1,), (1,)), ((), ())), preferred_element_type=jnp.float32
                    )
                    * scale
                )
                parts = []
                for place in range(band):
                    key_tile = slab * tiles_dev + block + place - reach
                    inside = ((key_tile >= 0) & (key_tile < slabs * tiles_dev)).astype(jnp.int32)
                    flag = mask_buf[place, block, global_head] * inside
                    allowed = jnp.full((tile, tile), flag, jnp.int32) > 0
                    parts.append(
                        jnp.where(allowed, scores[place * tile : (place + 1) * tile], FLOOR)
                    )
                masked = jnp.concatenate(parts, axis=0)
                highest = jnp.max(masked, axis=0, keepdims=True)
                weights = jnp.exp(masked - highest)
                total = jnp.sum(weights, axis=0, keepdims=True)
                summed = lax.dot_general(
                    values,
                    weights.astype(jnp.bfloat16),
                    (((0,), (0,)), ((), ())),
                    preferred_element_type=jnp.float32,
                )
                result = jnp.transpose(summed / total)
                o_buf[chunk, q_rows, column] = result.astype(jnp.bfloat16)
                lse_buf[me, local_head, :, q_rows] = highest + jnp.log(total)

    def send_out(chunk):
        per_peer(lambda other: out_copy(chunk, me, other).start())
        out_own(chunk).start()

    if_held(me, 0, lambda: forward(0))

    def step(chunk, carry):
        if_held(me, chunk, lambda: forward(chunk))

        def finish():
            attend(chunk - 1)
            send_out(chunk - 1)

        if_held(me, chunk - 1, finish)
        return carry

    lax.fori_loop(1, chunks, step, 0)
    last = chunks - 1
    if_held(me, last, lambda: attend(last))
    per_peer(lambda other: lse_copy(me, other).start())
    if_held(me, last, lambda: send_out(last))

    per_peer(lambda other: lse_copy(other, me).wait_recv())
    slot_rows = lax.broadcasted_iota(jnp.int32, (capacity, tok_slab), 0) + me * capacity
    slot_lse = jnp.zeros((capacity, tok_slab), jnp.float32)
    for head in range(heads):
        row = jnp.broadcast_to(lse_buf[head // capacity, head % capacity], (capacity, tok_slab))
        slot_lse = jnp.where(slot_rows == slot_buf[head], row, slot_lse)
    slot_lse_ref[...] = slot_lse

    def drain(chunk, carry):
        for which in range(3):

            def sent(other, which=which):
                if_held(other, chunk, lambda: in_copy(which, chunk, me, other).wait_send())

            per_peer(sent)

        def mine():
            for which in range(2):
                when(has_up, lambda: halo_copy(which, chunk, True).wait_send())
                when(has_down, lambda: halo_copy(which, chunk, False).wait_send())
            per_peer(lambda other: out_copy(chunk, me, other).wait_send())
            out_own(chunk).wait()

        if_held(me, chunk, mine)

        def arrived(other):
            if_held(other, chunk, lambda: out_copy(chunk, other, me).wait_recv())

        per_peer(arrived)
        return carry

    lax.fori_loop(0, chunks, drain, 0)
    per_peer(lambda other: lse_copy(me, other).wait_send())


def line_kernel(
    owners,
    slabs,
    dims,
    q_ref,
    k_ref,
    v_ref,
    mask_ref,
    slot_ref,
    out_ref,
    slot_lse_ref,
    q_buf,
    k_buf,
    v_buf,
    o_buf,
    lse_buf,
    lse_box,
    last_box,
    mask_buf,
    slot_buf,
    in_send,
    in_recv,
    halo_send,
    halo_recv,
    out_send,
    out_recv,
    lse_send,
    lse_recv,
    seen,
    beside,
    small_sem,
):
    heads, head_dim, capacity, width, tok_dev, tile, reach = dims
    chunks = capacity // width
    lanes = width * head_dim
    tok_slab = tok_dev * owners
    tiles_dev = tok_slab // tile
    band = 2 * reach + 1
    halo = reach * tile
    mid = owners // 2
    early = min(EARLY_CHUNKS, chunks)
    hold_from = max(chunks - HELD_CHUNKS, 0)
    first_rows = (capacity - width) * tiles_dev
    scale = head_dim ** (-0.5)
    me = lax.axis_index("head")
    slab = lax.axis_index("slab")
    low = me < mid
    inward = jnp.where(low, 1, -1)
    inner = me + inward
    outer = me - inward
    across = jnp.where(low, mid, mid - 1)
    has_up = slab < slabs - 1
    has_down = slab > 0
    inputs = ((k_ref, k_buf, halo), (v_ref, v_buf, halo), (q_ref, q_buf, 0))
    peers = [(sign, dist) for dist in range(owners - 1, 0, -1) for sign in (1, -1)]

    def when(condition, body):
        pl.when(condition)(body)

    def exists(other):
        return (other >= 0) & (other < owners)

    def columns(owner, chunk):
        first = (owner * capacity + chunk * width) * head_dim
        return pl.ds(pl.multiple_of(first, head_dim), lanes)

    def rows(owner, base):
        return pl.ds(pl.multiple_of(owner * tok_dev + base, tok_dev), tok_dev)

    def wait_bytes(ref, sem):
        pltpu.make_async_copy(ref, ref, sem).wait()

    def in_copy(which, chunk, dst_owner):
        ref, buf, base = inputs[which]
        return pltpu.make_async_remote_copy(
            src_ref=ref.at[:, columns(dst_owner, chunk)],
            dst_ref=buf.at[chunk, rows(me, base), :],
            send_sem=in_send.at[which],
            recv_sem=in_recv.at[which, chunk],
            device_id={"head": dst_owner},
            device_id_type=MESH,
        )

    def own_copy(which, chunk):
        ref, buf, base = inputs[which]
        return pltpu.make_async_copy(
            ref.at[:, columns(me, chunk)],
            buf.at[chunk, rows(me, base), :],
            in_recv.at[which, chunk],
        )

    def halo_copy(which, chunk, up):
        buf = inputs[which][1]
        source = tok_slab if up else halo
        target = 0 if up else halo + tok_slab
        return pltpu.make_async_remote_copy(
            src_ref=buf.at[chunk, pl.ds(source, halo), :],
            dst_ref=buf.at[chunk, pl.ds(target, halo), :],
            send_sem=halo_send.at[which, int(up)],
            recv_sem=halo_recv.at[which, chunk, int(up)],
            device_id={"slab": slab + 1 if up else slab - 1},
            device_id_type=MESH,
        )

    def out_copy(chunk, dst_owner):
        return pltpu.make_async_remote_copy(
            src_ref=o_buf.at[chunk, rows(dst_owner, 0), :],
            dst_ref=out_ref.at[:, columns(me, chunk)],
            send_sem=out_send.at[0],
            recv_sem=out_recv.at[0],
            device_id={"head": dst_owner},
            device_id_type=MESH,
        )

    def out_own(chunk):
        return pltpu.make_async_copy(
            o_buf.at[chunk, rows(me, 0), :],
            out_ref.at[:, columns(me, chunk)],
            out_recv.at[0],
        )

    def lse_copy(dst_owner, crossing):
        return pltpu.make_async_remote_copy(
            src_ref=lse_box.at[me],
            dst_ref=lse_box.at[me],
            send_sem=lse_send.at[owners],
            recv_sem=lse_recv.at[int(crossing)],
            device_id={"head": dst_owner},
            device_id_type=MESH,
        )

    def lse_relay(dst_owner):
        boxes = lse_box.at[pl.ds(jnp.where(low, mid, 0), mid)]
        return pltpu.make_async_remote_copy(
            src_ref=boxes,
            dst_ref=boxes,
            send_sem=lse_send.at[dst_owner],
            recv_sem=lse_recv.at[1],
            device_id={"head": dst_owner},
            device_id_type=MESH,
        )

    def last_copy(dst_owner):
        return pltpu.make_async_remote_copy(
            src_ref=last_box.at[me],
            dst_ref=last_box.at[me],
            send_sem=lse_send.at[owners + 1],
            recv_sem=lse_recv.at[2],
            device_id={"head": dst_owner},
            device_id_type=MESH,
        )

    barrier = pltpu.get_barrier_semaphore()

    def greet(device):
        pl.semaphore_signal(barrier, inc=1, device_id=device, device_id_type=MESH)

    when(inner == across, lambda: greet({"head": inner}))
    when(exists(outer), lambda: greet({"head": outer}))
    at_end = jnp.logical_not(exists(outer))
    end_up = at_end & has_up
    end_down = at_end & has_down
    when(end_up, lambda: greet({"slab": slab + 1}))
    when(end_down, lambda: greet({"slab": slab - 1}))

    mask_copy = pltpu.make_async_copy(mask_ref, mask_buf, small_sem.at[0])
    slot_copy = pltpu.make_async_copy(slot_ref, slot_buf, small_sem.at[1])
    mask_copy.start()
    slot_copy.start()
    pl.semaphore_wait(barrier, 1 + end_up.astype(jnp.int32) + end_down.astype(jnp.int32))

    for chunk in range(early):
        for which in range(3):
            in_copy(which, chunk, inner).start()

    def tell(owner, about):
        pl.semaphore_signal(seen.at[about], inc=1, device_id={"head": owner}, device_id_type=MESH)

    when(inner != across, lambda: tell(inner, me))
    for dist in range(1, mid):
        other = me - inward * dist

        def outward(other=other, dist=dist):
            pl.semaphore_wait(seen.at[other], 1)
            tell(inner, other)
            if dist == 1:
                tell(outer, inner)

        when(exists(other), outward)
    for dist in range(2, owners):
        other = me + inward * dist

        def further(other=other):
            pl.semaphore_wait(seen.at[other], 1)
            when(exists(outer), lambda: tell(outer, other))

        when(exists(other), further)

    def tell_beside(which, device):
        pl.semaphore_signal(beside.at[which], inc=1, device_id=device, device_id_type=MESH)

    when(end_up, lambda: tell_beside(0, {"slab": slab + 1}))
    when(end_down, lambda: tell_beside(1, {"slab": slab - 1}))

    def send_input(which, chunk):
        for sign, dist in peers:
            other = me + sign * dist
            wanted = exists(other)
            if dist == 1:
                wanted = wanted & ((other != inner) | (chunk >= early))
            when(wanted, lambda other=other: in_copy(which, chunk, other).start())
        own_copy(which, chunk).start()

    lead = min(QUERY_LAG, chunks)

    def send_inputs(chunk, carry):
        def ahead():
            send_input(0, chunk)
            send_input(1, chunk)

        when(chunk < chunks, ahead)
        when(chunk >= lead, lambda: send_input(2, chunk - lead))
        return carry

    lax.fori_loop(0, chunks + lead, send_inputs, 0)

    @pl.when(jnp.logical_not(has_down))
    def _():
        v_buf[:, :halo, :] = jnp.zeros((chunks, halo, lanes), jnp.bfloat16)

    @pl.when(jnp.logical_not(has_up))
    def _():
        v_buf[:, halo + tok_slab :, :] = jnp.zeros((chunks, halo, lanes), jnp.bfloat16)

    lse_buf[...] = jnp.zeros(lse_buf.shape, jnp.float32)
    for which, there in ((0, has_down), (1, has_up)):

        def hear(which=which):
            pl.semaphore_wait(beside.at[which], 1)
            when(inner != across, lambda: tell_beside(which, {"head": inner}))

        when(there, hear)

    mask_copy.wait()
    slot_copy.wait()

    def wait_input(which, chunk):
        _, buf, base = inputs[which]
        wait_bytes(buf.at[chunk, pl.ds(base, tok_slab), :], in_recv.at[which, chunk])

    def forward(chunk):
        for which in range(2):
            wait_input(which, chunk)
            when(has_up, lambda which=which: halo_copy(which, chunk, True).start())
            when(has_down, lambda which=which: halo_copy(which, chunk, False).start())

    def attend(chunk):
        for which in range(2):
            when(has_down, lambda which=which: halo_copy(which, chunk, True).wait_recv())
            when(has_up, lambda which=which: halo_copy(which, chunk, False).wait_recv())
        wait_input(2, chunk)
        for within in range(width):
            column = slice(within * head_dim, (within + 1) * head_dim)
            local_head = chunk * width + within
            global_head = me * capacity + local_head
            for block in range(tiles_dev):
                q_rows = slice(block * tile, (block + 1) * tile)
                queries = q_buf[chunk, q_rows, column]
                window = slice(block * tile, (block + band) * tile)
                keys = k_buf[chunk, window, column]
                values = v_buf[chunk, window, column]
                scores = (
                    lax.dot_general(
                        keys, queries, (((1,), (1,)), ((), ())), preferred_element_type=jnp.float32
                    )
                    * scale
                )
                parts = []
                for place in range(band):
                    key_tile = slab * tiles_dev + block + place - reach
                    inside = ((key_tile >= 0) & (key_tile < slabs * tiles_dev)).astype(jnp.int32)
                    flag = mask_buf[place, block, global_head] * inside
                    allowed = jnp.full((tile, tile), flag, jnp.int32) > 0
                    parts.append(
                        jnp.where(allowed, scores[place * tile : (place + 1) * tile], FLOOR)
                    )
                masked = jnp.concatenate(parts, axis=0)
                highest = jnp.max(masked, axis=0, keepdims=True)
                weights = jnp.exp(masked - highest)
                total = jnp.sum(weights, axis=0, keepdims=True)
                summed = lax.dot_general(
                    values,
                    weights.astype(jnp.bfloat16),
                    (((0,), (0,)), ((), ())),
                    preferred_element_type=jnp.float32,
                )
                result = jnp.transpose(summed / total)
                o_buf[chunk, q_rows, column] = result.astype(jnp.bfloat16)
                row = local_head * tiles_dev + block
                lse_buf[pl.ds(row, 1), :] = highest + jnp.log(total)

    def send_out(chunk):
        for sign, dist in peers:
            other = me + sign * dist
            wanted = exists(other) & ((other != across) | (chunk < hold_from))
            when(wanted, lambda other=other: out_copy(chunk, other).start())
        out_own(chunk).start()

    side = jnp.where(low, 0, mid)
    mates = [(sign, dist) for dist in range(mid - 1, 0, -1) for sign in (1, -1)]

    def per_mate(body):
        for sign, dist in mates:
            other = me + sign * dist
            when((other >= side) & (other < side + mid), functools.partial(body, other))

    def send_lse():
        lse_box[me] = lse_buf[:first_rows, :].astype(jnp.bfloat16)
        lse_copy(across, True).start()
        per_mate(lambda other: lse_copy(other, False).start())

    forward(0)

    def step(chunk, carry):
        when(chunk < chunks, lambda: forward(chunk))
        attend(chunk - 1)
        when(chunk == chunks - 1, send_lse)
        send_out(chunk - 1)
        return carry

    lax.fori_loop(1, chunks + 1, step, 0)

    last_box[me] = lse_buf[first_rows:, :].astype(jnp.bfloat16)
    for sign, dist in peers:
        other = me + sign * dist
        when(exists(other), lambda other=other: last_copy(other).start())
    for chunk in range(hold_from, chunks):
        out_copy(chunk, across).start()

    half = lse_box.at[pl.ds(0, mid)]
    wait_bytes(half, lse_recv.at[1])
    when(inner == across, lambda: per_mate(lambda other: lse_relay(other).start()))
    if mid > 1:
        wait_bytes(lse_box.at[pl.ds(0, mid - 1)], lse_recv.at[0])
    wait_bytes(last_box.at[pl.ds(0, owners - 1)], lse_recv.at[2])
    slot_rows = lax.broadcasted_iota(jnp.int32, (capacity, tile), 0) + me * capacity
    slot_lse = [jnp.zeros((capacity, tile), jnp.float32) for _ in range(tiles_dev)]
    for owner in range(owners):
        mine = (me == owner).astype(jnp.int32)

        def values(own, box, owner=owner, mine=mine):
            return jnp.where(jnp.full(own.shape, mine) > 0, own, box[owner].astype(jnp.float32))

        theirs = values(lse_buf[:first_rows, :], lse_box)
        last = values(lse_buf[first_rows:, :], last_box)
        for head in range(capacity):
            here = slot_rows == slot_buf[owner * capacity + head]
            source, first = (theirs, 0) if head < capacity - width else (last, capacity - width)
            for block in range(tiles_dev):
                row = (head - first) * tiles_dev + block
                row = jnp.broadcast_to(source[row : row + 1], (capacity, tile))
                slot_lse[block] = jnp.where(here, row, slot_lse[block])
    for block in range(tiles_dev):
        slot_lse_ref[:, block * tile : (block + 1) * tile] = slot_lse[block]

    others = (owners - 1) * capacity * head_dim
    for which in range(3):
        wait_bytes(inputs[which][0].at[:, pl.ds(0, others)], in_send.at[which])
    for which in range(2):
        edge = inputs[which][1].at[:, pl.ds(0, halo), :]
        when(has_up, lambda which=which, edge=edge: wait_bytes(edge, halo_send.at[which, 1]))
        when(has_down, lambda which=which, edge=edge: wait_bytes(edge, halo_send.at[which, 0]))
    wait_bytes(half, lse_send.at[owners])
    when(inner == across, lambda: per_mate(lambda other: lse_relay(other).wait_send()))
    wait_bytes(last_box.at[pl.ds(0, owners - 1)], lse_send.at[owners + 1])
    wait_bytes(o_buf.at[:, pl.ds(0, (owners - 1) * tok_dev), :], out_send.at[0])
    wait_bytes(out_ref, out_recv.at[0])


def hand_over_kernel(out_in, lse_in, out_ref, lse_ref, sems):
    copies = [
        pltpu.make_async_copy(out_in, out_ref, sems.at[0]),
        pltpu.make_async_copy(lse_in, lse_ref, sems.at[1]),
    ]
    for copy in copies:
        copy.start()
    for copy in copies:
        copy.wait()


def on_device(query_rows, key_rows, value_rows, tile_mask, head_slot):
    owners = lax.axis_size("head")
    slabs = lax.axis_size("slab")
    tok_dev, model = query_rows.shape
    heads, tiles_dev, band = tile_mask.shape
    head_dim = model // heads
    capacity = (heads + owners - 1) // owners
    reach = (band - 1) // 2
    tok_slab = tok_dev * owners
    tile = tok_slab // tiles_dev
    halo = reach * tile
    whole = heads == owners * capacity
    width = HEADS_PER_CHUNK if whole and capacity % HEADS_PER_CHUNK == 0 else 1
    chunks = capacity // width
    line = whole and owners % 2 == 0 and chunks > 1
    lanes = width * head_dim
    dims = (heads, head_dim, capacity, width, tok_dev, tile, reach)
    dma = pltpu.SemaphoreType.DMA
    buffers = [
        pltpu.VMEM((chunks, tok_slab, lanes), jnp.bfloat16),
        pltpu.VMEM((chunks, tok_slab + 2 * halo, lanes), jnp.bfloat16),
        pltpu.VMEM((chunks, tok_slab + 2 * halo, lanes), jnp.bfloat16),
        pltpu.VMEM((chunks, tok_slab, lanes), jnp.bfloat16),
    ]
    tables = [
        pltpu.SMEM((band, tiles_dev, heads), jnp.int32),
        pltpu.SMEM((heads,), jnp.int32),
    ]
    if line:
        kernel = line_kernel
        first_rows = (capacity - width) * tiles_dev
        last_rows = -(-width * tiles_dev // 8) * 8
        scratch = [
            *buffers,
            pltpu.VMEM((first_rows + last_rows, tile), jnp.float32),
            pltpu.VMEM((owners, first_rows, tile), jnp.bfloat16),
            pltpu.VMEM((owners, last_rows, tile), jnp.bfloat16),
            *tables,
            dma((3,)),
            dma((3, chunks)),
            dma((2, 2)),
            dma((2, chunks, 2)),
            dma((1,)),
            dma((1,)),
            dma((owners + 2,)),
            dma((3,)),
            pltpu.SemaphoreType.REGULAR((owners,)),
            pltpu.SemaphoreType.REGULAR((2,)),
            dma((2,)),
        ]
    else:
        kernel = attention_kernel
        scratch = [
            *buffers,
            pltpu.VMEM((owners, capacity, 1, tok_slab), jnp.float32),
            *tables,
            dma((3, chunks, owners)),
            dma((3, chunks, owners)),
            dma((2, chunks, 2)),
            dma((2, chunks, 2)),
            dma((chunks, owners)),
            dma((chunks, owners)),
            dma((owners,)),
            dma((owners,)),
            dma((2,)),
        ]
    gathered, gathered_lse = pl.pallas_call(
        functools.partial(kernel, owners, slabs, dims),
        out_shape=(
            jax.ShapeDtypeStruct((tok_dev, model), jnp.bfloat16),
            jax.ShapeDtypeStruct((capacity, tok_slab), jnp.float32),
        ),
        in_specs=[pl.BlockSpec(memory_space=pltpu.HBM)] * 5,
        out_specs=(pl.BlockSpec(memory_space=pltpu.VMEM), pl.BlockSpec(memory_space=pltpu.VMEM)),
        scratch_shapes=scratch,
        compiler_params=pltpu.CompilerParams(collective_id=0, has_side_effects=True, vmem_limit_bytes=16 << 20),
    )(*[pltpu.with_memory_space_constraint(x, pltpu.HBM) for x in (query_rows, key_rows, value_rows, jnp.transpose(tile_mask, (2, 1, 0)), head_slot)])
    vmem = pl.BlockSpec(memory_space=pltpu.VMEM)
    hbm = pl.BlockSpec(memory_space=pltpu.HBM)
    return pl.pallas_call(
        hand_over_kernel,
        out_shape=(
            jax.ShapeDtypeStruct(gathered.shape, gathered.dtype),
            jax.ShapeDtypeStruct(gathered_lse.shape, gathered_lse.dtype),
        ),
        in_specs=[vmem, vmem],
        out_specs=(hbm, hbm),
        scratch_shapes=[dma((2,))],
        compiler_params=pltpu.CompilerParams(vmem_limit_bytes=16 << 20),
    )(gathered, gathered_lse)


def solution(mesh):
    in_specs = (
        P(("groups", "slab", "head"), None),
        P(("groups", "slab", "head"), None),
        P(("groups", "slab", "head"), None),
        P(None, ("groups", "slab"), None),
        P(),
    )
    out_specs = (P(("groups", "slab", "head"), None), P("head", ("groups", "slab")))
    return jax.shard_map(
        on_device, mesh=mesh, in_specs=in_specs, out_specs=out_specs, check_vma=False
    )
```

```python
import functools

import jax
import jax.numpy as jnp
from jax import lax
from jax.experimental import pallas as pl
from jax.experimental.pallas import tpu as pltpu
from jax.sharding import PartitionSpec as P

MESH = pl.DeviceIdType.MESH
HEADS_PER_CHUNK = 2
EARLY_CHUNKS = 3
QUERY_LAG = 0
HELD_CHUNKS = 3
FLOOR = -1e30


def attention_kernel(
    owners,
    slabs,
    dims,
    q_ref,
    k_ref,
    v_ref,
    mask_ref,
    slot_ref,
    out_ref,
    slot_lse_ref,
    q_buf,
    k_buf,
    v_buf,
    o_buf,
    lse_buf,
    mask_buf,
    slot_buf,
    in_send,
    in_recv,
    halo_send,
    halo_recv,
    out_send,
    out_recv,
    lse_send,
    lse_recv,
    small_sem,
):
    heads, head_dim, capacity, width, tok_dev, tile, reach = dims
    chunks = capacity // width
    lanes = width * head_dim
    tok_slab = tok_dev * owners
    tiles_dev = tok_slab // tile
    band = 2 * reach + 1
    halo = reach * tile
    full = heads == owners * capacity
    scale = head_dim ** (-0.5)
    me = lax.axis_index("head")
    slab = lax.axis_index("slab")
    inputs = ((k_ref, k_buf, halo), (v_ref, v_buf, halo), (q_ref, q_buf, 0))
    peers = [(sign, dist) for dist in range(owners - 1, 0, -1) for sign in (1, -1)]

    def when(condition, body):
        pl.when(condition)(body)

    def per_peer(body):
        for sign, dist in peers:
            other = me + sign * dist
            when((other >= 0) & (other < owners), functools.partial(body, other))

    def if_held(owner, chunk, body):
        if full:
            body()
        else:
            when(owner * capacity + chunk * width < heads, body)

    def columns(owner, chunk):
        first = (owner * capacity + chunk * width) * head_dim
        return pl.ds(pl.multiple_of(first, head_dim), lanes)

    def rows(owner, base):
        return pl.ds(pl.multiple_of(owner * tok_dev + base, tok_dev), tok_dev)

    def in_copy(which, chunk, src_owner, dst_owner):
        ref, buf, base = inputs[which]
        return pltpu.make_async_remote_copy(
            src_ref=ref.at[:, columns(dst_owner, chunk)],
            dst_ref=buf.at[chunk, rows(src_owner, base), :],
            send_sem=in_send.at[which, chunk, dst_owner],
            recv_sem=in_recv.at[which, chunk, src_owner],
            device_id={"head": dst_owner},
            device_id_type=MESH,
        )

    def own_copy(which, chunk):
        ref, buf, base = inputs[which]
        return pltpu.make_async_copy(
            ref.at[:, columns(me, chunk)],
            buf.at[chunk, rows(me, base), :],
            in_recv.at[which, chunk, me],
        )

    def halo_copy(which, chunk, up):
        buf = inputs[which][1]
        source = tok_slab if up else halo
        target = 0 if up else halo + tok_slab
        return pltpu.make_async_remote_copy(
            src_ref=buf.at[chunk, pl.ds(source, halo), :],
            dst_ref=buf.at[chunk, pl.ds(target, halo), :],
            send_sem=halo_send.at[which, chunk, int(up)],
            recv_sem=halo_recv.at[which, chunk, int(up)],
            device_id={"slab": slab + 1 if up else slab - 1},
            device_id_type=MESH,
        )

    def out_copy(chunk, src_owner, dst_owner):
        return pltpu.make_async_remote_copy(
            src_ref=o_buf.at[chunk, rows(dst_owner, 0), :],
            dst_ref=out_ref.at[:, columns(src_owner, chunk)],
            send_sem=out_send.at[chunk, dst_owner],
            recv_sem=out_recv.at[chunk, src_owner],
            device_id={"head": dst_owner},
            device_id_type=MESH,
        )

    def out_own(chunk):
        return pltpu.make_async_copy(
            o_buf.at[chunk, rows(me, 0), :],
            out_ref.at[:, columns(me, chunk)],
            out_recv.at[chunk, me],
        )

    def lse_copy(src_owner, dst_owner):
        return pltpu.make_async_remote_copy(
            src_ref=lse_buf.at[src_owner],
            dst_ref=lse_buf.at[src_owner],
            send_sem=lse_send.at[dst_owner],
            recv_sem=lse_recv.at[src_owner],
            device_id={"head": dst_owner},
            device_id_type=MESH,
        )

    has_up = slab < slabs - 1
    has_down = slab > 0
    barrier = pltpu.get_barrier_semaphore()

    def greet(other):
        pl.semaphore_signal(barrier, inc=1, device_id={"head": other}, device_id_type=MESH)

    per_peer(greet)

    @pl.when(has_up)
    def _():
        pl.semaphore_signal(barrier, inc=1, device_id={"slab": slab + 1}, device_id_type=MESH)

    @pl.when(has_down)
    def _():
        pl.semaphore_signal(barrier, inc=1, device_id={"slab": slab - 1}, device_id_type=MESH)

    mask_copy = pltpu.make_async_copy(mask_ref, mask_buf, small_sem.at[0])
    slot_copy = pltpu.make_async_copy(slot_ref, slot_buf, small_sem.at[1])
    mask_copy.start()
    slot_copy.start()
    pl.semaphore_wait(
        barrier, owners - 1 + has_up.astype(jnp.int32) + has_down.astype(jnp.int32)
    )

    low_half = me < owners // 2

    def send_inputs(crossing, chunk, carry):
        for which in range(3):

            def to_peer(other, which=which):
                def go():
                    if_held(other, chunk, lambda: in_copy(which, chunk, me, other).start())

                other_side = low_half != (other < owners // 2)
                when(other_side if crossing else jnp.logical_not(other_side), go)

            per_peer(to_peer)
            if crossing:
                if_held(me, chunk, lambda which=which: own_copy(which, chunk).start())
        return carry

    lax.fori_loop(0, chunks, functools.partial(send_inputs, False), 0)
    lax.fori_loop(0, chunks, functools.partial(send_inputs, True), 0)

    if not full:
        lse_buf[me] = jnp.zeros(lse_buf.shape[1:], jnp.float32)

    @pl.when(jnp.logical_not(has_down))
    def _():
        v_buf[:, :halo, :] = jnp.zeros((chunks, halo, lanes), jnp.bfloat16)

    @pl.when(jnp.logical_not(has_up))
    def _():
        v_buf[:, halo + tok_slab :, :] = jnp.zeros((chunks, halo, lanes), jnp.bfloat16)

    mask_copy.wait()
    slot_copy.wait()

    def wait_input(which, chunk):
        per_peer(lambda other: in_copy(which, chunk, other, me).wait_recv())
        own_copy(which, chunk).wait()

    def forward(chunk):
        for which in range(2):
            wait_input(which, chunk)
            when(has_up, lambda: halo_copy(which, chunk, True).start())
            when(has_down, lambda: halo_copy(which, chunk, False).start())

    def attend(chunk):
        for which in range(2):
            when(has_down, lambda: halo_copy(which, chunk, True).wait_recv())
            when(has_up, lambda: halo_copy(which, chunk, False).wait_recv())
        wait_input(2, chunk)
        for within in range(width):
            column = slice(within * head_dim, (within + 1) * head_dim)
            local_head = chunk * width + within
            global_head = me * capacity + local_head
            for block in range(tiles_dev):
                q_rows = slice(block * tile, (block + 1) * tile)
                queries = q_buf[chunk, q_rows, column]
                window = slice(block * tile, (block + band) * tile)
                keys = k_buf[chunk, window, column]
                values = v_buf[chunk, window, column]
                scores = (
                    lax.dot_general(
                        keys, queries, (((1,), (1,)), ((), ())), preferred_element_type=jnp.float32
                    )
                    * scale
                )
                parts = []
                for place in range(band):
                    key_tile = slab * tiles_dev + block + place - reach
                    inside = ((key_tile >= 0) & (key_tile < slabs * tiles_dev)).astype(jnp.int32)
                    flag = mask_buf[place, block, global_head] * inside
                    allowed = jnp.full((tile, tile), flag, jnp.int32) > 0
                    parts.append(
                        jnp.where(allowed, scores[place * tile : (place + 1) * tile], FLOOR)
                    )
                masked = jnp.concatenate(parts, axis=0)
                highest = jnp.max(masked, axis=0, keepdims=True)
                weights = jnp.exp(masked - highest)
                total = jnp.sum(weights, axis=0, keepdims=True)
                summed = lax.dot_general(
                    values,
                    weights.astype(jnp.bfloat16),
                    (((0,), (0,)), ((), ())),
                    preferred_element_type=jnp.float32,
                )
                result = jnp.transpose(summed / total)
                o_buf[chunk, q_rows, column] = result.astype(jnp.bfloat16)
                lse_buf[me, local_head, :, q_rows] = highest + jnp.log(total)

    def send_out(chunk):
        per_peer(lambda other: out_copy(chunk, me, other).start())
        out_own(chunk).start()

    if_held(me, 0, lambda: forward(0))

    def step(chunk, carry):
        if_held(me, chunk, lambda: forward(chunk))

        def finish():
            attend(chunk - 1)
            send_out(chunk - 1)

        if_held(me, chunk - 1, finish)
        return carry

    lax.fori_loop(1, chunks, step, 0)
    last = chunks - 1
    if_held(me, last, lambda: attend(last))
    per_peer(lambda other: lse_copy(me, other).start())
    if_held(me, last, lambda: send_out(last))

    per_peer(lambda other: lse_copy(other, me).wait_recv())
    slot_rows = lax.broadcasted_iota(jnp.int32, (capacity, tok_slab), 0) + me * capacity
    slot_lse = jnp.zeros((capacity, tok_slab), jnp.float32)
    for head in range(heads):
        row = jnp.broadcast_to(lse_buf[head // capacity, head % capacity], (capacity, tok_slab))
        slot_lse = jnp.where(slot_rows == slot_buf[head], row, slot_lse)
    slot_lse_ref[...] = slot_lse

    def drain(chunk, carry):
        for which in range(3):

            def sent(other, which=which):
                if_held(other, chunk, lambda: in_copy(which, chunk, me, other).wait_send())

            per_peer(sent)

        def mine():
            for which in range(2):
                when(has_up, lambda: halo_copy(which, chunk, True).wait_send())
                when(has_down, lambda: halo_copy(which, chunk, False).wait_send())
            per_peer(lambda other: out_copy(chunk, me, other).wait_send())
            out_own(chunk).wait()

        if_held(me, chunk, mine)

        def arrived(other):
            if_held(other, chunk, lambda: out_copy(chunk, other, me).wait_recv())

        per_peer(arrived)
        return carry

    lax.fori_loop(0, chunks, drain, 0)
    per_peer(lambda other: lse_copy(me, other).wait_send())


def line_kernel(
    owners,
    slabs,
    dims,
    q_ref,
    k_ref,
    v_ref,
    mask_ref,
    slot_ref,
    out_ref,
    slot_lse_ref,
    q_buf,
    kv_buf,
    o_buf,
    lse_buf,
    lse_box,
    last_box,
    mask_buf,
    slot_buf,
    in_send,
    in_recv,
    halo_send,
    halo_recv,
    out_send,
    out_recv,
    lse_send,
    lse_recv,
    seen,
    beside,
    small_sem,
):
    heads, head_dim, capacity, width, tok_dev, tile, reach = dims
    chunks = capacity // width
    lanes = width * head_dim
    tok_slab = tok_dev * owners
    tiles_dev = tok_slab // tile
    band = 2 * reach + 1
    halo = reach * tile
    mid = owners // 2
    early = min(EARLY_CHUNKS, chunks)
    hold_from = max(chunks - HELD_CHUNKS, 0)
    first_rows = (capacity - width) * tiles_dev
    scale = head_dim ** (-0.5)
    me = lax.axis_index("head")
    slab = lax.axis_index("slab")
    low = me < mid
    inward = jnp.where(low, 1, -1)
    inner = me + inward
    outer = me - inward
    across = jnp.where(low, mid, mid - 1)
    has_up = slab < slabs - 1
    has_down = slab > 0
    inputs = ((k_ref, kv_buf.at[0], halo), (v_ref, kv_buf.at[1], halo), (q_ref, q_buf, 0))
    peers = [(sign, dist) for dist in range(owners - 1, 0, -1) for sign in (1, -1)]

    def when(condition, body):
        pl.when(condition)(body)

    def exists(other):
        return (other >= 0) & (other < owners)

    def columns(owner, chunk):
        first = (owner * capacity + chunk * width) * head_dim
        return pl.ds(pl.multiple_of(first, head_dim), lanes)

    def rows(owner, base):
        return pl.ds(pl.multiple_of(owner * tok_dev + base, tok_dev), tok_dev)

    def wait_bytes(ref, sem):
        pltpu.make_async_copy(ref, ref, sem).wait()

    def in_copy(which, chunk, dst_owner):
        ref, buf, base = inputs[which]
        return pltpu.make_async_remote_copy(
            src_ref=ref.at[:, columns(dst_owner, chunk)],
            dst_ref=buf.at[chunk, rows(me, base), :],
            send_sem=in_send.at[0],
            recv_sem=in_recv.at[which, chunk],
            device_id={"head": dst_owner},
            device_id_type=MESH,
        )

    def own_copy(which, chunk):
        ref, buf, base = inputs[which]
        return pltpu.make_async_copy(
            ref.at[:, columns(me, chunk)],
            buf.at[chunk, rows(me, base), :],
            in_recv.at[which, chunk],
        )

    def halo_copy(which, chunk, up):
        source = tok_slab if up else halo
        target = 0 if up else halo + tok_slab
        return pltpu.make_async_remote_copy(
            src_ref=kv_buf.at[which, chunk, pl.ds(source, halo), :],
            dst_ref=kv_buf.at[which, chunk, pl.ds(target, halo), :],
            send_sem=halo_send.at[0],
            recv_sem=halo_recv.at[chunk],
            device_id={"slab": slab + 1 if up else slab - 1},
            device_id_type=MESH,
        )

    def per_sides(body):
        both = has_up & has_down
        when(both, lambda: body(2))
        when(jnp.logical_not(both) & (has_up | has_down), lambda: body(1))

    def out_copy(chunk, dst_owner):
        return pltpu.make_async_remote_copy(
            src_ref=o_buf.at[chunk, rows(dst_owner, 0), :],
            dst_ref=out_ref.at[:, columns(me, chunk)],
            send_sem=out_send.at[0],
            recv_sem=out_recv.at[0],
            device_id={"head": dst_owner},
            device_id_type=MESH,
        )

    def out_own(chunk):
        return pltpu.make_async_copy(
            o_buf.at[chunk, rows(me, 0), :],
            out_ref.at[:, columns(me, chunk)],
            out_recv.at[0],
        )

    def lse_copy(dst_owner, crossing):
        return pltpu.make_async_remote_copy(
            src_ref=lse_box.at[me],
            dst_ref=lse_box.at[me],
            send_sem=lse_send.at[0],
            recv_sem=lse_recv.at[int(crossing)],
            device_id={"head": dst_owner},
            device_id_type=MESH,
        )

    def lse_relay(dst_owner):
        boxes = lse_box.at[pl.ds(jnp.where(low, mid, 0), mid)]
        return pltpu.make_async_remote_copy(
            src_ref=boxes,
            dst_ref=boxes,
            send_sem=lse_send.at[1],
            recv_sem=lse_recv.at[1],
            device_id={"head": dst_owner},
            device_id_type=MESH,
        )

    def last_copy(dst_owner):
        return pltpu.make_async_remote_copy(
            src_ref=last_box.at[me],
            dst_ref=last_box.at[me],
            send_sem=lse_send.at[2],
            recv_sem=lse_recv.at[2],
            device_id={"head": dst_owner},
            device_id_type=MESH,
        )

    barrier = pltpu.get_barrier_semaphore()

    def greet(device):
        pl.semaphore_signal(barrier, inc=1, device_id=device, device_id_type=MESH)

    when(inner == across, lambda: greet({"head": inner}))
    when(exists(outer), lambda: greet({"head": outer}))
    at_end = jnp.logical_not(exists(outer))
    end_up = at_end & has_up
    end_down = at_end & has_down
    when(end_up, lambda: greet({"slab": slab + 1}))
    when(end_down, lambda: greet({"slab": slab - 1}))

    mask_copy = pltpu.make_async_copy(mask_ref, mask_buf, small_sem.at[0])
    slot_copy = pltpu.make_async_copy(slot_ref, slot_buf, small_sem.at[1])
    mask_copy.start()
    slot_copy.start()
    pl.semaphore_wait(barrier, 1 + end_up.astype(jnp.int32) + end_down.astype(jnp.int32))

    for chunk in range(early):
        for which in range(3):
            in_copy(which, chunk, inner).start()

    def tell(owner, about):
        pl.semaphore_signal(seen.at[about], inc=1, device_id={"head": owner}, device_id_type=MESH)

    when(inner != across, lambda: tell(inner, me))
    for dist in range(1, mid):
        other = me - inward * dist

        def outward(other=other, dist=dist):
            pl.semaphore_wait(seen.at[other], 1)
            tell(inner, other)
            if dist == 1:
                tell(outer, inner)

        when(exists(other), outward)
    for dist in range(2, owners):
        other = me + inward * dist

        def further(other=other):
            pl.semaphore_wait(seen.at[other], 1)
            when(exists(outer), lambda: tell(outer, other))

        when(exists(other), further)

    def tell_beside(device):
        pl.semaphore_signal(beside.at[0], inc=1, device_id=device, device_id_type=MESH)

    when(end_up, lambda: tell_beside({"slab": slab + 1}))
    when(end_down, lambda: tell_beside({"slab": slab - 1}))

    def send_input(which, chunk):
        for sign, dist in peers:
            other = me + sign * dist
            wanted = exists(other)
            if dist == 1:
                wanted = wanted & ((other != inner) | (chunk >= early))
            when(wanted, lambda other=other: in_copy(which, chunk, other).start())
        own_copy(which, chunk).start()

    lead = min(QUERY_LAG, chunks)

    def send_inputs(chunk, carry):
        def ahead():
            send_input(0, chunk)
            send_input(1, chunk)

        when(chunk < chunks, ahead)
        when(chunk >= lead, lambda: send_input(2, chunk - lead))
        return carry

    lax.fori_loop(0, chunks + lead, send_inputs, 0)

    @pl.when(jnp.logical_not(has_down))
    def _():
        kv_buf[1, :, :halo, :] = jnp.zeros((chunks, halo, lanes), jnp.bfloat16)

    @pl.when(jnp.logical_not(has_up))
    def _():
        kv_buf[1, :, halo + tok_slab :, :] = jnp.zeros((chunks, halo, lanes), jnp.bfloat16)

    lse_buf[...] = jnp.zeros(lse_buf.shape, jnp.float32)
    if slabs > 1:
        heard = jnp.where(at_end, has_up.astype(jnp.int32) + has_down.astype(jnp.int32), 1)
        pl.semaphore_wait(beside.at[0], heard)
        when(inner != across, lambda: tell_beside({"head": inner}))

    mask_copy.wait()
    slot_copy.wait()

    def forward(chunk):
        for which in range(2):
            wait_bytes(kv_buf.at[which, chunk, pl.ds(halo, tok_slab), :], in_recv.at[which, chunk])
            when(has_up, lambda which=which: halo_copy(which, chunk, True).start())
            when(has_down, lambda which=which: halo_copy(which, chunk, False).start())

    def attend(chunk):
        per_sides(lambda n: wait_bytes(kv_buf.at[:, chunk, pl.ds(0, n * halo), :], halo_recv.at[chunk]))
        wait_bytes(q_buf.at[chunk], in_recv.at[2, chunk])
        for within in range(width):
            column = slice(within * head_dim, (within + 1) * head_dim)
            local_head = chunk * width + within
            global_head = me * capacity + local_head
            for block in range(tiles_dev):
                q_rows = slice(block * tile, (block + 1) * tile)
                queries = q_buf[chunk, q_rows, column]
                window = slice(block * tile, (block + band) * tile)
                keys = kv_buf[0, chunk, window, column]
                values = kv_buf[1, chunk, window, column]
                scores = (
                    lax.dot_general(
                        keys, queries, (((1,), (1,)), ((), ())), preferred_element_type=jnp.float32
                    )
                    * scale
                )
                parts = []
                for place in range(band):
                    key_tile = slab * tiles_dev + block + place - reach
                    inside = ((key_tile >= 0) & (key_tile < slabs * tiles_dev)).astype(jnp.int32)
                    flag = mask_buf[place, block, global_head] * inside
                    allowed = jnp.full((tile, tile), flag, jnp.int32) > 0
                    parts.append(
                        jnp.where(allowed, scores[place * tile : (place + 1) * tile], FLOOR)
                    )
                masked = jnp.concatenate(parts, axis=0)
                highest = jnp.max(masked, axis=0, keepdims=True)
                weights = jnp.exp(masked - highest)
                total = jnp.sum(weights, axis=0, keepdims=True)
                summed = lax.dot_general(
                    values,
                    weights.astype(jnp.bfloat16),
                    (((0,), (0,)), ((), ())),
                    preferred_element_type=jnp.float32,
                )
                result = jnp.transpose(summed / total)
                o_buf[chunk, q_rows, column] = result.astype(jnp.bfloat16)
                row = local_head * tiles_dev + block
                lse_buf[pl.ds(row, 1), :] = highest + jnp.log(total)

    def send_out(chunk):
        for sign, dist in peers:
            other = me + sign * dist
            wanted = exists(other) & ((other != across) | (chunk < hold_from))
            when(wanted, lambda other=other: out_copy(chunk, other).start())
        out_own(chunk).start()

    side = jnp.where(low, 0, mid)
    mates = [(sign, dist) for dist in range(mid - 1, 0, -1) for sign in (1, -1)]

    def per_mate(body):
        for sign, dist in mates:
            other = me + sign * dist
            when((other >= side) & (other < side + mid), functools.partial(body, other))

    def send_lse():
        lse_box[me] = lse_buf[:first_rows, :].astype(jnp.bfloat16)
        lse_copy(across, True).start()
        per_mate(lambda other: lse_copy(other, False).start())

    forward(0)

    def step(chunk, carry):
        when(chunk < chunks, lambda: forward(chunk))
        attend(chunk - 1)
        when(chunk == chunks - 1, send_lse)
        send_out(chunk - 1)
        return carry

    lax.fori_loop(1, chunks + 1, step, 0)

    last_box[me] = lse_buf[first_rows:, :].astype(jnp.bfloat16)
    for sign, dist in peers:
        other = me + sign * dist
        when(exists(other), lambda other=other: last_copy(other).start())
    for chunk in range(hold_from, chunks):
        out_copy(chunk, across).start()

    half = lse_box.at[pl.ds(0, mid)]
    wait_bytes(half, lse_recv.at[1])
    when(inner == across, lambda: per_mate(lambda other: lse_relay(other).start()))
    if mid > 1:
        wait_bytes(lse_box.at[pl.ds(0, mid - 1)], lse_recv.at[0])
    wait_bytes(last_box.at[pl.ds(0, owners - 1)], lse_recv.at[2])
    slot_rows = lax.broadcasted_iota(jnp.int32, (capacity, tile), 0) + me * capacity
    slot_lse = [jnp.zeros((capacity, tile), jnp.float32) for _ in range(tiles_dev)]
    for owner in range(owners):
        mine = (me == owner).astype(jnp.int32)

        def values(own, box, owner=owner, mine=mine):
            return jnp.where(jnp.full(own.shape, mine) > 0, own, box[owner].astype(jnp.float32))

        theirs = values(lse_buf[:first_rows, :], lse_box)
        last = values(lse_buf[first_rows:, :], last_box)
        for head in range(capacity):
            here = slot_rows == slot_buf[owner * capacity + head]
            source, first = (theirs, 0) if head < capacity - width else (last, capacity - width)
            for block in range(tiles_dev):
                row = (head - first) * tiles_dev + block
                row = jnp.broadcast_to(source[row : row + 1], (capacity, tile))
                slot_lse[block] = jnp.where(here, row, slot_lse[block])
    for block in range(tiles_dev):
        slot_lse_ref[:, block * tile : (block + 1) * tile] = slot_lse[block]

    wait_bytes(kv_buf.at[:, :, pl.ds(0, 3 * (owners - 1) * tok_dev // 2), :], in_send.at[0])
    per_sides(lambda n: wait_bytes(kv_buf.at[:, :, pl.ds(0, n * halo), :], halo_send.at[0]))
    wait_bytes(half, lse_send.at[0])
    when(inner == across, lambda: per_mate(lambda other: lse_relay(other).wait_send()))
    wait_bytes(last_box.at[pl.ds(0, owners - 1)], lse_send.at[2])
    wait_bytes(o_buf.at[:, pl.ds(0, (owners - 1) * tok_dev), :], out_send.at[0])
    wait_bytes(out_ref, out_recv.at[0])


def hand_over_kernel(out_in, lse_in, out_ref, lse_ref, sems):
    copies = [
        pltpu.make_async_copy(out_in, out_ref, sems.at[0]),
        pltpu.make_async_copy(lse_in, lse_ref, sems.at[1]),
    ]
    for copy in copies:
        copy.start()
    for copy in copies:
        copy.wait()


def on_device(query_rows, key_rows, value_rows, tile_mask, head_slot):
    owners = lax.axis_size("head")
    slabs = lax.axis_size("slab")
    tok_dev, model = query_rows.shape
    heads, tiles_dev, band = tile_mask.shape
    head_dim = model // heads
    capacity = (heads + owners - 1) // owners
    reach = (band - 1) // 2
    tok_slab = tok_dev * owners
    tile = tok_slab // tiles_dev
    halo = reach * tile
    whole = heads == owners * capacity
    width = HEADS_PER_CHUNK if whole and capacity % HEADS_PER_CHUNK == 0 else 1
    chunks = capacity // width
    line = whole and owners % 2 == 0 and owners <= 4 and chunks > 1 and 4 * halo >= tok_slab
    lanes = width * head_dim
    dims = (heads, head_dim, capacity, width, tok_dev, tile, reach)
    dma = pltpu.SemaphoreType.DMA
    tables = [
        pltpu.SMEM((band, tiles_dev, heads), jnp.int32),
        pltpu.SMEM((heads,), jnp.int32),
    ]
    if line:
        kernel = line_kernel
        first_rows = (capacity - width) * tiles_dev
        last_rows = -(-width * tiles_dev // 8) * 8
        scratch = [
            pltpu.VMEM((chunks, tok_slab, lanes), jnp.bfloat16),
            pltpu.VMEM((2, chunks, tok_slab + 2 * halo, lanes), jnp.bfloat16),
            pltpu.VMEM((chunks, tok_slab, lanes), jnp.bfloat16),
            pltpu.VMEM((first_rows + last_rows, tile), jnp.float32),
            pltpu.VMEM((owners, first_rows, tile), jnp.bfloat16),
            pltpu.VMEM((owners, last_rows, tile), jnp.bfloat16),
            *tables,
            dma((1,)),
            dma((3, chunks)),
            dma((1,)),
            dma((chunks,)),
            dma((1,)),
            dma((1,)),
            dma((3,)),
            dma((3,)),
            pltpu.SemaphoreType.REGULAR((owners,)),
            pltpu.SemaphoreType.REGULAR((1,)),
            dma((2,)),
        ]
    else:
        kernel = attention_kernel
        scratch = [
            pltpu.VMEM((chunks, tok_slab, lanes), jnp.bfloat16),
            pltpu.VMEM((chunks, tok_slab + 2 * halo, lanes), jnp.bfloat16),
            pltpu.VMEM((chunks, tok_slab + 2 * halo, lanes), jnp.bfloat16),
            pltpu.VMEM((chunks, tok_slab, lanes), jnp.bfloat16),
            pltpu.VMEM((owners, capacity, 1, tok_slab), jnp.float32),
            *tables,
            dma((3, chunks, owners)),
            dma((3, chunks, owners)),
            dma((2, chunks, 2)),
            dma((2, chunks, 2)),
            dma((chunks, owners)),
            dma((chunks, owners)),
            dma((owners,)),
            dma((owners,)),
            dma((2,)),
        ]
    gathered, gathered_lse = pl.pallas_call(
        functools.partial(kernel, owners, slabs, dims),
        out_shape=(
            jax.ShapeDtypeStruct((tok_dev, model), jnp.bfloat16),
            jax.ShapeDtypeStruct((capacity, tok_slab), jnp.float32),
        ),
        in_specs=[pl.BlockSpec(memory_space=pltpu.HBM)] * 5,
        out_specs=(pl.BlockSpec(memory_space=pltpu.VMEM), pl.BlockSpec(memory_space=pltpu.VMEM)),
        scratch_shapes=scratch,
        compiler_params=pltpu.CompilerParams(collective_id=0, has_side_effects=True, vmem_limit_bytes=16 << 20),
    )(*[pltpu.with_memory_space_constraint(x, pltpu.HBM) for x in (query_rows, key_rows, value_rows, jnp.transpose(tile_mask, (2, 1, 0)), head_slot)])
    vmem = pl.BlockSpec(memory_space=pltpu.VMEM)
    hbm = pl.BlockSpec(memory_space=pltpu.HBM)
    return pl.pallas_call(
        hand_over_kernel,
        out_shape=(
            jax.ShapeDtypeStruct(gathered.shape, gathered.dtype),
            jax.ShapeDtypeStruct(gathered_lse.shape, gathered_lse.dtype),
        ),
        in_specs=[vmem, vmem],
        out_specs=(hbm, hbm),
        scratch_shapes=[dma((2,))],
        compiler_params=pltpu.CompilerParams(vmem_limit_bytes=16 << 20),
    )(gathered, gathered_lse)


def solution(mesh):
    in_specs = (
        P(("groups", "slab", "head"), None),
        P(("groups", "slab", "head"), None),
        P(("groups", "slab", "head"), None),
        P(None, ("groups", "slab"), None),
        P(),
    )
    out_specs = (P(("groups", "slab", "head"), None), P("head", ("groups", "slab")))
    return jax.shard_map(
        on_device, mesh=mesh, in_specs=in_specs, out_specs=out_specs, check_vma=False
    )
```

```python
import functools

import jax
import jax.numpy as jnp
from jax import lax
from jax.experimental import pallas as pl
from jax.experimental.pallas import tpu as pltpu
from jax.sharding import PartitionSpec as P

MESH = pl.DeviceIdType.MESH
HEADS_PER_CHUNK = 2
EARLY_CHUNKS = 4
QUERY_LAG = 0
HELD_CHUNKS = 3
FLOOR = -1e30


def attention_kernel(
    owners,
    slabs,
    dims,
    q_ref,
    k_ref,
    v_ref,
    mask_ref,
    slot_ref,
    out_ref,
    slot_lse_ref,
    q_buf,
    k_buf,
    v_buf,
    o_buf,
    lse_buf,
    mask_buf,
    slot_buf,
    in_send,
    in_recv,
    halo_send,
    halo_recv,
    out_send,
    out_recv,
    lse_send,
    lse_recv,
    small_sem,
):
    heads, head_dim, capacity, width, tok_dev, tile, reach = dims
    chunks = capacity // width
    lanes = width * head_dim
    tok_slab = tok_dev * owners
    tiles_dev = tok_slab // tile
    band = 2 * reach + 1
    halo = reach * tile
    full = heads == owners * capacity
    scale = head_dim ** (-0.5)
    me = lax.axis_index("head")
    slab = lax.axis_index("slab")
    inputs = ((k_ref, k_buf, halo), (v_ref, v_buf, halo), (q_ref, q_buf, 0))
    peers = [(sign, dist) for dist in range(owners - 1, 0, -1) for sign in (1, -1)]

    def when(condition, body):
        pl.when(condition)(body)

    def per_peer(body):
        for sign, dist in peers:
            other = me + sign * dist
            when((other >= 0) & (other < owners), functools.partial(body, other))

    def if_held(owner, chunk, body):
        if full:
            body()
        else:
            when(owner * capacity + chunk * width < heads, body)

    def columns(owner, chunk):
        first = (owner * capacity + chunk * width) * head_dim
        return pl.ds(pl.multiple_of(first, head_dim), lanes)

    def rows(owner, base):
        return pl.ds(pl.multiple_of(owner * tok_dev + base, tok_dev), tok_dev)

    def in_copy(which, chunk, src_owner, dst_owner):
        ref, buf, base = inputs[which]
        return pltpu.make_async_remote_copy(
            src_ref=ref.at[:, columns(dst_owner, chunk)],
            dst_ref=buf.at[chunk, rows(src_owner, base), :],
            send_sem=in_send.at[which, chunk, dst_owner],
            recv_sem=in_recv.at[which, chunk, src_owner],
            device_id={"head": dst_owner},
            device_id_type=MESH,
        )

    def own_copy(which, chunk):
        ref, buf, base = inputs[which]
        return pltpu.make_async_copy(
            ref.at[:, columns(me, chunk)],
            buf.at[chunk, rows(me, base), :],
            in_recv.at[which, chunk, me],
        )

    def halo_copy(which, chunk, up):
        buf = inputs[which][1]
        source = tok_slab if up else halo
        target = 0 if up else halo + tok_slab
        return pltpu.make_async_remote_copy(
            src_ref=buf.at[chunk, pl.ds(source, halo), :],
            dst_ref=buf.at[chunk, pl.ds(target, halo), :],
            send_sem=halo_send.at[which, chunk, int(up)],
            recv_sem=halo_recv.at[which, chunk, int(up)],
            device_id={"slab": slab + 1 if up else slab - 1},
            device_id_type=MESH,
        )

    def out_copy(chunk, src_owner, dst_owner):
        return pltpu.make_async_remote_copy(
            src_ref=o_buf.at[chunk, rows(dst_owner, 0), :],
            dst_ref=out_ref.at[:, columns(src_owner, chunk)],
            send_sem=out_send.at[chunk, dst_owner],
            recv_sem=out_recv.at[chunk, src_owner],
            device_id={"head": dst_owner},
            device_id_type=MESH,
        )

    def out_own(chunk):
        return pltpu.make_async_copy(
            o_buf.at[chunk, rows(me, 0), :],
            out_ref.at[:, columns(me, chunk)],
            out_recv.at[chunk, me],
        )

    def lse_copy(src_owner, dst_owner):
        return pltpu.make_async_remote_copy(
            src_ref=lse_buf.at[src_owner],
            dst_ref=lse_buf.at[src_owner],
            send_sem=lse_send.at[dst_owner],
            recv_sem=lse_recv.at[src_owner],
            device_id={"head": dst_owner},
            device_id_type=MESH,
        )

    has_up = slab < slabs - 1
    has_down = slab > 0
    barrier = pltpu.get_barrier_semaphore()

    def greet(other):
        pl.semaphore_signal(barrier, inc=1, device_id={"head": other}, device_id_type=MESH)

    per_peer(greet)

    @pl.when(has_up)
    def _():
        pl.semaphore_signal(barrier, inc=1, device_id={"slab": slab + 1}, device_id_type=MESH)

    @pl.when(has_down)
    def _():
        pl.semaphore_signal(barrier, inc=1, device_id={"slab": slab - 1}, device_id_type=MESH)

    mask_copy = pltpu.make_async_copy(mask_ref, mask_buf, small_sem.at[0])
    slot_copy = pltpu.make_async_copy(slot_ref, slot_buf, small_sem.at[1])
    mask_copy.start()
    slot_copy.start()
    pl.semaphore_wait(
        barrier, owners - 1 + has_up.astype(jnp.int32) + has_down.astype(jnp.int32)
    )

    low_half = me < owners // 2

    def send_inputs(crossing, chunk, carry):
        for which in range(3):

            def to_peer(other, which=which):
                def go():
                    if_held(other, chunk, lambda: in_copy(which, chunk, me, other).start())

                other_side = low_half != (other < owners // 2)
                when(other_side if crossing else jnp.logical_not(other_side), go)

            per_peer(to_peer)
            if crossing:
                if_held(me, chunk, lambda which=which: own_copy(which, chunk).start())
        return carry

    lax.fori_loop(0, chunks, functools.partial(send_inputs, False), 0)
    lax.fori_loop(0, chunks, functools.partial(send_inputs, True), 0)

    if not full:
        lse_buf[me] = jnp.zeros(lse_buf.shape[1:], jnp.float32)

    @pl.when(jnp.logical_not(has_down))
    def _():
        v_buf[:, :halo, :] = jnp.zeros((chunks, halo, lanes), jnp.bfloat16)

    @pl.when(jnp.logical_not(has_up))
    def _():
        v_buf[:, halo + tok_slab :, :] = jnp.zeros((chunks, halo, lanes), jnp.bfloat16)

    mask_copy.wait()
    slot_copy.wait()

    def wait_input(which, chunk):
        per_peer(lambda other: in_copy(which, chunk, other, me).wait_recv())
        own_copy(which, chunk).wait()

    def forward(chunk):
        for which in range(2):
            wait_input(which, chunk)
            when(has_up, lambda: halo_copy(which, chunk, True).start())
            when(has_down, lambda: halo_copy(which, chunk, False).start())

    def attend(chunk):
        for which in range(2):
            when(has_down, lambda: halo_copy(which, chunk, True).wait_recv())
            when(has_up, lambda: halo_copy(which, chunk, False).wait_recv())
        wait_input(2, chunk)
        for within in range(width):
            column = slice(within * head_dim, (within + 1) * head_dim)
            local_head = chunk * width + within
            global_head = me * capacity + local_head
            for block in range(tiles_dev):
                q_rows = slice(block * tile, (block + 1) * tile)
                queries = q_buf[chunk, q_rows, column]
                window = slice(block * tile, (block + band) * tile)
                keys = k_buf[chunk, window, column]
                values = v_buf[chunk, window, column]
                scores = (
                    lax.dot_general(
                        keys, queries, (((1,), (1,)), ((), ())), preferred_element_type=jnp.float32
                    )
                    * scale
                )
                parts = []
                for place in range(band):
                    key_tile = slab * tiles_dev + block + place - reach
                    inside = ((key_tile >= 0) & (key_tile < slabs * tiles_dev)).astype(jnp.int32)
                    flag = mask_buf[place, block, global_head] * inside
                    allowed = jnp.full((tile, tile), flag, jnp.int32) > 0
                    parts.append(
                        jnp.where(allowed, scores[place * tile : (place + 1) * tile], FLOOR)
                    )
                masked = jnp.concatenate(parts, axis=0)
                highest = jnp.max(masked, axis=0, keepdims=True)
                weights = jnp.exp(masked - highest)
                total = jnp.sum(weights, axis=0, keepdims=True)
                summed = lax.dot_general(
                    values,
                    weights.astype(jnp.bfloat16),
                    (((0,), (0,)), ((), ())),
                    preferred_element_type=jnp.float32,
                )
                result = jnp.transpose(summed / total)
                o_buf[chunk, q_rows, column] = result.astype(jnp.bfloat16)
                lse_buf[me, local_head, :, q_rows] = highest + jnp.log(total)

    def send_out(chunk):
        per_peer(lambda other: out_copy(chunk, me, other).start())
        out_own(chunk).start()

    if_held(me, 0, lambda: forward(0))

    def step(chunk, carry):
        if_held(me, chunk, lambda: forward(chunk))

        def finish():
            attend(chunk - 1)
            send_out(chunk - 1)

        if_held(me, chunk - 1, finish)
        return carry

    lax.fori_loop(1, chunks, step, 0)
    last = chunks - 1
    if_held(me, last, lambda: attend(last))
    per_peer(lambda other: lse_copy(me, other).start())
    if_held(me, last, lambda: send_out(last))

    per_peer(lambda other: lse_copy(other, me).wait_recv())
    slot_rows = lax.broadcasted_iota(jnp.int32, (capacity, tok_slab), 0) + me * capacity
    slot_lse = jnp.zeros((capacity, tok_slab), jnp.float32)
    for head in range(heads):
        row = jnp.broadcast_to(lse_buf[head // capacity, head % capacity], (capacity, tok_slab))
        slot_lse = jnp.where(slot_rows == slot_buf[head], row, slot_lse)
    slot_lse_ref[...] = slot_lse

    def drain(chunk, carry):
        for which in range(3):

            def sent(other, which=which):
                if_held(other, chunk, lambda: in_copy(which, chunk, me, other).wait_send())

            per_peer(sent)

        def mine():
            for which in range(2):
                when(has_up, lambda: halo_copy(which, chunk, True).wait_send())
                when(has_down, lambda: halo_copy(which, chunk, False).wait_send())
            per_peer(lambda other: out_copy(chunk, me, other).wait_send())
            out_own(chunk).wait()

        if_held(me, chunk, mine)

        def arrived(other):
            if_held(other, chunk, lambda: out_copy(chunk, other, me).wait_recv())

        per_peer(arrived)
        return carry

    lax.fori_loop(0, chunks, drain, 0)
    per_peer(lambda other: lse_copy(me, other).wait_send())


def line_kernel(
    owners,
    slabs,
    dims,
    q_ref,
    k_ref,
    v_ref,
    mask_ref,
    slot_ref,
    out_ref,
    slot_lse_ref,
    q_buf,
    kv_buf,
    o_buf,
    lse_buf,
    lse_box,
    last_box,
    mask_buf,
    slot_buf,
    in_send,
    in_recv,
    halo_send,
    halo_recv,
    out_send,
    out_recv,
    lse_send,
    lse_recv,
    seen,
    beside,
    small_sem,
):
    heads, head_dim, capacity, width, tok_dev, tile, reach = dims
    chunks = capacity // width
    lanes = width * head_dim
    tok_slab = tok_dev * owners
    tiles_dev = tok_slab // tile
    band = 2 * reach + 1
    halo = reach * tile
    mid = owners // 2
    early = min(EARLY_CHUNKS, chunks)
    hold_from = max(chunks - HELD_CHUNKS, 0)
    first_rows = (capacity - width) * tiles_dev
    scale = head_dim ** (-0.5)
    me = lax.axis_index("head")
    slab = lax.axis_index("slab")
    low = me < mid
    inward = jnp.where(low, 1, -1)
    inner = me + inward
    outer = me - inward
    across = jnp.where(low, mid, mid - 1)
    has_up = slab < slabs - 1
    has_down = slab > 0
    inputs = ((k_ref, kv_buf.at[0], halo), (v_ref, kv_buf.at[1], halo), (q_ref, q_buf, 0))
    peers = [(sign, dist) for dist in range(owners - 1, 0, -1) for sign in (1, -1)]

    def when(condition, body):
        pl.when(condition)(body)

    def exists(other):
        return (other >= 0) & (other < owners)

    def columns(owner, chunk):
        first = (owner * capacity + chunk * width) * head_dim
        return pl.ds(pl.multiple_of(first, head_dim), lanes)

    def rows(owner, base):
        return pl.ds(pl.multiple_of(owner * tok_dev + base, tok_dev), tok_dev)

    def wait_bytes(ref, sem):
        pltpu.make_async_copy(ref, ref, sem).wait()

    def in_copy(which, chunk, dst_owner):
        ref, buf, base = inputs[which]
        return pltpu.make_async_remote_copy(
            src_ref=ref.at[:, columns(dst_owner, chunk)],
            dst_ref=buf.at[chunk, rows(me, base), :],
            send_sem=in_send.at[0],
            recv_sem=in_recv.at[which, chunk],
            device_id={"head": dst_owner},
            device_id_type=MESH,
        )

    def own_copy(which, chunk):
        ref, buf, base = inputs[which]
        return pltpu.make_async_copy(
            ref.at[:, columns(me, chunk)],
            buf.at[chunk, rows(me, base), :],
            in_recv.at[which, chunk],
        )

    def halo_copy(which, chunk, up):
        source = tok_slab if up else halo
        target = 0 if up else halo + tok_slab
        return pltpu.make_async_remote_copy(
            src_ref=kv_buf.at[which, chunk, pl.ds(source, halo), :],
            dst_ref=kv_buf.at[which, chunk, pl.ds(target, halo), :],
            send_sem=halo_send.at[0],
            recv_sem=halo_recv.at[chunk],
            device_id={"slab": slab + 1 if up else slab - 1},
            device_id_type=MESH,
        )

    def per_sides(body):
        both = has_up & has_down
        when(both, lambda: body(2))
        when(jnp.logical_not(both) & (has_up | has_down), lambda: body(1))

    def out_copy(chunk, dst_owner):
        return pltpu.make_async_remote_copy(
            src_ref=o_buf.at[chunk, rows(dst_owner, 0), :],
            dst_ref=out_ref.at[:, columns(me, chunk)],
            send_sem=out_send.at[0],
            recv_sem=out_recv.at[0],
            device_id={"head": dst_owner},
            device_id_type=MESH,
        )

    def out_own(chunk):
        return pltpu.make_async_copy(
            o_buf.at[chunk, rows(me, 0), :],
            out_ref.at[:, columns(me, chunk)],
            out_recv.at[0],
        )

    def lse_copy(dst_owner, crossing):
        return pltpu.make_async_remote_copy(
            src_ref=lse_box.at[me],
            dst_ref=lse_box.at[me],
            send_sem=lse_send.at[0],
            recv_sem=lse_recv.at[int(crossing)],
            device_id={"head": dst_owner},
            device_id_type=MESH,
        )

    def lse_relay(dst_owner):
        boxes = lse_box.at[pl.ds(jnp.where(low, mid, 0), mid)]
        return pltpu.make_async_remote_copy(
            src_ref=boxes,
            dst_ref=boxes,
            send_sem=lse_send.at[1],
            recv_sem=lse_recv.at[1],
            device_id={"head": dst_owner},
            device_id_type=MESH,
        )

    def last_copy(dst_owner):
        return pltpu.make_async_remote_copy(
            src_ref=last_box.at[me],
            dst_ref=last_box.at[me],
            send_sem=lse_send.at[2],
            recv_sem=lse_recv.at[2],
            device_id={"head": dst_owner},
            device_id_type=MESH,
        )

    barrier = pltpu.get_barrier_semaphore()

    def greet(device):
        pl.semaphore_signal(barrier, inc=1, device_id=device, device_id_type=MESH)

    when(inner == across, lambda: greet({"head": inner}))
    when(exists(outer), lambda: greet({"head": outer}))
    at_end = jnp.logical_not(exists(outer))
    end_up = at_end & has_up
    end_down = at_end & has_down
    when(end_up, lambda: greet({"slab": slab + 1}))
    when(end_down, lambda: greet({"slab": slab - 1}))

    mask_copy = pltpu.make_async_copy(mask_ref, mask_buf, small_sem.at[0])
    slot_copy = pltpu.make_async_copy(slot_ref, slot_buf, small_sem.at[1])
    pl.semaphore_wait(barrier, 1 + end_up.astype(jnp.int32) + end_down.astype(jnp.int32))

    for chunk in range(early):
        for which in range(3):
            in_copy(which, chunk, inner).start()

    mask_copy.start()
    slot_copy.start()

    def tell(owner, about):
        pl.semaphore_signal(seen.at[about], inc=1, device_id={"head": owner}, device_id_type=MESH)

    when(inner != across, lambda: tell(inner, me))
    for dist in range(1, mid):
        other = me - inward * dist

        def outward(other=other, dist=dist):
            pl.semaphore_wait(seen.at[other], 1)
            tell(inner, other)
            if dist == 1:
                tell(outer, inner)

        when(exists(other), outward)
    for dist in range(2, owners):
        other = me + inward * dist

        def further(other=other):
            pl.semaphore_wait(seen.at[other], 1)
            when(exists(outer), lambda: tell(outer, other))

        when(exists(other), further)

    def tell_beside(device):
        pl.semaphore_signal(beside.at[0], inc=1, device_id=device, device_id_type=MESH)

    when(end_up, lambda: tell_beside({"slab": slab + 1}))
    when(end_down, lambda: tell_beside({"slab": slab - 1}))

    def send_input(which, chunk):
        for sign, dist in peers:
            other = me + sign * dist
            wanted = exists(other)
            if dist == 1:
                wanted = wanted & ((other != inner) | (chunk >= early))
            when(wanted, lambda other=other: in_copy(which, chunk, other).start())
        own_copy(which, chunk).start()

    lead = min(QUERY_LAG, chunks)

    def send_inputs(chunk, carry):
        def ahead():
            send_input(0, chunk)
            send_input(1, chunk)

        when(chunk < chunks, ahead)
        when(chunk >= lead, lambda: send_input(2, chunk - lead))
        return carry

    lax.fori_loop(0, chunks + lead, send_inputs, 0)

    @pl.when(jnp.logical_not(has_down))
    def _():
        kv_buf[1, :, :halo, :] = jnp.zeros((chunks, halo, lanes), jnp.bfloat16)

    @pl.when(jnp.logical_not(has_up))
    def _():
        kv_buf[1, :, halo + tok_slab :, :] = jnp.zeros((chunks, halo, lanes), jnp.bfloat16)

    lse_buf[...] = jnp.zeros(lse_buf.shape, jnp.float32)
    if slabs > 1:
        heard = jnp.where(at_end, has_up.astype(jnp.int32) + has_down.astype(jnp.int32), 1)
        pl.semaphore_wait(beside.at[0], heard)
        when(inner != across, lambda: tell_beside({"head": inner}))

    mask_copy.wait()
    slot_copy.wait()

    def forward(chunk):
        for which in range(2):
            wait_bytes(kv_buf.at[which, chunk, pl.ds(halo, tok_slab), :], in_recv.at[which, chunk])
            when(has_up, lambda which=which: halo_copy(which, chunk, True).start())
            when(has_down, lambda which=which: halo_copy(which, chunk, False).start())

    def attend(chunk):
        per_sides(lambda n: wait_bytes(kv_buf.at[:, chunk, pl.ds(0, n * halo), :], halo_recv.at[chunk]))
        wait_bytes(q_buf.at[chunk], in_recv.at[2, chunk])
        for within in range(width):
            column = slice(within * head_dim, (within + 1) * head_dim)
            local_head = chunk * width + within
            global_head = me * capacity + local_head
            for block in range(tiles_dev):
                q_rows = slice(block * tile, (block + 1) * tile)
                queries = q_buf[chunk, q_rows, column]
                window = slice(block * tile, (block + band) * tile)
                keys = kv_buf[0, chunk, window, column]
                values = kv_buf[1, chunk, window, column]
                scores = (
                    lax.dot_general(
                        keys, queries, (((1,), (1,)), ((), ())), preferred_element_type=jnp.float32
                    )
                    * scale
                )
                parts = []
                for place in range(band):
                    key_tile = slab * tiles_dev + block + place - reach
                    inside = ((key_tile >= 0) & (key_tile < slabs * tiles_dev)).astype(jnp.int32)
                    flag = mask_buf[place, block, global_head] * inside
                    allowed = jnp.full((tile, tile), flag, jnp.int32) > 0
                    parts.append(
                        jnp.where(allowed, scores[place * tile : (place + 1) * tile], FLOOR)
                    )
                masked = jnp.concatenate(parts, axis=0)
                highest = jnp.max(masked, axis=0, keepdims=True)
                weights = jnp.exp(masked - highest)
                total = jnp.sum(weights, axis=0, keepdims=True)
                summed = lax.dot_general(
                    values,
                    weights.astype(jnp.bfloat16),
                    (((0,), (0,)), ((), ())),
                    preferred_element_type=jnp.float32,
                )
                result = jnp.transpose(summed / total)
                o_buf[chunk, q_rows, column] = result.astype(jnp.bfloat16)
                row = local_head * tiles_dev + block
                lse_buf[pl.ds(row, 1), :] = highest + jnp.log(total)

    def send_out(chunk):
        for sign, dist in peers:
            other = me + sign * dist
            wanted = exists(other) & ((other != across) | (chunk < hold_from))
            when(wanted, lambda other=other: out_copy(chunk, other).start())
        out_own(chunk).start()

    side = jnp.where(low, 0, mid)
    mates = [(sign, dist) for dist in range(mid - 1, 0, -1) for sign in (1, -1)]

    def per_mate(body):
        for sign, dist in mates:
            other = me + sign * dist
            when((other >= side) & (other < side + mid), functools.partial(body, other))

    def send_lse():
        lse_box[me] = lse_buf[:first_rows, :].astype(jnp.bfloat16)
        lse_copy(across, True).start()
        per_mate(lambda other: lse_copy(other, False).start())

    forward(0)

    def step(chunk, carry):
        when(chunk < chunks, lambda: forward(chunk))
        attend(chunk - 1)
        when(chunk == chunks - 1, send_lse)
        send_out(chunk - 1)
        return carry

    lax.fori_loop(1, chunks + 1, step, 0)

    last_box[me] = lse_buf[first_rows:, :].astype(jnp.bfloat16)
    for sign, dist in peers:
        other = me + sign * dist
        when(exists(other), lambda other=other: last_copy(other).start())
    for chunk in range(hold_from, chunks):
        out_copy(chunk, across).start()

    half = lse_box.at[pl.ds(0, mid)]
    wait_bytes(half, lse_recv.at[1])
    when(inner == across, lambda: per_mate(lambda other: lse_relay(other).start()))
    if mid > 1:
        wait_bytes(lse_box.at[pl.ds(0, mid - 1)], lse_recv.at[0])
    wait_bytes(last_box.at[pl.ds(0, owners - 1)], lse_recv.at[2])
    slot_rows = lax.broadcasted_iota(jnp.int32, (capacity, tile), 0) + me * capacity
    slot_lse = [jnp.zeros((capacity, tile), jnp.float32) for _ in range(tiles_dev)]
    for owner in range(owners):
        mine = (me == owner).astype(jnp.int32)

        def values(own, box, owner=owner, mine=mine):
            return jnp.where(jnp.full(own.shape, mine) > 0, own, box[owner].astype(jnp.float32))

        theirs = values(lse_buf[:first_rows, :], lse_box)
        last = values(lse_buf[first_rows:, :], last_box)
        for head in range(capacity):
            here = slot_rows == slot_buf[owner * capacity + head]
            source, first = (theirs, 0) if head < capacity - width else (last, capacity - width)
            for block in range(tiles_dev):
                row = (head - first) * tiles_dev + block
                row = jnp.broadcast_to(source[row : row + 1], (capacity, tile))
                slot_lse[block] = jnp.where(here, row, slot_lse[block])
    for block in range(tiles_dev):
        slot_lse_ref[:, block * tile : (block + 1) * tile] = slot_lse[block]

    wait_bytes(kv_buf.at[:, :, pl.ds(0, 3 * (owners - 1) * tok_dev // 2), :], in_send.at[0])
    per_sides(lambda n: wait_bytes(kv_buf.at[:, :, pl.ds(0, n * halo), :], halo_send.at[0]))
    wait_bytes(half, lse_send.at[0])
    when(inner == across, lambda: per_mate(lambda other: lse_relay(other).wait_send()))
    wait_bytes(last_box.at[pl.ds(0, owners - 1)], lse_send.at[2])
    wait_bytes(o_buf.at[:, pl.ds(0, (owners - 1) * tok_dev), :], out_send.at[0])
    wait_bytes(out_ref, out_recv.at[0])


def hand_over_kernel(out_in, lse_in, out_ref, lse_ref, sems):
    copies = [
        pltpu.make_async_copy(out_in, out_ref, sems.at[0]),
        pltpu.make_async_copy(lse_in, lse_ref, sems.at[1]),
    ]
    for copy in copies:
        copy.start()
    for copy in copies:
        copy.wait()


def on_device(query_rows, key_rows, value_rows, tile_mask, head_slot):
    owners = lax.axis_size("head")
    slabs = lax.axis_size("slab")
    tok_dev, model = query_rows.shape
    heads, tiles_dev, band = tile_mask.shape
    head_dim = model // heads
    capacity = (heads + owners - 1) // owners
    reach = (band - 1) // 2
    tok_slab = tok_dev * owners
    tile = tok_slab // tiles_dev
    halo = reach * tile
    whole = heads == owners * capacity
    width = HEADS_PER_CHUNK if whole and capacity % HEADS_PER_CHUNK == 0 else 1
    chunks = capacity // width
    line = whole and owners % 2 == 0 and owners <= 4 and chunks > 1 and 4 * halo >= tok_slab
    lanes = width * head_dim
    dims = (heads, head_dim, capacity, width, tok_dev, tile, reach)
    dma = pltpu.SemaphoreType.DMA
    tables = [
        pltpu.SMEM((band, tiles_dev, heads), jnp.int32),
        pltpu.SMEM((heads,), jnp.int32),
    ]
    if line:
        kernel = line_kernel
        first_rows = (capacity - width) * tiles_dev
        last_rows = -(-width * tiles_dev // 8) * 8
        scratch = [
            pltpu.VMEM((chunks, tok_slab, lanes), jnp.bfloat16),
            pltpu.VMEM((2, chunks, tok_slab + 2 * halo, lanes), jnp.bfloat16),
            pltpu.VMEM((chunks, tok_slab, lanes), jnp.bfloat16),
            pltpu.VMEM((first_rows + last_rows, tile), jnp.float32),
            pltpu.VMEM((owners, first_rows, tile), jnp.bfloat16),
            pltpu.VMEM((owners, last_rows, tile), jnp.bfloat16),
            *tables,
            dma((1,)),
            dma((3, chunks)),
            dma((1,)),
            dma((chunks,)),
            dma((1,)),
            dma((1,)),
            dma((3,)),
            dma((3,)),
            pltpu.SemaphoreType.REGULAR((owners,)),
            pltpu.SemaphoreType.REGULAR((1,)),
            dma((2,)),
        ]
    else:
        kernel = attention_kernel
        scratch = [
            pltpu.VMEM((chunks, tok_slab, lanes), jnp.bfloat16),
            pltpu.VMEM((chunks, tok_slab + 2 * halo, lanes), jnp.bfloat16),
            pltpu.VMEM((chunks, tok_slab + 2 * halo, lanes), jnp.bfloat16),
            pltpu.VMEM((chunks, tok_slab, lanes), jnp.bfloat16),
            pltpu.VMEM((owners, capacity, 1, tok_slab), jnp.float32),
            *tables,
            dma((3, chunks, owners)),
            dma((3, chunks, owners)),
            dma((2, chunks, 2)),
            dma((2, chunks, 2)),
            dma((chunks, owners)),
            dma((chunks, owners)),
            dma((owners,)),
            dma((owners,)),
            dma((2,)),
        ]
    gathered, gathered_lse = pl.pallas_call(
        functools.partial(kernel, owners, slabs, dims),
        out_shape=(
            jax.ShapeDtypeStruct((tok_dev, model), jnp.bfloat16),
            jax.ShapeDtypeStruct((capacity, tok_slab), jnp.float32),
        ),
        in_specs=[pl.BlockSpec(memory_space=pltpu.HBM)] * 5,
        out_specs=(pl.BlockSpec(memory_space=pltpu.VMEM), pl.BlockSpec(memory_space=pltpu.VMEM)),
        scratch_shapes=scratch,
        compiler_params=pltpu.CompilerParams(collective_id=0, has_side_effects=True, vmem_limit_bytes=16 << 20),
    )(*[pltpu.with_memory_space_constraint(x, pltpu.HBM) for x in (query_rows, key_rows, value_rows, jnp.transpose(tile_mask, (2, 1, 0)), head_slot)])
    vmem = pl.BlockSpec(memory_space=pltpu.VMEM)
    hbm = pl.BlockSpec(memory_space=pltpu.HBM)
    return pl.pallas_call(
        hand_over_kernel,
        out_shape=(
            jax.ShapeDtypeStruct(gathered.shape, gathered.dtype),
            jax.ShapeDtypeStruct(gathered_lse.shape, gathered_lse.dtype),
        ),
        in_specs=[vmem, vmem],
        out_specs=(hbm, hbm),
        scratch_shapes=[dma((2,))],
        compiler_params=pltpu.CompilerParams(vmem_limit_bytes=16 << 20),
    )(gathered, gathered_lse)


def solution(mesh):
    in_specs = (
        P(("groups", "slab", "head"), None),
        P(("groups", "slab", "head"), None),
        P(("groups", "slab", "head"), None),
        P(None, ("groups", "slab"), None),
        P(),
    )
    out_specs = (P(("groups", "slab", "head"), None), P("head", ("groups", "slab")))
    return jax.shard_map(
        on_device, mesh=mesh, in_specs=in_specs, out_specs=out_specs, check_vma=False
    )
```

```python
import functools

import jax
import jax.numpy as jnp
from jax import lax
from jax.experimental import pallas as pl
from jax.experimental.pallas import tpu as pltpu
from jax.sharding import PartitionSpec as P

MESH = pl.DeviceIdType.MESH
HEADS_PER_CHUNK = 2
EARLY_CHUNKS = 3
QUERY_LAG = 0
HELD_CHUNKS = 3
FLOOR = -1e30


def attention_kernel(
    owners,
    slabs,
    dims,
    q_ref,
    k_ref,
    v_ref,
    mask_ref,
    slot_ref,
    out_ref,
    slot_lse_ref,
    q_buf,
    k_buf,
    v_buf,
    o_buf,
    lse_buf,
    mask_buf,
    slot_buf,
    in_send,
    in_recv,
    halo_send,
    halo_recv,
    out_send,
    out_recv,
    lse_send,
    lse_recv,
    small_sem,
):
    heads, head_dim, capacity, width, tok_dev, tile, reach = dims
    chunks = capacity // width
    lanes = width * head_dim
    tok_slab = tok_dev * owners
    tiles_dev = tok_slab // tile
    band = 2 * reach + 1
    halo = reach * tile
    full = heads == owners * capacity
    scale = head_dim ** (-0.5)
    me = lax.axis_index("head")
    slab = lax.axis_index("slab")
    inputs = ((k_ref, k_buf, halo), (v_ref, v_buf, halo), (q_ref, q_buf, 0))
    peers = [(sign, dist) for dist in range(owners - 1, 0, -1) for sign in (1, -1)]

    def when(condition, body):
        pl.when(condition)(body)

    def per_peer(body):
        for sign, dist in peers:
            other = me + sign * dist
            when((other >= 0) & (other < owners), functools.partial(body, other))

    def if_held(owner, chunk, body):
        if full:
            body()
        else:
            when(owner * capacity + chunk * width < heads, body)

    def columns(owner, chunk):
        first = (owner * capacity + chunk * width) * head_dim
        return pl.ds(pl.multiple_of(first, head_dim), lanes)

    def rows(owner, base):
        return pl.ds(pl.multiple_of(owner * tok_dev + base, tok_dev), tok_dev)

    def in_copy(which, chunk, src_owner, dst_owner):
        ref, buf, base = inputs[which]
        return pltpu.make_async_remote_copy(
            src_ref=ref.at[:, columns(dst_owner, chunk)],
            dst_ref=buf.at[chunk, rows(src_owner, base), :],
            send_sem=in_send.at[which, chunk, dst_owner],
            recv_sem=in_recv.at[which, chunk, src_owner],
            device_id={"head": dst_owner},
            device_id_type=MESH,
        )

    def own_copy(which, chunk):
        ref, buf, base = inputs[which]
        return pltpu.make_async_copy(
            ref.at[:, columns(me, chunk)],
            buf.at[chunk, rows(me, base), :],
            in_recv.at[which, chunk, me],
        )

    def halo_copy(which, chunk, up):
        buf = inputs[which][1]
        source = tok_slab if up else halo
        target = 0 if up else halo + tok_slab
        return pltpu.make_async_remote_copy(
            src_ref=buf.at[chunk, pl.ds(source, halo), :],
            dst_ref=buf.at[chunk, pl.ds(target, halo), :],
            send_sem=halo_send.at[which, chunk, int(up)],
            recv_sem=halo_recv.at[which, chunk, int(up)],
            device_id={"slab": slab + 1 if up else slab - 1},
            device_id_type=MESH,
        )

    def out_copy(chunk, src_owner, dst_owner):
        return pltpu.make_async_remote_copy(
            src_ref=o_buf.at[chunk, rows(dst_owner, 0), :],
            dst_ref=out_ref.at[:, columns(src_owner, chunk)],
            send_sem=out_send.at[chunk, dst_owner],
            recv_sem=out_recv.at[chunk, src_owner],
            device_id={"head": dst_owner},
            device_id_type=MESH,
        )

    def out_own(chunk):
        return pltpu.make_async_copy(
            o_buf.at[chunk, rows(me, 0), :],
            out_ref.at[:, columns(me, chunk)],
            out_recv.at[chunk, me],
        )

    def lse_copy(src_owner, dst_owner):
        return pltpu.make_async_remote_copy(
            src_ref=lse_buf.at[src_owner],
            dst_ref=lse_buf.at[src_owner],
            send_sem=lse_send.at[dst_owner],
            recv_sem=lse_recv.at[src_owner],
            device_id={"head": dst_owner},
            device_id_type=MESH,
        )

    has_up = slab < slabs - 1
    has_down = slab > 0
    barrier = pltpu.get_barrier_semaphore()

    def greet(other):
        pl.semaphore_signal(barrier, inc=1, device_id={"head": other}, device_id_type=MESH)

    per_peer(greet)

    @pl.when(has_up)
    def _():
        pl.semaphore_signal(barrier, inc=1, device_id={"slab": slab + 1}, device_id_type=MESH)

    @pl.when(has_down)
    def _():
        pl.semaphore_signal(barrier, inc=1, device_id={"slab": slab - 1}, device_id_type=MESH)

    mask_copy = pltpu.make_async_copy(mask_ref, mask_buf, small_sem.at[0])
    slot_copy = pltpu.make_async_copy(slot_ref, slot_buf, small_sem.at[1])
    mask_copy.start()
    slot_copy.start()
    pl.semaphore_wait(
        barrier, owners - 1 + has_up.astype(jnp.int32) + has_down.astype(jnp.int32)
    )

    low_half = me < owners // 2

    def send_inputs(crossing, chunk, carry):
        for which in range(3):

            def to_peer(other, which=which):
                def go():
                    if_held(other, chunk, lambda: in_copy(which, chunk, me, other).start())

                other_side = low_half != (other < owners // 2)
                when(other_side if crossing else jnp.logical_not(other_side), go)

            per_peer(to_peer)
            if crossing:
                if_held(me, chunk, lambda which=which: own_copy(which, chunk).start())
        return carry

    lax.fori_loop(0, chunks, functools.partial(send_inputs, False), 0)
    lax.fori_loop(0, chunks, functools.partial(send_inputs, True), 0)

    if not full:
        lse_buf[me] = jnp.zeros(lse_buf.shape[1:], jnp.float32)

    @pl.when(jnp.logical_not(has_down))
    def _():
        v_buf[:, :halo, :] = jnp.zeros((chunks, halo, lanes), jnp.bfloat16)

    @pl.when(jnp.logical_not(has_up))
    def _():
        v_buf[:, halo + tok_slab :, :] = jnp.zeros((chunks, halo, lanes), jnp.bfloat16)

    mask_copy.wait()
    slot_copy.wait()

    def wait_input(which, chunk):
        per_peer(lambda other: in_copy(which, chunk, other, me).wait_recv())
        own_copy(which, chunk).wait()

    def forward(chunk):
        for which in range(2):
            wait_input(which, chunk)
            when(has_up, lambda: halo_copy(which, chunk, True).start())
            when(has_down, lambda: halo_copy(which, chunk, False).start())

    def attend(chunk):
        for which in range(2):
            when(has_down, lambda: halo_copy(which, chunk, True).wait_recv())
            when(has_up, lambda: halo_copy(which, chunk, False).wait_recv())
        wait_input(2, chunk)
        for within in range(width):
            column = slice(within * head_dim, (within + 1) * head_dim)
            local_head = chunk * width + within
            global_head = me * capacity + local_head
            for block in range(tiles_dev):
                q_rows = slice(block * tile, (block + 1) * tile)
                queries = q_buf[chunk, q_rows, column]
                window = slice(block * tile, (block + band) * tile)
                keys = k_buf[chunk, window, column]
                values = v_buf[chunk, window, column]
                scores = (
                    lax.dot_general(
                        keys, queries, (((1,), (1,)), ((), ())), preferred_element_type=jnp.float32
                    )
                    * scale
                )
                parts = []
                for place in range(band):
                    key_tile = slab * tiles_dev + block + place - reach
                    inside = ((key_tile >= 0) & (key_tile < slabs * tiles_dev)).astype(jnp.int32)
                    flag = mask_buf[place, block, global_head] * inside
                    allowed = jnp.full((tile, tile), flag, jnp.int32) > 0
                    parts.append(
                        jnp.where(allowed, scores[place * tile : (place + 1) * tile], FLOOR)
                    )
                masked = jnp.concatenate(parts, axis=0)
                highest = jnp.max(masked, axis=0, keepdims=True)
                weights = jnp.exp(masked - highest)
                total = jnp.sum(weights, axis=0, keepdims=True)
                summed = lax.dot_general(
                    values,
                    weights.astype(jnp.bfloat16),
                    (((0,), (0,)), ((), ())),
                    preferred_element_type=jnp.float32,
                )
                result = jnp.transpose(summed / total)
                o_buf[chunk, q_rows, column] = result.astype(jnp.bfloat16)
                lse_buf[me, local_head, :, q_rows] = highest + jnp.log(total)

    def send_out(chunk):
        per_peer(lambda other: out_copy(chunk, me, other).start())
        out_own(chunk).start()

    if_held(me, 0, lambda: forward(0))

    def step(chunk, carry):
        if_held(me, chunk, lambda: forward(chunk))

        def finish():
            attend(chunk - 1)
            send_out(chunk - 1)

        if_held(me, chunk - 1, finish)
        return carry

    lax.fori_loop(1, chunks, step, 0)
    last = chunks - 1
    if_held(me, last, lambda: attend(last))
    per_peer(lambda other: lse_copy(me, other).start())
    if_held(me, last, lambda: send_out(last))

    per_peer(lambda other: lse_copy(other, me).wait_recv())
    slot_rows = lax.broadcasted_iota(jnp.int32, (capacity, tok_slab), 0) + me * capacity
    slot_lse = jnp.zeros((capacity, tok_slab), jnp.float32)
    for head in range(heads):
        row = jnp.broadcast_to(lse_buf[head // capacity, head % capacity], (capacity, tok_slab))
        slot_lse = jnp.where(slot_rows == slot_buf[head], row, slot_lse)
    slot_lse_ref[...] = slot_lse

    def drain(chunk, carry):
        for which in range(3):

            def sent(other, which=which):
                if_held(other, chunk, lambda: in_copy(which, chunk, me, other).wait_send())

            per_peer(sent)

        def mine():
            for which in range(2):
                when(has_up, lambda: halo_copy(which, chunk, True).wait_send())
                when(has_down, lambda: halo_copy(which, chunk, False).wait_send())
            per_peer(lambda other: out_copy(chunk, me, other).wait_send())
            out_own(chunk).wait()

        if_held(me, chunk, mine)

        def arrived(other):
            if_held(other, chunk, lambda: out_copy(chunk, other, me).wait_recv())

        per_peer(arrived)
        return carry

    lax.fori_loop(0, chunks, drain, 0)
    per_peer(lambda other: lse_copy(me, other).wait_send())


def line_kernel(
    owners,
    slabs,
    dims,
    q_ref,
    k_ref,
    v_ref,
    mask_ref,
    slot_ref,
    out_ref,
    slot_lse_ref,
    q_buf,
    kv_buf,
    o_buf,
    lse_buf,
    lse_box,
    last_box,
    first_buf,
    mask_buf,
    slot_buf,
    in_send,
    in_recv,
    halo_send,
    halo_recv,
    out_send,
    out_recv,
    lse_send,
    lse_recv,
    seen,
    beside,
    first_sem,
    small_sem,
):
    heads, head_dim, capacity, width, tok_dev, tile, reach = dims
    chunks = capacity // width
    lanes = width * head_dim
    tok_slab = tok_dev * owners
    tiles_dev = tok_slab // tile
    band = 2 * reach + 1
    halo = reach * tile
    mid = owners // 2
    early = min(EARLY_CHUNKS, chunks)
    hold_from = max(chunks - HELD_CHUNKS, 0)
    first_rows = (capacity - width) * tiles_dev
    scale = head_dim ** (-0.5)
    me = lax.axis_index("head")
    slab = lax.axis_index("slab")
    low = me < mid
    inward = jnp.where(low, 1, -1)
    inner = me + inward
    outer = me - inward
    across = jnp.where(low, mid, mid - 1)
    has_up = slab < slabs - 1
    has_down = slab > 0
    inputs = ((k_ref, kv_buf.at[0], halo), (v_ref, kv_buf.at[1], halo), (q_ref, q_buf, 0))
    peers = [(sign, dist) for dist in range(owners - 1, 0, -1) for sign in (1, -1)]

    def when(condition, body):
        pl.when(condition)(body)

    def exists(other):
        return (other >= 0) & (other < owners)

    def columns(owner, chunk):
        first = (owner * capacity + chunk * width) * head_dim
        return pl.ds(pl.multiple_of(first, head_dim), lanes)

    def rows(owner, base):
        return pl.ds(pl.multiple_of(owner * tok_dev + base, tok_dev), tok_dev)

    def wait_bytes(ref, sem):
        pltpu.make_async_copy(ref, ref, sem).wait()

    def in_copy(which, chunk, dst_owner, source=None):
        ref, buf, base = inputs[which]
        return pltpu.make_async_remote_copy(
            src_ref=ref.at[:, columns(dst_owner, chunk)] if source is None else source,
            dst_ref=buf.at[chunk, rows(me, base), :],
            send_sem=in_send.at[0],
            recv_sem=in_recv.at[which, chunk],
            device_id={"head": dst_owner},
            device_id_type=MESH,
        )

    def own_copy(which, chunk):
        ref, buf, base = inputs[which]
        return pltpu.make_async_copy(
            ref.at[:, columns(me, chunk)],
            buf.at[chunk, rows(me, base), :],
            in_recv.at[which, chunk],
        )

    def halo_copy(which, chunk, up):
        source = tok_slab if up else halo
        target = 0 if up else halo + tok_slab
        return pltpu.make_async_remote_copy(
            src_ref=kv_buf.at[which, chunk, pl.ds(source, halo), :],
            dst_ref=kv_buf.at[which, chunk, pl.ds(target, halo), :],
            send_sem=halo_send.at[0],
            recv_sem=halo_recv.at[chunk],
            device_id={"slab": slab + 1 if up else slab - 1},
            device_id_type=MESH,
        )

    def per_sides(body):
        both = has_up & has_down
        when(both, lambda: body(2))
        when(jnp.logical_not(both) & (has_up | has_down), lambda: body(1))

    def out_copy(chunk, dst_owner):
        return pltpu.make_async_remote_copy(
            src_ref=o_buf.at[chunk, rows(dst_owner, 0), :],
            dst_ref=out_ref.at[:, columns(me, chunk)],
            send_sem=out_send.at[0],
            recv_sem=out_recv.at[0],
            device_id={"head": dst_owner},
            device_id_type=MESH,
        )

    def out_own(chunk):
        return pltpu.make_async_copy(
            o_buf.at[chunk, rows(me, 0), :],
            out_ref.at[:, columns(me, chunk)],
            out_recv.at[0],
        )

    def lse_copy(dst_owner, crossing):
        return pltpu.make_async_remote_copy(
            src_ref=lse_box.at[me],
            dst_ref=lse_box.at[me],
            send_sem=lse_send.at[0],
            recv_sem=lse_recv.at[int(crossing)],
            device_id={"head": dst_owner},
            device_id_type=MESH,
        )

    def lse_relay(dst_owner):
        boxes = lse_box.at[pl.ds(jnp.where(low, mid, 0), mid)]
        return pltpu.make_async_remote_copy(
            src_ref=boxes,
            dst_ref=boxes,
            send_sem=lse_send.at[1],
            recv_sem=lse_recv.at[1],
            device_id={"head": dst_owner},
            device_id_type=MESH,
        )

    def last_copy(dst_owner):
        return pltpu.make_async_remote_copy(
            src_ref=last_box.at[me],
            dst_ref=last_box.at[me],
            send_sem=lse_send.at[2],
            recv_sem=lse_recv.at[2],
            device_id={"head": dst_owner},
            device_id_type=MESH,
        )

    barrier = pltpu.get_barrier_semaphore()

    def greet(device):
        pl.semaphore_signal(barrier, inc=1, device_id=device, device_id_type=MESH)

    when(inner == across, lambda: greet({"head": inner}))
    when(exists(outer), lambda: greet({"head": outer}))
    at_end = jnp.logical_not(exists(outer))
    end_up = at_end & has_up
    end_down = at_end & has_down
    when(end_up, lambda: greet({"slab": slab + 1}))
    when(end_down, lambda: greet({"slab": slab - 1}))

    mask_copy = pltpu.make_async_copy(mask_ref, mask_buf, small_sem.at[0])
    slot_copy = pltpu.make_async_copy(slot_ref, slot_buf, small_sem.at[1])
    def stage():
        for which in range(3):
            pltpu.make_async_copy(
                inputs[which][0].at[:, columns(inner, 0)], first_buf.at[which], first_sem.at[0]
            ).start()

    when(low, stage)
    pl.semaphore_wait(barrier, 1 + end_up.astype(jnp.int32) + end_down.astype(jnp.int32))

    def begin_staged():
        wait_bytes(first_buf, first_sem.at[0])
        for which in range(3):
            in_copy(which, 0, inner, first_buf.at[which]).start()

    def begin():
        for which in range(3):
            in_copy(which, 0, inner).start()

    when(low, begin_staged)
    when(jnp.logical_not(low), begin)
    for chunk in range(1, early):
        for which in range(3):
            in_copy(which, chunk, inner).start()

    mask_copy.start()
    slot_copy.start()

    def tell(owner, about):
        pl.semaphore_signal(seen.at[about], inc=1, device_id={"head": owner}, device_id_type=MESH)

    when(inner != across, lambda: tell(inner, me))
    for dist in range(1, mid):
        other = me - inward * dist

        def outward(other=other, dist=dist):
            pl.semaphore_wait(seen.at[other], 1)
            tell(inner, other)
            if dist == 1:
                tell(outer, inner)

        when(exists(other), outward)
    for dist in range(2, owners):
        other = me + inward * dist

        def further(other=other):
            pl.semaphore_wait(seen.at[other], 1)
            when(exists(outer), lambda: tell(outer, other))

        when(exists(other), further)

    def tell_beside(device):
        pl.semaphore_signal(beside.at[0], inc=1, device_id=device, device_id_type=MESH)

    when(end_up, lambda: tell_beside({"slab": slab + 1}))
    when(end_down, lambda: tell_beside({"slab": slab - 1}))

    def send_input(which, chunk):
        for sign, dist in peers:
            other = me + sign * dist
            wanted = exists(other)
            if dist == 1:
                wanted = wanted & ((other != inner) | (chunk >= early))
            when(wanted, lambda other=other: in_copy(which, chunk, other).start())
        own_copy(which, chunk).start()

    lead = min(QUERY_LAG, chunks)

    def send_inputs(chunk, carry):
        def ahead():
            send_input(0, chunk)
            send_input(1, chunk)

        when(chunk < chunks, ahead)
        when(chunk >= lead, lambda: send_input(2, chunk - lead))
        return carry

    lax.fori_loop(0, chunks + lead, send_inputs, 0)

    @pl.when(jnp.logical_not(has_down))
    def _():
        kv_buf[1, :, :halo, :] = jnp.zeros((chunks, halo, lanes), jnp.bfloat16)

    @pl.when(jnp.logical_not(has_up))
    def _():
        kv_buf[1, :, halo + tok_slab :, :] = jnp.zeros((chunks, halo, lanes), jnp.bfloat16)

    lse_buf[...] = jnp.zeros(lse_buf.shape, jnp.float32)
    if slabs > 1:
        heard = jnp.where(at_end, has_up.astype(jnp.int32) + has_down.astype(jnp.int32), 1)
        pl.semaphore_wait(beside.at[0], heard)
        when(inner != across, lambda: tell_beside({"head": inner}))

    mask_copy.wait()
    slot_copy.wait()

    def forward(chunk):
        for which in range(2):
            wait_bytes(kv_buf.at[which, chunk, pl.ds(halo, tok_slab), :], in_recv.at[which, chunk])
            when(has_up, lambda which=which: halo_copy(which, chunk, True).start())
            when(has_down, lambda which=which: halo_copy(which, chunk, False).start())

    def attend(chunk):
        per_sides(lambda n: wait_bytes(kv_buf.at[:, chunk, pl.ds(0, n * halo), :], halo_recv.at[chunk]))
        wait_bytes(q_buf.at[chunk], in_recv.at[2, chunk])
        for within in range(width):
            column = slice(within * head_dim, (within + 1) * head_dim)
            local_head = chunk * width + within
            global_head = me * capacity + local_head
            for block in range(tiles_dev):
                q_rows = slice(block * tile, (block + 1) * tile)
                queries = q_buf[chunk, q_rows, column]
                window = slice(block * tile, (block + band) * tile)
                keys = kv_buf[0, chunk, window, column]
                values = kv_buf[1, chunk, window, column]
                scores = (
                    lax.dot_general(
                        keys, queries, (((1,), (1,)), ((), ())), preferred_element_type=jnp.float32
                    )
                    * scale
                )
                parts = []
                for place in range(band):
                    key_tile = slab * tiles_dev + block + place - reach
                    inside = ((key_tile >= 0) & (key_tile < slabs * tiles_dev)).astype(jnp.int32)
                    flag = mask_buf[place, block, global_head] * inside
                    allowed = jnp.full((tile, tile), flag, jnp.int32) > 0
                    parts.append(
                        jnp.where(allowed, scores[place * tile : (place + 1) * tile], FLOOR)
                    )
                masked = jnp.concatenate(parts, axis=0)
                highest = jnp.max(masked, axis=0, keepdims=True)
                weights = jnp.exp(masked - highest)
                total = jnp.sum(weights, axis=0, keepdims=True)
                summed = lax.dot_general(
                    values,
                    weights.astype(jnp.bfloat16),
                    (((0,), (0,)), ((), ())),
                    preferred_element_type=jnp.float32,
                )
                result = jnp.transpose(summed / total)
                o_buf[chunk, q_rows, column] = result.astype(jnp.bfloat16)
                row = local_head * tiles_dev + block
                lse_buf[pl.ds(row, 1), :] = highest + jnp.log(total)

    def send_out(chunk):
        for sign, dist in peers:
            other = me + sign * dist
            wanted = exists(other) & ((other != across) | (chunk < hold_from))
            when(wanted, lambda other=other: out_copy(chunk, other).start())
        out_own(chunk).start()

    side = jnp.where(low, 0, mid)
    mates = [(sign, dist) for dist in range(mid - 1, 0, -1) for sign in (1, -1)]

    def per_mate(body):
        for sign, dist in mates:
            other = me + sign * dist
            when((other >= side) & (other < side + mid), functools.partial(body, other))

    def send_lse():
        lse_box[me] = lse_buf[:first_rows, :].astype(jnp.bfloat16)
        lse_copy(across, True).start()
        per_mate(lambda other: lse_copy(other, False).start())

    forward(0)

    def step(chunk, carry):
        when(chunk < chunks, lambda: forward(chunk))
        attend(chunk - 1)
        when(chunk == chunks - 1, send_lse)
        send_out(chunk - 1)
        return carry

    lax.fori_loop(1, chunks + 1, step, 0)

    last_box[me] = lse_buf[first_rows:, :].astype(jnp.bfloat16)
    for sign, dist in peers:
        other = me + sign * dist
        when(exists(other), lambda other=other: last_copy(other).start())
    for chunk in range(hold_from, chunks):
        out_copy(chunk, across).start()

    half = lse_box.at[pl.ds(0, mid)]
    wait_bytes(half, lse_recv.at[1])
    when(inner == across, lambda: per_mate(lambda other: lse_relay(other).start()))
    if mid > 1:
        wait_bytes(lse_box.at[pl.ds(0, mid - 1)], lse_recv.at[0])
    wait_bytes(last_box.at[pl.ds(0, owners - 1)], lse_recv.at[2])
    slot_rows = lax.broadcasted_iota(jnp.int32, (capacity, tile), 0) + me * capacity
    slot_lse = [jnp.zeros((capacity, tile), jnp.float32) for _ in range(tiles_dev)]
    for owner in range(owners):
        mine = (me == owner).astype(jnp.int32)

        def values(own, box, owner=owner, mine=mine):
            return jnp.where(jnp.full(own.shape, mine) > 0, own, box[owner].astype(jnp.float32))

        theirs = values(lse_buf[:first_rows, :], lse_box)
        last = values(lse_buf[first_rows:, :], last_box)
        for head in range(capacity):
            here = slot_rows == slot_buf[owner * capacity + head]
            source, first = (theirs, 0) if head < capacity - width else (last, capacity - width)
            for block in range(tiles_dev):
                row = (head - first) * tiles_dev + block
                row = jnp.broadcast_to(source[row : row + 1], (capacity, tile))
                slot_lse[block] = jnp.where(here, row, slot_lse[block])
    for block in range(tiles_dev):
        slot_lse_ref[:, block * tile : (block + 1) * tile] = slot_lse[block]

    wait_bytes(kv_buf.at[:, :, pl.ds(0, 3 * (owners - 1) * tok_dev // 2), :], in_send.at[0])
    per_sides(lambda n: wait_bytes(kv_buf.at[:, :, pl.ds(0, n * halo), :], halo_send.at[0]))
    wait_bytes(half, lse_send.at[0])
    when(inner == across, lambda: per_mate(lambda other: lse_relay(other).wait_send()))
    wait_bytes(last_box.at[pl.ds(0, owners - 1)], lse_send.at[2])
    wait_bytes(o_buf.at[:, pl.ds(0, (owners - 1) * tok_dev), :], out_send.at[0])
    wait_bytes(out_ref, out_recv.at[0])


def hand_over_kernel(out_in, lse_in, out_ref, lse_ref, sems):
    copies = [
        pltpu.make_async_copy(out_in, out_ref, sems.at[0]),
        pltpu.make_async_copy(lse_in, lse_ref, sems.at[1]),
    ]
    for copy in copies:
        copy.start()
    for copy in copies:
        copy.wait()


def on_device(query_rows, key_rows, value_rows, tile_mask, head_slot):
    owners = lax.axis_size("head")
    slabs = lax.axis_size("slab")
    tok_dev, model = query_rows.shape
    heads, tiles_dev, band = tile_mask.shape
    head_dim = model // heads
    capacity = (heads + owners - 1) // owners
    reach = (band - 1) // 2
    tok_slab = tok_dev * owners
    tile = tok_slab // tiles_dev
    halo = reach * tile
    whole = heads == owners * capacity
    width = HEADS_PER_CHUNK if whole and capacity % HEADS_PER_CHUNK == 0 else 1
    chunks = capacity // width
    line = whole and owners % 2 == 0 and owners <= 4 and chunks > 1 and 4 * halo >= tok_slab
    lanes = width * head_dim
    dims = (heads, head_dim, capacity, width, tok_dev, tile, reach)
    dma = pltpu.SemaphoreType.DMA
    tables = [
        pltpu.SMEM((band, tiles_dev, heads), jnp.int32),
        pltpu.SMEM((heads,), jnp.int32),
    ]
    if line:
        kernel = line_kernel
        first_rows = (capacity - width) * tiles_dev
        last_rows = -(-width * tiles_dev // 8) * 8
        scratch = [
            pltpu.VMEM((chunks, tok_slab, lanes), jnp.bfloat16),
            pltpu.VMEM((2, chunks, tok_slab + 2 * halo, lanes), jnp.bfloat16),
            pltpu.VMEM((chunks, tok_slab, lanes), jnp.bfloat16),
            pltpu.VMEM((first_rows + last_rows, tile), jnp.float32),
            pltpu.VMEM((owners, first_rows, tile), jnp.bfloat16),
            pltpu.VMEM((owners, last_rows, tile), jnp.bfloat16),
            pltpu.VMEM((3, tok_dev, lanes), jnp.bfloat16),
            *tables,
            dma((1,)),
            dma((3, chunks)),
            dma((1,)),
            dma((chunks,)),
            dma((1,)),
            dma((1,)),
            dma((3,)),
            dma((3,)),
            pltpu.SemaphoreType.REGULAR((owners,)),
            pltpu.SemaphoreType.REGULAR((1,)),
            dma((1,)),
            dma((2,)),
        ]
    else:
        kernel = attention_kernel
        scratch = [
            pltpu.VMEM((chunks, tok_slab, lanes), jnp.bfloat16),
            pltpu.VMEM((chunks, tok_slab + 2 * halo, lanes), jnp.bfloat16),
            pltpu.VMEM((chunks, tok_slab + 2 * halo, lanes), jnp.bfloat16),
            pltpu.VMEM((chunks, tok_slab, lanes), jnp.bfloat16),
            pltpu.VMEM((owners, capacity, 1, tok_slab), jnp.float32),
            *tables,
            dma((3, chunks, owners)),
            dma((3, chunks, owners)),
            dma((2, chunks, 2)),
            dma((2, chunks, 2)),
            dma((chunks, owners)),
            dma((chunks, owners)),
            dma((owners,)),
            dma((owners,)),
            dma((2,)),
        ]
    gathered, gathered_lse = pl.pallas_call(
        functools.partial(kernel, owners, slabs, dims),
        out_shape=(
            jax.ShapeDtypeStruct((tok_dev, model), jnp.bfloat16),
            jax.ShapeDtypeStruct((capacity, tok_slab), jnp.float32),
        ),
        in_specs=[pl.BlockSpec(memory_space=pltpu.HBM)] * 5,
        out_specs=(pl.BlockSpec(memory_space=pltpu.VMEM), pl.BlockSpec(memory_space=pltpu.VMEM)),
        scratch_shapes=scratch,
        compiler_params=pltpu.CompilerParams(collective_id=0, has_side_effects=True, vmem_limit_bytes=16 << 20),
    )(*[pltpu.with_memory_space_constraint(x, pltpu.HBM) for x in (query_rows, key_rows, value_rows, jnp.transpose(tile_mask, (2, 1, 0)), head_slot)])
    vmem = pl.BlockSpec(memory_space=pltpu.VMEM)
    hbm = pl.BlockSpec(memory_space=pltpu.HBM)
    return pl.pallas_call(
        hand_over_kernel,
        out_shape=(
            jax.ShapeDtypeStruct(gathered.shape, gathered.dtype),
            jax.ShapeDtypeStruct(gathered_lse.shape, gathered_lse.dtype),
        ),
        in_specs=[vmem, vmem],
        out_specs=(hbm, hbm),
        scratch_shapes=[dma((2,))],
        compiler_params=pltpu.CompilerParams(vmem_limit_bytes=16 << 20),
    )(gathered, gathered_lse)


def solution(mesh):
    in_specs = (
        P(("groups", "slab", "head"), None),
        P(("groups", "slab", "head"), None),
        P(("groups", "slab", "head"), None),
        P(None, ("groups", "slab"), None),
        P(),
    )
    out_specs = (P(("groups", "slab", "head"), None), P("head", ("groups", "slab")))
    return jax.shard_map(
        on_device, mesh=mesh, in_specs=in_specs, out_specs=out_specs, check_vma=False
    )
```

```python
import functools

import jax
import jax.numpy as jnp
from jax import lax
from jax.experimental import pallas as pl
from jax.experimental.pallas import tpu as pltpu
from jax.sharding import PartitionSpec as P

MESH = pl.DeviceIdType.MESH
HEADS_PER_CHUNK = 2
EARLY_CHUNKS = 3
QUERY_LAG = 0
HELD_CHUNKS = 3
FLOOR = -1e30


def attention_kernel(
    owners,
    slabs,
    dims,
    q_ref,
    k_ref,
    v_ref,
    mask_ref,
    slot_ref,
    out_ref,
    slot_lse_ref,
    q_buf,
    k_buf,
    v_buf,
    o_buf,
    lse_buf,
    mask_buf,
    slot_buf,
    in_send,
    in_recv,
    halo_send,
    halo_recv,
    out_send,
    out_recv,
    lse_send,
    lse_recv,
    small_sem,
):
    heads, head_dim, capacity, width, tok_dev, tile, reach = dims
    chunks = capacity // width
    lanes = width * head_dim
    tok_slab = tok_dev * owners
    tiles_dev = tok_slab // tile
    band = 2 * reach + 1
    halo = reach * tile
    full = heads == owners * capacity
    scale = head_dim ** (-0.5)
    me = lax.axis_index("head")
    slab = lax.axis_index("slab")
    inputs = ((k_ref, k_buf, halo), (v_ref, v_buf, halo), (q_ref, q_buf, 0))
    peers = [(sign, dist) for dist in range(owners - 1, 0, -1) for sign in (1, -1)]

    def when(condition, body):
        pl.when(condition)(body)

    def per_peer(body):
        for sign, dist in peers:
            other = me + sign * dist
            when((other >= 0) & (other < owners), functools.partial(body, other))

    def if_held(owner, chunk, body):
        if full:
            body()
        else:
            when(owner * capacity + chunk * width < heads, body)

    def columns(owner, chunk):
        first = (owner * capacity + chunk * width) * head_dim
        return pl.ds(pl.multiple_of(first, head_dim), lanes)

    def rows(owner, base):
        return pl.ds(pl.multiple_of(owner * tok_dev + base, tok_dev), tok_dev)

    def in_copy(which, chunk, src_owner, dst_owner):
        ref, buf, base = inputs[which]
        return pltpu.make_async_remote_copy(
            src_ref=ref.at[:, columns(dst_owner, chunk)],
            dst_ref=buf.at[chunk, rows(src_owner, base), :],
            send_sem=in_send.at[which, chunk, dst_owner],
            recv_sem=in_recv.at[which, chunk, src_owner],
            device_id={"head": dst_owner},
            device_id_type=MESH,
        )

    def own_copy(which, chunk):
        ref, buf, base = inputs[which]
        return pltpu.make_async_copy(
            ref.at[:, columns(me, chunk)],
            buf.at[chunk, rows(me, base), :],
            in_recv.at[which, chunk, me],
        )

    def halo_copy(which, chunk, up):
        buf = inputs[which][1]
        source = tok_slab if up else halo
        target = 0 if up else halo + tok_slab
        return pltpu.make_async_remote_copy(
            src_ref=buf.at[chunk, pl.ds(source, halo), :],
            dst_ref=buf.at[chunk, pl.ds(target, halo), :],
            send_sem=halo_send.at[which, chunk, int(up)],
            recv_sem=halo_recv.at[which, chunk, int(up)],
            device_id={"slab": slab + 1 if up else slab - 1},
            device_id_type=MESH,
        )

    def out_copy(chunk, src_owner, dst_owner):
        return pltpu.make_async_remote_copy(
            src_ref=o_buf.at[chunk, rows(dst_owner, 0), :],
            dst_ref=out_ref.at[:, columns(src_owner, chunk)],
            send_sem=out_send.at[chunk, dst_owner],
            recv_sem=out_recv.at[chunk, src_owner],
            device_id={"head": dst_owner},
            device_id_type=MESH,
        )

    def out_own(chunk):
        return pltpu.make_async_copy(
            o_buf.at[chunk, rows(me, 0), :],
            out_ref.at[:, columns(me, chunk)],
            out_recv.at[chunk, me],
        )

    def lse_copy(src_owner, dst_owner):
        return pltpu.make_async_remote_copy(
            src_ref=lse_buf.at[src_owner],
            dst_ref=lse_buf.at[src_owner],
            send_sem=lse_send.at[dst_owner],
            recv_sem=lse_recv.at[src_owner],
            device_id={"head": dst_owner},
            device_id_type=MESH,
        )

    has_up = slab < slabs - 1
    has_down = slab > 0
    barrier = pltpu.get_barrier_semaphore()

    def greet(other):
        pl.semaphore_signal(barrier, inc=1, device_id={"head": other}, device_id_type=MESH)

    per_peer(greet)

    @pl.when(has_up)
    def _():
        pl.semaphore_signal(barrier, inc=1, device_id={"slab": slab + 1}, device_id_type=MESH)

    @pl.when(has_down)
    def _():
        pl.semaphore_signal(barrier, inc=1, device_id={"slab": slab - 1}, device_id_type=MESH)

    mask_copy = pltpu.make_async_copy(mask_ref, mask_buf, small_sem.at[0])
    slot_copy = pltpu.make_async_copy(slot_ref, slot_buf, small_sem.at[1])
    mask_copy.start()
    slot_copy.start()
    pl.semaphore_wait(
        barrier, owners - 1 + has_up.astype(jnp.int32) + has_down.astype(jnp.int32)
    )

    low_half = me < owners // 2

    def send_inputs(crossing, chunk, carry):
        for which in range(3):

            def to_peer(other, which=which):
                def go():
                    if_held(other, chunk, lambda: in_copy(which, chunk, me, other).start())

                other_side = low_half != (other < owners // 2)
                when(other_side if crossing else jnp.logical_not(other_side), go)

            per_peer(to_peer)
            if crossing:
                if_held(me, chunk, lambda which=which: own_copy(which, chunk).start())
        return carry

    lax.fori_loop(0, chunks, functools.partial(send_inputs, False), 0)
    lax.fori_loop(0, chunks, functools.partial(send_inputs, True), 0)

    if not full:
        lse_buf[me] = jnp.zeros(lse_buf.shape[1:], jnp.float32)

    @pl.when(jnp.logical_not(has_down))
    def _():
        v_buf[:, :halo, :] = jnp.zeros((chunks, halo, lanes), jnp.bfloat16)

    @pl.when(jnp.logical_not(has_up))
    def _():
        v_buf[:, halo + tok_slab :, :] = jnp.zeros((chunks, halo, lanes), jnp.bfloat16)

    mask_copy.wait()
    slot_copy.wait()

    def wait_input(which, chunk):
        per_peer(lambda other: in_copy(which, chunk, other, me).wait_recv())
        own_copy(which, chunk).wait()

    def forward(chunk):
        for which in range(2):
            wait_input(which, chunk)
            when(has_up, lambda: halo_copy(which, chunk, True).start())
            when(has_down, lambda: halo_copy(which, chunk, False).start())

    def attend(chunk):
        for which in range(2):
            when(has_down, lambda: halo_copy(which, chunk, True).wait_recv())
            when(has_up, lambda: halo_copy(which, chunk, False).wait_recv())
        wait_input(2, chunk)
        for within in range(width):
            column = slice(within * head_dim, (within + 1) * head_dim)
            local_head = chunk * width + within
            global_head = me * capacity + local_head
            for block in range(tiles_dev):
                q_rows = slice(block * tile, (block + 1) * tile)
                queries = q_buf[chunk, q_rows, column]
                window = slice(block * tile, (block + band) * tile)
                keys = k_buf[chunk, window, column]
                values = v_buf[chunk, window, column]
                scores = (
                    lax.dot_general(
                        keys, queries, (((1,), (1,)), ((), ())), preferred_element_type=jnp.float32
                    )
                    * scale
                )
                parts = []
                for place in range(band):
                    key_tile = slab * tiles_dev + block + place - reach
                    inside = ((key_tile >= 0) & (key_tile < slabs * tiles_dev)).astype(jnp.int32)
                    flag = mask_buf[place, block, global_head] * inside
                    allowed = jnp.full((tile, tile), flag, jnp.int32) > 0
                    parts.append(
                        jnp.where(allowed, scores[place * tile : (place + 1) * tile], FLOOR)
                    )
                masked = jnp.concatenate(parts, axis=0)
                highest = jnp.max(masked, axis=0, keepdims=True)
                weights = jnp.exp(masked - highest)
                total = jnp.sum(weights, axis=0, keepdims=True)
                summed = lax.dot_general(
                    values,
                    weights.astype(jnp.bfloat16),
                    (((0,), (0,)), ((), ())),
                    preferred_element_type=jnp.float32,
                )
                result = jnp.transpose(summed * (1.0 / total))
                o_buf[chunk, q_rows, column] = result.astype(jnp.bfloat16)
                lse_buf[me, local_head, :, q_rows] = highest + jnp.log(total)

    def send_out(chunk):
        per_peer(lambda other: out_copy(chunk, me, other).start())
        out_own(chunk).start()

    if_held(me, 0, lambda: forward(0))

    def step(chunk, carry):
        if_held(me, chunk, lambda: forward(chunk))

        def finish():
            attend(chunk - 1)
            send_out(chunk - 1)

        if_held(me, chunk - 1, finish)
        return carry

    lax.fori_loop(1, chunks, step, 0)
    last = chunks - 1
    if_held(me, last, lambda: attend(last))
    per_peer(lambda other: lse_copy(me, other).start())
    if_held(me, last, lambda: send_out(last))

    per_peer(lambda other: lse_copy(other, me).wait_recv())
    slot_rows = lax.broadcasted_iota(jnp.int32, (capacity, tok_slab), 0) + me * capacity
    slot_lse = jnp.zeros((capacity, tok_slab), jnp.float32)
    for head in range(heads):
        row = jnp.broadcast_to(lse_buf[head // capacity, head % capacity], (capacity, tok_slab))
        slot_lse = jnp.where(slot_rows == slot_buf[head], row, slot_lse)
    slot_lse_ref[...] = slot_lse

    def drain(chunk, carry):
        for which in range(3):

            def sent(other, which=which):
                if_held(other, chunk, lambda: in_copy(which, chunk, me, other).wait_send())

            per_peer(sent)

        def mine():
            for which in range(2):
                when(has_up, lambda: halo_copy(which, chunk, True).wait_send())
                when(has_down, lambda: halo_copy(which, chunk, False).wait_send())
            per_peer(lambda other: out_copy(chunk, me, other).wait_send())
            out_own(chunk).wait()

        if_held(me, chunk, mine)

        def arrived(other):
            if_held(other, chunk, lambda: out_copy(chunk, other, me).wait_recv())

        per_peer(arrived)
        return carry

    lax.fori_loop(0, chunks, drain, 0)
    per_peer(lambda other: lse_copy(me, other).wait_send())


def line_kernel(
    owners,
    slabs,
    dims,
    q_ref,
    k_ref,
    v_ref,
    mask_ref,
    slot_ref,
    out_ref,
    slot_lse_ref,
    q_buf,
    kv_buf,
    o_buf,
    lse_buf,
    lse_box,
    last_box,
    first_buf,
    mask_buf,
    slot_buf,
    in_send,
    in_recv,
    halo_send,
    halo_recv,
    out_send,
    out_recv,
    lse_send,
    lse_recv,
    seen,
    beside,
    first_sem,
    small_sem,
):
    heads, head_dim, capacity, width, tok_dev, tile, reach = dims
    chunks = capacity // width
    lanes = width * head_dim
    tok_slab = tok_dev * owners
    tiles_dev = tok_slab // tile
    band = 2 * reach + 1
    halo = reach * tile
    mid = owners // 2
    early = min(EARLY_CHUNKS, chunks)
    hold_from = max(chunks - HELD_CHUNKS, 0)
    first_rows = (capacity - width) * tiles_dev
    scale = head_dim ** (-0.5)
    me = lax.axis_index("head")
    slab = lax.axis_index("slab")
    low = me < mid
    inward = jnp.where(low, 1, -1)
    inner = me + inward
    outer = me - inward
    across = jnp.where(low, mid, mid - 1)
    has_up = slab < slabs - 1
    has_down = slab > 0
    inputs = ((k_ref, kv_buf.at[0], halo), (v_ref, kv_buf.at[1], halo), (q_ref, q_buf, 0))
    peers = [(sign, dist) for dist in range(owners - 1, 0, -1) for sign in (1, -1)]

    def when(condition, body):
        pl.when(condition)(body)

    def exists(other):
        return (other >= 0) & (other < owners)

    def columns(owner, chunk):
        first = (owner * capacity + chunk * width) * head_dim
        return pl.ds(pl.multiple_of(first, head_dim), lanes)

    def rows(owner, base):
        return pl.ds(pl.multiple_of(owner * tok_dev + base, tok_dev), tok_dev)

    def wait_bytes(ref, sem):
        pltpu.make_async_copy(ref, ref, sem).wait()

    def in_copy(which, chunk, dst_owner, source=None):
        ref, buf, base = inputs[which]
        return pltpu.make_async_remote_copy(
            src_ref=ref.at[:, columns(dst_owner, chunk)] if source is None else source,
            dst_ref=buf.at[chunk, rows(me, base), :],
            send_sem=in_send.at[0],
            recv_sem=in_recv.at[which, chunk],
            device_id={"head": dst_owner},
            device_id_type=MESH,
        )

    def own_copy(which, chunk):
        ref, buf, base = inputs[which]
        return pltpu.make_async_copy(
            ref.at[:, columns(me, chunk)],
            buf.at[chunk, rows(me, base), :],
            in_recv.at[which, chunk],
        )

    def halo_copy(which, chunk, up):
        source = tok_slab if up else halo
        target = 0 if up else halo + tok_slab
        return pltpu.make_async_remote_copy(
            src_ref=kv_buf.at[which, chunk, pl.ds(source, halo), :],
            dst_ref=kv_buf.at[which, chunk, pl.ds(target, halo), :],
            send_sem=halo_send.at[0],
            recv_sem=halo_recv.at[chunk],
            device_id={"slab": slab + 1 if up else slab - 1},
            device_id_type=MESH,
        )

    def per_sides(body):
        both = has_up & has_down
        when(both, lambda: body(2))
        when(jnp.logical_not(both) & (has_up | has_down), lambda: body(1))

    def out_copy(chunk, dst_owner):
        return pltpu.make_async_remote_copy(
            src_ref=o_buf.at[chunk, rows(dst_owner, 0), :],
            dst_ref=out_ref.at[:, columns(me, chunk)],
            send_sem=out_send.at[0],
            recv_sem=out_recv.at[0],
            device_id={"head": dst_owner},
            device_id_type=MESH,
        )

    def out_own(chunk):
        return pltpu.make_async_copy(
            o_buf.at[chunk, rows(me, 0), :],
            out_ref.at[:, columns(me, chunk)],
            out_recv.at[0],
        )

    def lse_copy(dst_owner, crossing):
        return pltpu.make_async_remote_copy(
            src_ref=lse_box.at[me],
            dst_ref=lse_box.at[me],
            send_sem=lse_send.at[0],
            recv_sem=lse_recv.at[int(crossing)],
            device_id={"head": dst_owner},
            device_id_type=MESH,
        )

    def lse_relay(dst_owner):
        boxes = lse_box.at[pl.ds(jnp.where(low, mid, 0), mid)]
        return pltpu.make_async_remote_copy(
            src_ref=boxes,
            dst_ref=boxes,
            send_sem=lse_send.at[1],
            recv_sem=lse_recv.at[1],
            device_id={"head": dst_owner},
            device_id_type=MESH,
        )

    def last_copy(dst_owner):
        return pltpu.make_async_remote_copy(
            src_ref=last_box.at[me],
            dst_ref=last_box.at[me],
            send_sem=lse_send.at[2],
            recv_sem=lse_recv.at[2],
            device_id={"head": dst_owner},
            device_id_type=MESH,
        )

    barrier = pltpu.get_barrier_semaphore()

    def greet(device):
        pl.semaphore_signal(barrier, inc=1, device_id=device, device_id_type=MESH)

    when(inner == across, lambda: greet({"head": inner}))
    when(exists(outer), lambda: greet({"head": outer}))
    at_end = jnp.logical_not(exists(outer))
    end_up = at_end & has_up
    end_down = at_end & has_down
    when(end_up, lambda: greet({"slab": slab + 1}))
    when(end_down, lambda: greet({"slab": slab - 1}))

    mask_copy = pltpu.make_async_copy(mask_ref, mask_buf, small_sem.at[0])
    slot_copy = pltpu.make_async_copy(slot_ref, slot_buf, small_sem.at[1])
    def stage():
        for which in range(3):
            pltpu.make_async_copy(
                inputs[which][0].at[:, columns(inner, 0)], first_buf.at[which], first_sem.at[0]
            ).start()

    when(low, stage)
    pl.semaphore_wait(barrier, 1 + end_up.astype(jnp.int32) + end_down.astype(jnp.int32))

    def begin_staged():
        wait_bytes(first_buf, first_sem.at[0])
        for which in range(3):
            in_copy(which, 0, inner, first_buf.at[which]).start()

    def begin():
        for which in range(3):
            in_copy(which, 0, inner).start()

    when(low, begin_staged)
    when(jnp.logical_not(low), begin)
    for chunk in range(1, early):
        for which in range(3):
            in_copy(which, chunk, inner).start()

    mask_copy.start()
    slot_copy.start()

    def tell(owner, about):
        pl.semaphore_signal(seen.at[about], inc=1, device_id={"head": owner}, device_id_type=MESH)

    when(inner != across, lambda: tell(inner, me))
    for dist in range(1, mid):
        other = me - inward * dist

        def outward(other=other, dist=dist):
            pl.semaphore_wait(seen.at[other], 1)
            tell(inner, other)
            if dist == 1:
                tell(outer, inner)

        when(exists(other), outward)
    for dist in range(2, owners):
        other = me + inward * dist

        def further(other=other):
            pl.semaphore_wait(seen.at[other], 1)
            when(exists(outer), lambda: tell(outer, other))

        when(exists(other), further)

    def tell_beside(device):
        pl.semaphore_signal(beside.at[0], inc=1, device_id=device, device_id_type=MESH)

    when(end_up, lambda: tell_beside({"slab": slab + 1}))
    when(end_down, lambda: tell_beside({"slab": slab - 1}))

    def send_input(which, chunk):
        for sign, dist in peers:
            other = me + sign * dist
            wanted = exists(other)
            if dist == 1:
                wanted = wanted & ((other != inner) | (chunk >= early))
            when(wanted, lambda other=other: in_copy(which, chunk, other).start())
        own_copy(which, chunk).start()

    lead = min(QUERY_LAG, chunks)

    def send_inputs(chunk, carry):
        def ahead():
            send_input(0, chunk)
            send_input(1, chunk)

        when(chunk < chunks, ahead)
        when(chunk >= lead, lambda: send_input(2, chunk - lead))
        return carry

    lax.fori_loop(0, chunks + lead, send_inputs, 0)

    @pl.when(jnp.logical_not(has_down))
    def _():
        kv_buf[1, :, :halo, :] = jnp.zeros((chunks, halo, lanes), jnp.bfloat16)

    @pl.when(jnp.logical_not(has_up))
    def _():
        kv_buf[1, :, halo + tok_slab :, :] = jnp.zeros((chunks, halo, lanes), jnp.bfloat16)

    lse_buf[...] = jnp.zeros(lse_buf.shape, jnp.float32)
    if slabs > 1:
        heard = jnp.where(at_end, has_up.astype(jnp.int32) + has_down.astype(jnp.int32), 1)
        pl.semaphore_wait(beside.at[0], heard)
        when(inner != across, lambda: tell_beside({"head": inner}))

    mask_copy.wait()
    slot_copy.wait()

    def forward(chunk):
        for which in range(2):
            wait_bytes(kv_buf.at[which, chunk, pl.ds(halo, tok_slab), :], in_recv.at[which, chunk])
            when(has_up, lambda which=which: halo_copy(which, chunk, True).start())
            when(has_down, lambda which=which: halo_copy(which, chunk, False).start())

    def attend(chunk):
        per_sides(lambda n: wait_bytes(kv_buf.at[:, chunk, pl.ds(0, n * halo), :], halo_recv.at[chunk]))
        wait_bytes(q_buf.at[chunk], in_recv.at[2, chunk])
        for within in range(width):
            column = slice(within * head_dim, (within + 1) * head_dim)
            local_head = chunk * width + within
            global_head = me * capacity + local_head
            for block in range(tiles_dev):
                q_rows = slice(block * tile, (block + 1) * tile)
                queries = q_buf[chunk, q_rows, column]
                window = slice(block * tile, (block + band) * tile)
                keys = kv_buf[0, chunk, window, column]
                values = kv_buf[1, chunk, window, column]
                scores = (
                    lax.dot_general(
                        keys, queries, (((1,), (1,)), ((), ())), preferred_element_type=jnp.float32
                    )
                    * scale
                )
                parts = []
                for place in range(band):
                    key_tile = slab * tiles_dev + block + place - reach
                    inside = ((key_tile >= 0) & (key_tile < slabs * tiles_dev)).astype(jnp.int32)
                    flag = mask_buf[place, block, global_head] * inside
                    allowed = jnp.full((tile, tile), flag, jnp.int32) > 0
                    parts.append(
                        jnp.where(allowed, scores[place * tile : (place + 1) * tile], FLOOR)
                    )
                masked = jnp.concatenate(parts, axis=0)
                highest = jnp.max(masked, axis=0, keepdims=True)
                weights = jnp.exp(masked - highest)
                total = jnp.sum(weights, axis=0, keepdims=True)
                summed = lax.dot_general(
                    values,
                    weights.astype(jnp.bfloat16),
                    (((0,), (0,)), ((), ())),
                    preferred_element_type=jnp.float32,
                )
                result = jnp.transpose(summed * (1.0 / total))
                o_buf[chunk, q_rows, column] = result.astype(jnp.bfloat16)
                row = local_head * tiles_dev + block
                lse_buf[pl.ds(row, 1), :] = highest + jnp.log(total)

    def send_out(chunk):
        for sign, dist in peers:
            other = me + sign * dist
            wanted = exists(other) & ((other != across) | (chunk < hold_from))
            when(wanted, lambda other=other: out_copy(chunk, other).start())
        out_own(chunk).start()

    side = jnp.where(low, 0, mid)
    mates = [(sign, dist) for dist in range(mid - 1, 0, -1) for sign in (1, -1)]

    def per_mate(body):
        for sign, dist in mates:
            other = me + sign * dist
            when((other >= side) & (other < side + mid), functools.partial(body, other))

    def send_lse():
        lse_box[me] = lse_buf[:first_rows, :].astype(jnp.bfloat16)
        lse_copy(across, True).start()
        per_mate(lambda other: lse_copy(other, False).start())

    forward(0)

    def step(chunk, carry):
        when(chunk < chunks, lambda: forward(chunk))
        attend(chunk - 1)
        when(chunk == chunks - 1, send_lse)
        send_out(chunk - 1)
        return carry

    lax.fori_loop(1, chunks + 1, step, 0)

    last_box[me] = lse_buf[first_rows:, :].astype(jnp.bfloat16)
    for sign, dist in peers:
        other = me + sign * dist
        when(exists(other), lambda other=other: last_copy(other).start())
    for chunk in range(hold_from, chunks):
        out_copy(chunk, across).start()

    half = lse_box.at[pl.ds(0, mid)]
    wait_bytes(half, lse_recv.at[1])
    when(inner == across, lambda: per_mate(lambda other: lse_relay(other).start()))
    if mid > 1:
        wait_bytes(lse_box.at[pl.ds(0, mid - 1)], lse_recv.at[0])
    wait_bytes(last_box.at[pl.ds(0, owners - 1)], lse_recv.at[2])
    slot_rows = lax.broadcasted_iota(jnp.int32, (capacity, tile), 0) + me * capacity
    slot_lse = [jnp.zeros((capacity, tile), jnp.float32) for _ in range(tiles_dev)]
    for owner in range(owners):
        mine = (me == owner).astype(jnp.int32)

        def values(own, box, owner=owner, mine=mine):
            return jnp.where(jnp.full(own.shape, mine) > 0, own, box[owner].astype(jnp.float32))

        theirs = values(lse_buf[:first_rows, :], lse_box)
        last = values(lse_buf[first_rows:, :], last_box)
        for head in range(capacity):
            here = slot_rows == slot_buf[owner * capacity + head]
            source, first = (theirs, 0) if head < capacity - width else (last, capacity - width)
            for block in range(tiles_dev):
                row = (head - first) * tiles_dev + block
                row = jnp.broadcast_to(source[row : row + 1], (capacity, tile))
                slot_lse[block] = jnp.where(here, row, slot_lse[block])
    for block in range(tiles_dev):
        slot_lse_ref[:, block * tile : (block + 1) * tile] = slot_lse[block]

    wait_bytes(kv_buf.at[:, :, pl.ds(0, 3 * (owners - 1) * tok_dev // 2), :], in_send.at[0])
    per_sides(lambda n: wait_bytes(kv_buf.at[:, :, pl.ds(0, n * halo), :], halo_send.at[0]))
    wait_bytes(half, lse_send.at[0])
    when(inner == across, lambda: per_mate(lambda other: lse_relay(other).wait_send()))
    wait_bytes(last_box.at[pl.ds(0, owners - 1)], lse_send.at[2])
    wait_bytes(o_buf.at[:, pl.ds(0, (owners - 1) * tok_dev), :], out_send.at[0])
    wait_bytes(out_ref, out_recv.at[0])


def hand_over_kernel(out_in, lse_in, out_ref, lse_ref, sems):
    copies = [
        pltpu.make_async_copy(out_in, out_ref, sems.at[0]),
        pltpu.make_async_copy(lse_in, lse_ref, sems.at[1]),
    ]
    for copy in copies:
        copy.start()
    for copy in copies:
        copy.wait()


def on_device(query_rows, key_rows, value_rows, tile_mask, head_slot):
    owners = lax.axis_size("head")
    slabs = lax.axis_size("slab")
    tok_dev, model = query_rows.shape
    heads, tiles_dev, band = tile_mask.shape
    head_dim = model // heads
    capacity = (heads + owners - 1) // owners
    reach = (band - 1) // 2
    tok_slab = tok_dev * owners
    tile = tok_slab // tiles_dev
    halo = reach * tile
    whole = heads == owners * capacity
    width = HEADS_PER_CHUNK if whole and capacity % HEADS_PER_CHUNK == 0 else 1
    chunks = capacity // width
    line = whole and owners % 2 == 0 and owners <= 4 and chunks > 1 and 4 * halo >= tok_slab
    lanes = width * head_dim
    dims = (heads, head_dim, capacity, width, tok_dev, tile, reach)
    dma = pltpu.SemaphoreType.DMA
    tables = [
        pltpu.SMEM((band, tiles_dev, heads), jnp.int32),
        pltpu.SMEM((heads,), jnp.int32),
    ]
    if line:
        kernel = line_kernel
        first_rows = (capacity - width) * tiles_dev
        last_rows = -(-width * tiles_dev // 8) * 8
        scratch = [
            pltpu.VMEM((chunks, tok_slab, lanes), jnp.bfloat16),
            pltpu.VMEM((2, chunks, tok_slab + 2 * halo, lanes), jnp.bfloat16),
            pltpu.VMEM((chunks, tok_slab, lanes), jnp.bfloat16),
            pltpu.VMEM((first_rows + last_rows, tile), jnp.float32),
            pltpu.VMEM((owners, first_rows, tile), jnp.bfloat16),
            pltpu.VMEM((owners, last_rows, tile), jnp.bfloat16),
            pltpu.VMEM((3, tok_dev, lanes), jnp.bfloat16),
            *tables,
            dma((1,)),
            dma((3, chunks)),
            dma((1,)),
            dma((chunks,)),
            dma((1,)),
            dma((1,)),
            dma((3,)),
            dma((3,)),
            pltpu.SemaphoreType.REGULAR((owners,)),
            pltpu.SemaphoreType.REGULAR((1,)),
            dma((1,)),
            dma((2,)),
        ]
    else:
        kernel = attention_kernel
        scratch = [
            pltpu.VMEM((chunks, tok_slab, lanes), jnp.bfloat16),
            pltpu.VMEM((chunks, tok_slab + 2 * halo, lanes), jnp.bfloat16),
            pltpu.VMEM((chunks, tok_slab + 2 * halo, lanes), jnp.bfloat16),
            pltpu.VMEM((chunks, tok_slab, lanes), jnp.bfloat16),
            pltpu.VMEM((owners, capacity, 1, tok_slab), jnp.float32),
            *tables,
            dma((3, chunks, owners)),
            dma((3, chunks, owners)),
            dma((2, chunks, 2)),
            dma((2, chunks, 2)),
            dma((chunks, owners)),
            dma((chunks, owners)),
            dma((owners,)),
            dma((owners,)),
            dma((2,)),
        ]
    gathered, gathered_lse = pl.pallas_call(
        functools.partial(kernel, owners, slabs, dims),
        out_shape=(
            jax.ShapeDtypeStruct((tok_dev, model), jnp.bfloat16),
            jax.ShapeDtypeStruct((capacity, tok_slab), jnp.float32),
        ),
        in_specs=[pl.BlockSpec(memory_space=pltpu.HBM)] * 5,
        out_specs=(pl.BlockSpec(memory_space=pltpu.VMEM), pl.BlockSpec(memory_space=pltpu.VMEM)),
        scratch_shapes=scratch,
        compiler_params=pltpu.CompilerParams(collective_id=0, has_side_effects=True, vmem_limit_bytes=16 << 20),
    )(*[pltpu.with_memory_space_constraint(x, pltpu.HBM) for x in (query_rows, key_rows, value_rows, jnp.transpose(tile_mask, (2, 1, 0)), head_slot)])
    vmem = pl.BlockSpec(memory_space=pltpu.VMEM)
    hbm = pl.BlockSpec(memory_space=pltpu.HBM)
    return pl.pallas_call(
        hand_over_kernel,
        out_shape=(
            jax.ShapeDtypeStruct(gathered.shape, gathered.dtype),
            jax.ShapeDtypeStruct(gathered_lse.shape, gathered_lse.dtype),
        ),
        in_specs=[vmem, vmem],
        out_specs=(hbm, hbm),
        scratch_shapes=[dma((2,))],
        compiler_params=pltpu.CompilerParams(vmem_limit_bytes=16 << 20),
    )(gathered, gathered_lse)


def solution(mesh):
    in_specs = (
        P(("groups", "slab", "head"), None),
        P(("groups", "slab", "head"), None),
        P(("groups", "slab", "head"), None),
        P(None, ("groups", "slab"), None),
        P(),
    )
    out_specs = (P(("groups", "slab", "head"), None), P("head", ("groups", "slab")))
    return jax.shard_map(
        on_device, mesh=mesh, in_specs=in_specs, out_specs=out_specs, check_vma=False
    )
```
